32 devices in a mesh: groups: 2 (over y), dp: 4 (over z), replica: 2 (over x), chan: 2 (over core).
Axes of the slice: x: 2, y: 2, z: 4, core: 2. Of those that a mesh axis runs over, the one named last changes fastest.
Arguments:
- activations: bfloat16 [8192, 768], P(('groups', 'dp', 'replica'), 'chan'), parts along dimension 0, may hold values from -6 to 6
- cotangent: bfloat16 [8192, 768], P(('groups', 'dp', 'replica'), 'chan'), parts along dimension 0, may hold values from -0.1875 to 0.1875
- conv_weights: bfloat16 [3, 3, 768, 768], P(None, None, None, 'chan'), may hold values from -0.125 to 0.125
- snake_alpha: float32 [3, 768], P(None, 'chan'), may hold values from 0.4 to 2.5
- seg_lengths: int32 [32], P('groups'), parts along dimension 0, may hold values from 32 to 248, as said below
- seg_owner: int32 [32], P('groups'), parts along dimension 0, may hold values from 0 to 7, as said below
- seg_start: int32 [32], P('groups'), parts along dimension 0, may hold values from 5 to 261, as said below
Outputs:
- residual_out: bfloat16 [8192, 768], P(('groups', 'dp', 'replica'), 'chan'), parts along dimension 0
- weight_grads: float32 [6, 3, 768, 768], P('groups', None, 'dp', 'chan'), parts along dimension 0
- alpha_grads: float32 [6, 768], P('groups', 'chan'), parts along dimension 0
The draws below stay inside these ranges and needn't reach their ends.
There are 2 independent parts, one for each index of `groups`. The reference program is written for one: setup_inputs(seed, part) draws one part's arguments, and reference() takes and returns one part's arrays. A program takes and returns all parts, laid end to end along the dimension named above; an argument that names none is the same for every part. Nothing has to cross between parts.
Inputs may be any that keep to these rules, and one draw needn't show every extreme that they name: `seg_lengths`: every clip has 32 to 248 positions; some clip has exactly 248. `seg_owner`: every data device (numbered in the order dp, then replica) holds exactly 2 clips. `seg_start`: A device's clips lie one after another in its buffer; the first starts at position 5, and 5 to 8 unused positions stand before every later one; all end within the buffer; some clip starts at exactly 261.
All inputs are finite; a program needn't handle non-finite values.
Results may differ from the reference program's by a relative error of at most 0.014.
The reference program's roundings to bfloat16 on the way count: a program that leaves them out, or rounds other values in their place, can miss the bound.
Values may be sent and summed in bfloat16 or wider, within the bound.
No kernel may reach another device: no remote copies, remote signals or barrier semaphores. Data moves between devices by JAX's collectives and lax.ppermute only.
A program may use at most 64 MiB of HBM per device.

```python
import math
import jax
import jax.numpy as jnp
from jax import lax

C = 768
KERNEL = 3
LAYERS = 3
SEG_DEV = 2
TOK_DEV = 512
DATA_DEVS = 8
SEGS = 16
ROWS = 4096
MAX_LEN = 248
MIN_LEN = 32


def deal_clips(key):
    base = jax.random.fold_in(key, 4711)
    key_len, key_force, key_perm, key_gap = jax.random.split(base, 4)
    order = jax.random.permutation(key_perm, SEGS).astype(jnp.int32)
    owner = (order // SEG_DEV).astype(jnp.int32)
    rank = (order % SEG_DEV).astype(jnp.int32)
    forced_dev = jax.random.randint(key_force, (), 0, DATA_DEVS, dtype=jnp.int32)
    lengths = jax.random.randint(key_len, (SEGS,), MIN_LEN, MAX_LEN + 1, dtype=jnp.int32)
    lengths = jnp.where((owner == forced_dev) & (rank == 0), MAX_LEN, lengths).astype(jnp.int32)
    gaps = jax.random.randint(key_gap, (SEGS,), 5, 9, dtype=jnp.int32)
    gaps = jnp.where((owner == forced_dev) & (rank == 1), 8, gaps).astype(jnp.int32)
    gaps = jnp.where(rank == 0, 5, gaps).astype(jnp.int32)
    before = (owner[None, :] == owner[:, None]) & (rank[None, :] < rank[:, None])
    prior = jnp.sum(jnp.where(before, (lengths + gaps)[None, :], 0), axis=1).astype(jnp.int32)
    return (lengths, owner, (prior + gaps).astype(jnp.int32))


def draw_seg_lengths(key, part):
    return deal_clips(key)[0]


def draw_seg_owner(key, part):
    return deal_clips(key)[1]


def draw_seg_start(key, part):
    return deal_clips(key)[2]


def spiked(entries, stream_key, source, target, shards_of, factor):
    owner, partner = [(jnp.arange(entries.shape[dim]) // (entries.shape[dim] // shards_of)).reshape([-1 if axis == dim else 1 for axis in range(entries.ndim)]) for dim in (source, target)]
    chosen = jax.random.permutation(stream_key, shards_of)[partner]
    strong = (owner == chosen) | (owner == (partner + shards_of // 2) % shards_of)
    return jnp.where(strong, factor * entries, entries)


def block_scale(own_key, shape, cuts, smallest, top_value):
    gain, own = 1.0, jax.random.fold_in(own_key, 6)
    for dim, shards_of in cuts:
        heights = jnp.exp(jax.random.uniform(jax.random.fold_in(own, dim), (shards_of,), jnp.float32, smallest / len(cuts), top_value / len(cuts)))
        gain = gain * jnp.repeat(heights, shape[dim] // shards_of).reshape([-1 if axis == dim else 1 for axis in range(len(shape))])
    return gain


def bell_draw(rng, dims, width, most, shards=(), kind=jnp.bfloat16):
    level = block_scale(rng, dims, shards, -0.22, 0.18) if shards else 1.0
    array = jax.random.normal(rng, dims, jnp.float32) * width * level
    return jnp.minimum(jnp.maximum(array, -most), most).astype(kind)


def gaussian_with(rng, dims, deviation, limit, pieces, heavy, kind=jnp.bfloat16):
    values = deviation * jax.random.normal(rng, dims, jnp.float32)
    if pieces:
        values = values * block_scale(rng, dims, pieces, -0.22, 0.18)
    return jnp.clip(spiked(values, jax.random.fold_in(rng, 3), *heavy), -limit, limit).astype(kind)


def setup_inputs(seed: int = 0, part: int = 0) -> dict:
    key_of = jax.random.split(jax.random.key(seed), 8)
    part_splits = jax.random.split(jax.random.fold_in(key_of[7], part), 8)
    activations = gaussian_with(part_splits[0], (ROWS, C), 1.0, 6.0, ((0, 8), (1, 2)), (0, 1, 8, 2.0))
    cotangent = bell_draw(part_splits[1], (ROWS, C), (TOK_DEV * DATA_DEVS // 4) ** -0.5, 0.1875, ((0, 8), (1, 2)))
    conv_weights = bell_draw(key_of[2], (LAYERS, KERNEL, C, C), (KERNEL * C) ** -0.5, 0.125, ((3, 2),))
    snake_alpha = jnp.clip(jnp.exp(math.log(2.5) - 1.8325814 * jax.random.uniform(key_of[3], (LAYERS, C), jnp.float32) ** block_scale(key_of[3], (LAYERS, C), ((1, 2),), -0.2, 0.2)), 0.4, 2.5)
    seg_lengths = draw_seg_lengths(jax.random.fold_in(jax.random.fold_in(key_of[7], part), 71), part)
    seg_owner = draw_seg_owner(jax.random.fold_in(jax.random.fold_in(key_of[7], part), 71), part)
    seg_start = draw_seg_start(jax.random.fold_in(jax.random.fold_in(key_of[7], part), 71), part)
    return {"activations": activations, "cotangent": cotangent, "conv_weights": conv_weights, "snake_alpha": snake_alpha, "seg_lengths": seg_lengths, "seg_owner": seg_owner, "seg_start": seg_start}


dilations = (1, 3, 5)


def shift_rows(values, offset):
    if offset == 0:
        return values
    if offset > 0:
        return jnp.pad(values[offset:], ((0, offset), (0, 0)))
    return jnp.pad(values[:offset], ((-offset, 0), (0, 0)))


def live_mask(seg_lengths, seg_owner, seg_start, device):
    position = jnp.arange(TOK_DEV, dtype=jnp.int32)[None, :]
    inside = (seg_owner[:, None] == device) & (position >= seg_start[:, None]) & (position < seg_start[:, None] + seg_lengths[:, None])
    return jnp.any(inside, axis=0).astype(jnp.float32)[:, None]


def one_device(inputs, cotangent, live_rows, conv_weights, snake_alpha):
    stream = inputs.astype(jnp.float32) * live_rows
    saved_streams = []
    saved_snaked = []
    for layer_idx in range(LAYERS):
        dilation = dilations[layer_idx]
        alpha_row = snake_alpha[layer_idx][None, :]
        snaked = (stream + jnp.sin(alpha_row * stream) ** 2 / alpha_row).astype(jnp.bfloat16)
        conv_out = jnp.zeros(stream.shape, jnp.float32)
        for tap_index in range(KERNEL):
            conv_out = conv_out + jnp.dot(shift_rows(snaked, (tap_index - 1) * dilation), conv_weights[layer_idx, tap_index], preferred_element_type=jnp.float32)
        saved_streams.append(stream)
        saved_snaked.append(snaked)
        stream = (stream + conv_out) * live_rows
    residual_out = stream.astype(jnp.bfloat16)
    grad_flow = cotangent.astype(jnp.float32) * live_rows
    weight_parts = [None] * LAYERS
    alpha_parts = [None] * LAYERS
    for layer_idx in reversed(range(LAYERS)):
        dilation = dilations[layer_idx]
        alpha_row = snake_alpha[layer_idx][None, :]
        grad_bf = grad_flow.astype(jnp.bfloat16)
        snaked = saved_snaked[layer_idx]
        weight_parts[layer_idx] = jnp.stack([lax.dot_general(shift_rows(snaked, (tap_index - 1) * dilation), grad_bf, (((0,), (0,)), ((), ())), preferred_element_type=jnp.float32) for tap_index in range(KERNEL)]).astype(jnp.bfloat16)
        snake_back = jnp.zeros(grad_flow.shape, jnp.float32)
        for tap_index in range(KERNEL):
            snake_back = snake_back + lax.dot_general(shift_rows(grad_bf, -(tap_index - 1) * dilation), conv_weights[layer_idx, tap_index], (((1,), (1,)), ((), ())), preferred_element_type=jnp.float32)
        previous = saved_streams[layer_idx]
        alpha_parts[layer_idx] = jnp.sum(snake_back * (previous * jnp.sin(2.0 * alpha_row * previous) / alpha_row - jnp.sin(alpha_row * previous) ** 2 / alpha_row ** 2), axis=0)
        if layer_idx > 0:
            grad_flow = (grad_flow + snake_back * (1.0 + jnp.sin(2.0 * alpha_row * previous))) * live_rows
    return residual_out, jnp.stack(weight_parts), jnp.stack(alpha_parts)


def reference(activations, cotangent, conv_weights, snake_alpha, seg_lengths, seg_owner, seg_start):
    blocks_in = activations.reshape(DATA_DEVS, TOK_DEV, C)
    blocks_grad = cotangent.reshape(DATA_DEVS, TOK_DEV, C)

    def visit(carry, items):
        weight_total, alpha_total = carry
        device, block_in, block_grad = items
        live_rows = live_mask(seg_lengths, seg_owner, seg_start, device)
        block_out, weight_part, alpha_part = one_device(block_in, block_grad, live_rows, conv_weights, snake_alpha)
        return (weight_total + weight_part.astype(jnp.float32), alpha_total + alpha_part), block_out

    start_carry = (jnp.zeros((LAYERS, KERNEL, C, C), jnp.float32), jnp.zeros((LAYERS, C), jnp.float32))
    devices = jnp.arange(DATA_DEVS, dtype=jnp.int32)
    (weight_total, alpha_total), outputs = lax.scan(visit, start_carry, (devices, blocks_in, blocks_grad))
    return outputs.reshape(ROWS, C), weight_total, alpha_total
```

```python
import functools

import jax
import jax.numpy as jnp
from jax import lax
from jax.experimental import pallas as pl
from jax.experimental.pallas import tpu as pltpu
from jax.sharding import PartitionSpec as P

dilations = (1, 3, 5)
F32, BF16 = jnp.float32, jnp.bfloat16
PI_PARTS = (3.140625, 9.67502593994140625e-4, 1.509957990978376432e-7)
SIN_TERMS = (-1.0 / 39916800, 1.0 / 362880, -1.0 / 5040, 1.0 / 120, -1.0 / 6)
COS_TERMS = (1.0 / 479001600, -1.0 / 3628800, 1.0 / 40320, -1.0 / 720, 1.0 / 24, -0.5)
RANGE = 8192.0
CHUNK = 64


def horner(terms, x):
    total = jnp.full_like(x, terms[0])
    for term in terms[1:]:
        total = total * x + term
    return total


def reduced(angle):
    turns = jnp.round(angle * (1.0 / 3.14159265358979))
    for part in PI_PARTS:
        angle = angle - turns * part
    return angle


def sine(angle, exact_range):
    if not exact_range:
        return jnp.sin(angle)
    rest = reduced(angle)
    square = rest * rest
    return rest + rest * (square * horner(SIN_TERMS, square))


def sine_cosine(angle, exact_range):
    if not exact_range:
        return jnp.sin(angle), jnp.cos(angle)
    rest = reduced(angle)
    square = rest * rest
    return (
        rest + rest * (square * horner(SIN_TERMS, square)),
        1.0 + square * horner(COS_TERMS, square),
    )


def by_range(bound, body):
    @pl.when(bound < RANGE)
    def _():
        body(True)

    @pl.when(bound >= RANGE)
    def _():
        body(False)


def wide(live_ref, rows, width):
    return jnp.tile(live_ref[rows, :], (1, width // 128))


def write_snake(stream_ref, alpha_ref, out_ref):
    alpha = alpha_ref[0]
    inverse = 1.0 / alpha
    bound = jnp.max(jnp.abs(stream_ref[...])) * jnp.max(alpha)

    def body(exact_range):
        @pl.loop(0, stream_ref.shape[0] // CHUNK)
        def _(step):
            rows = pl.ds(pl.multiple_of(step * CHUNK, CHUNK), CHUNK)
            stream = stream_ref[rows, :]
            wave = sine(alpha * stream, exact_range)
            out_ref[rows, :] = (stream + wave * wave * inverse).astype(BF16)

    by_range(bound, body)


def moved(values, offset):
    if offset == 0:
        return values
    rows = values.shape[0]
    place = lax.broadcasted_iota(jnp.int32, values.shape, 0)
    turned = pltpu.roll(values, (-offset) % rows, 0)
    inside = place < rows - offset if offset > 0 else place >= -offset
    return jnp.where(inside, turned, 0.0)


def prep_kernel(len_ref, own_ref, start_ref, act_ref, cot_ref, alpha_ref, stream_ref, snake_ref, grad_ref, live_ref):
    replicas = lax.axis_size("replica")
    device = lax.axis_index("dp") * replicas + lax.axis_index("replica")
    rows = act_ref.shape[0]
    place = lax.broadcasted_iota(jnp.int32, (rows, 128), 0)
    live_ref[...] = jnp.zeros((rows, 128), F32)

    @pl.loop(0, len_ref.shape[0])
    def _(clip):
        @pl.when(own_ref[clip] == device)
        def _():
            first = start_ref[clip]
            inside = (place >= first) & (place < first + len_ref[clip])
            live_ref[...] = jnp.where(inside, 1.0, live_ref[...])

    width = act_ref.shape[1]
    live = jnp.tile(live_ref[...], (1, width // 128))
    stream_ref[...] = act_ref[...].astype(F32) * live
    grad_ref[...] = cot_ref[...].astype(F32) * live
    write_snake(stream_ref, alpha_ref, snake_ref)


def forward_own_kernel(dilation, snake_ref, weight_ref, out_ref):
    half = snake_ref.shape[1]
    begin = pl.multiple_of(lax.axis_index("chan") * half, 128)
    part = jnp.dot(snake_ref[...], weight_ref[0, 0, pl.ds(begin, half), :], preferred_element_type=F32)
    step = pl.program_id(0)

    @pl.when(step == 0)
    def _():
        out_ref[...] = moved(part, -dilation)

    @pl.when(step == 1)
    def _():
        out_ref[...] += part

    @pl.when(step == 2)
    def _():
        out_ref[...] += moved(part, dilation)


def forward_partner_kernel(dilation, last, snake_ref, weight_ref, own_ref, old_ref, live_ref, *rest):
    if last:
        result_ref, total_ref = rest
    else:
        alpha_ref, stream_ref, next_ref, total_ref = rest
    half = snake_ref.shape[1]
    begin = pl.multiple_of((1 - lax.axis_index("chan")) * half, 128)
    part = jnp.dot(snake_ref[...], weight_ref[0, 0, pl.ds(begin, half), :], preferred_element_type=F32)
    step = pl.program_id(0)

    @pl.when(step == 0)
    def _():
        total_ref[...] = own_ref[...] + moved(part, -dilation)

    @pl.when(step == 1)
    def _():
        total_ref[...] += part

    @pl.when(step == 2)
    def _():
        live = jnp.tile(live_ref[...], (1, half // 128))
        new = (old_ref[...] + (total_ref[...] + moved(part, dilation))) * live
        if last:
            result_ref[...] = new.astype(BF16)
        else:
            stream_ref[...] = new
            write_snake(stream_ref, alpha_ref, next_ref)


def back_partner_kernel(dilation, grad_ref, weight_ref, shifted_ref, out_ref, total_ref):
    half = grad_ref.shape[1]
    begin = pl.multiple_of((1 - lax.axis_index("chan")) * half, 128)
    step = pl.program_id(0)
    for tap in range(3):

        @pl.when(step == tap)
        def _():
            rounded = grad_ref[...].astype(BF16).astype(F32)
            shifted_ref[...] = moved(rounded, (1 - tap) * dilation).astype(BF16)

    part = lax.dot_general(
        shifted_ref[...], weight_ref[0, 0, pl.ds(begin, half), :], (((1,), (1,)), ((), ())), preferred_element_type=F32
    )

    @pl.when(step == 0)
    def _():
        total_ref[...] = part

    @pl.when(step == 1)
    def _():
        total_ref[...] += part

    @pl.when(step == 2)
    def _():
        out_ref[...] = (total_ref[...] + part).astype(BF16)


def back_own_kernel(shifted_ref, weight_ref, out_ref):
    half = shifted_ref.shape[1]
    begin = pl.multiple_of(lax.axis_index("chan") * half, 128)
    part = lax.dot_general(
        shifted_ref[...], weight_ref[0, 0, pl.ds(begin, half), :], (((1,), (1,)), ((), ())), preferred_element_type=F32
    )
    step = pl.program_id(0)

    @pl.when(step == 0)
    def _():
        out_ref[...] = part

    @pl.when(step > 0)
    def _():
        out_ref[...] += part


def combine_kernel(first, own_ref, partner_ref, stream_ref, alpha_ref, *rest):
    if first:
        (alpha_grad_ref,) = rest
    else:
        old_ref, live_ref, alpha_grad_ref, grad_ref = rest
    alpha = alpha_ref[0]
    inverse = 1.0 / alpha
    bound = jnp.max(jnp.abs(stream_ref[...])) * jnp.max(alpha)
    width = stream_ref.shape[1]

    def body(exact_range):
        def step_body(step, total):
            rows = pl.ds(pl.multiple_of(step * CHUNK, CHUNK), CHUNK)
            stream = stream_ref[rows, :]
            back = own_ref[rows, :] + partner_ref[rows, :].astype(F32)
            sin, cos = sine_cosine(alpha * stream, exact_range)
            double = 2.0 * sin * cos
            ratio = sin * inverse
            term = back * (stream * double * inverse - ratio * ratio)
            if not first:
                live = wide(live_ref, rows, width)
                grad_ref[rows, :] = (old_ref[rows, :] + back * (1.0 + double)) * live
            return total + jnp.sum(term.reshape(CHUNK // 8, 8, width), axis=0)

        total = lax.fori_loop(0, stream_ref.shape[0] // CHUNK, step_body, jnp.zeros((8, width), F32))
        alpha_grad_ref[...] = jnp.sum(total, axis=0, keepdims=True)

    by_range(bound, body)


def block_place(fast, slice_index, part):
    if not fast:
        return slice_index * 2 + part
    apart = jnp.bitwise_xor(slice_index, lax.axis_index("dp"))
    order = (4, 0, 1, 5) if part == 0 else (6, 7, 3, 2)
    return jnp.where(
        apart == 0, order[0], jnp.where(apart == 1, order[1], jnp.where(apart == 2, order[2], order[3]))
    )


def weight_kernel(fast, own_ref, partner_ref, shifted_ref, *rest):
    outs, turned_ref = rest[:-1], rest[-1]
    half = own_ref.shape[1]
    rows = half // 4

    @pl.when(pl.program_id(0) == 0)
    def _():
        chan = lax.axis_index("chan")
        for ref, side in ((own_ref, chan), (partner_ref, 1 - chan)):
            turned = ref[...].T
            for local in range(2):
                for part in range(2):
                    place = block_place(fast, side * 2 + local, part)
                    begin = pl.multiple_of(place * rows, rows)
                    low = (local * 2 + part) * rows
                    turned_ref[pl.ds(begin, rows), :] = turned[low : low + rows, :]

    product = jnp.dot(turned_ref[...], shifted_ref[...], preferred_element_type=F32).astype(BF16)
    size = product.shape[0] // len(outs)
    for index, ref in enumerate(outs):
        ref[...] = product[index * size : (index + 1) * size, :]


def finish_kernel(aliased, *refs):
    mine_ref, other_ref, out_ref = refs[1:] if aliased else refs
    out_ref[0, 0] = mine_ref[...].astype(F32) + other_ref[...].astype(F32)


def full(shape):
    return pl.BlockSpec(shape, lambda *_: (0,) * len(shape))


def struct(shape, dtype):
    return jax.ShapeDtypeStruct(shape, dtype)


def cost(flops, size):
    return pl.CostEstimate(flops=int(flops), bytes_accessed=int(size), transcendentals=0)


PARAMS = pltpu.CompilerParams(vmem_limit_bytes=40 * 1024 * 1024)


def swap(x, axis, other):
    return lax.ppermute(x, axis, [(i, other(i)) for i in range(lax.axis_size(axis))])


def reduce_weights(parts, fast):
    if not fast:
        (whole,) = parts
        summed = lax.psum(lax.psum_scatter(whole, "dp", scatter_dimension=0, tiled=True), "replica")
        return summed, jnp.zeros_like(summed)
    send_a, send_b, keep_a, keep_b = parts
    rows = keep_a.shape[0] // 2
    got_a = swap(send_a, "dp", lambda i: i ^ 1)
    got_b = swap(send_b, "dp", lambda i: i ^ 3)
    late_a = swap(keep_a[rows:] + got_a[rows:], "dp", lambda i: i ^ 3)
    late_b = swap(keep_b[rows:] + got_b[rows:], "dp", lambda i: i ^ 1)

    def total(keep, got, late):
        return (keep[:rows].astype(F32) + got[:rows].astype(F32) + late.astype(F32)).astype(BF16)

    mine = jnp.concatenate([total(keep_a, got_a, late_a), total(keep_b, got_b, late_b)])
    return mine, swap(mine, "replica", lambda i: i ^ 1)


def sum_over(values, axis):
    size = lax.axis_size(axis)
    if size & (size - 1):
        return lax.psum(values, axis)
    apart = 1
    while apart < size:
        values = values + swap(values, axis, lambda i, apart=apart: i ^ apart)
        apart *= 2
    return values


def on_device(activations, cotangent, conv_weights, snake_alpha, seg_lengths, seg_owner, seg_start):
    rows, half = activations.shape
    layers, taps, channels, _ = conv_weights.shape
    fast = lax.axis_size("dp") == 4 and lax.axis_size("replica") == 2
    tile = (rows, half)
    alpha_rows = snake_alpha.reshape(layers, 1, half)
    flops = 2 * rows * half * half * taps
    smem = pl.BlockSpec(memory_space=pltpu.SMEM)

    def weight_spec(layer):
        return pl.BlockSpec((1, 1, channels, half), lambda tap: (layer, tap, 0, 0))

    def alpha_spec(layer):
        return pl.BlockSpec((1, 1, half), lambda *_: (layer, 0, 0))

    stream, snaked, grad, live = pl.pallas_call(
        prep_kernel,
        grid=(1,),
        in_specs=[smem, smem, smem, full(tile), full(tile), alpha_spec(0)],
        out_specs=[full(tile), full(tile), full(tile), full((rows, 128))],
        out_shape=[struct(tile, F32), struct(tile, BF16), struct(tile, F32), struct((rows, 128), F32)],
        compiler_params=PARAMS,
        cost_estimate=cost(40 * rows * half, 14 * rows * half),
        name="prep",
    )(seg_lengths, seg_owner, seg_start, activations, cotangent, alpha_rows)

    streams, mine, partners = [], [], []
    for layer in range(layers):
        dilation = dilations[layer]
        last = layer == layers - 1
        other = swap(snaked, "chan", lambda i: i ^ 1)
        streams.append(stream)
        mine.append(snaked)
        partners.append(other)
        own = pl.pallas_call(
            functools.partial(forward_own_kernel, dilation),
            grid=(taps,),
            in_specs=[full(tile), weight_spec(layer)],
            out_specs=full(tile),
            out_shape=struct(tile, F32),
            compiler_params=PARAMS,
            cost_estimate=cost(flops, 2 * taps * channels * half + 6 * rows * half),
            name="forward_own",
        )(snaked, conv_weights)
        ins = [full(tile), weight_spec(layer), full(tile), full(tile), full((rows, 128))]
        args = [other, conv_weights, own, stream, live]
        if last:
            outs, shapes = full(tile), struct(tile, BF16)
        else:
            ins.append(alpha_spec(layer + 1))
            args.append(alpha_rows)
            outs, shapes = [full(tile)] * 2, [struct(tile, F32), struct(tile, BF16)]
        result = pl.pallas_call(
            functools.partial(forward_partner_kernel, dilation, last),
            grid=(taps,),
            in_specs=ins,
            out_specs=outs,
            out_shape=shapes,
            scratch_shapes=[pltpu.VMEM(tile, F32)],
            compiler_params=PARAMS,
            cost_estimate=cost(flops, 2 * taps * channels * half + 16 * rows * half),
            name="forward_partner",
        )(*args)
        if last:
            residual_out = result
        else:
            stream, snaked = result

    alpha_parts = [None] * layers
    reduced_parts = [None] * layers
    for layer in reversed(range(layers)):
        dilation = dilations[layer]
        first = layer == 0
        shifted, partner_part = pl.pallas_call(
            functools.partial(back_partner_kernel, dilation),
            grid=(taps,),
            in_specs=[full(tile), weight_spec(layer)],
            out_specs=[pl.BlockSpec(tile, lambda tap: (0, tap)), full(tile)],
            out_shape=[struct((rows, taps * half), BF16), struct(tile, BF16)],
            scratch_shapes=[pltpu.VMEM(tile, F32)],
            compiler_params=PARAMS,
            cost_estimate=cost(flops, 2 * taps * channels * half + 12 * rows * half),
            name="back_partner",
        )(grad, conv_weights)
        arrived = swap(partner_part, "chan", lambda i: i ^ 1)
        own_part = pl.pallas_call(
            back_own_kernel,
            grid=(taps,),
            in_specs=[pl.BlockSpec(tile, lambda tap: (0, tap)), weight_spec(layer)],
            out_specs=full(tile),
            out_shape=struct(tile, F32),
            compiler_params=PARAMS,
            cost_estimate=cost(flops, 2 * taps * channels * half + 10 * rows * half),
            name="back_own",
        )(shifted, conv_weights)
        pieces = 4 if fast else 1
        piece = (channels // pieces, taps * half)
        parts = pl.pallas_call(
            functools.partial(weight_kernel, fast),
            grid=(taps,),
            in_specs=[full(tile), full(tile), pl.BlockSpec(tile, lambda tap: (0, tap))],
            out_specs=[pl.BlockSpec((piece[0], half), lambda tap: (0, tap))] * pieces,
            out_shape=[struct(piece, BF16)] * pieces,
            scratch_shapes=[pltpu.VMEM((channels, rows), BF16)],
            compiler_params=PARAMS,
            cost_estimate=cost(2 * flops, 10 * rows * half + 2 * taps * channels * half),
            name="weight_part",
        )(mine[layer], partners[layer], shifted)
        reduced_parts[layer] = reduce_weights(parts, fast)
        ins = [full(tile), full(tile), full(tile), alpha_spec(layer)]
        args = [own_part, arrived, streams[layer], alpha_rows]
        outs, shapes = [full((1, half))], [struct((1, half), F32)]
        if not first:
            ins += [full(tile), full((rows, 128))]
            args += [grad, live]
            outs.append(full(tile))
            shapes.append(struct(tile, F32))
        result = pl.pallas_call(
            functools.partial(combine_kernel, first),
            grid=(1,),
            in_specs=ins,
            out_specs=outs,
            out_shape=shapes,
            compiler_params=PARAMS,
            cost_estimate=cost(60 * rows * half, 18 * rows * half),
            name="combine",
        )(*args)
        alpha_parts[layer] = result[0]
        if not first:
            grad = result[1]

    alpha_grads = sum_over(sum_over(jnp.concatenate(alpha_parts), "replica"), "dp")
    weight_grads = None
    for layer in reversed(range(layers)):
        summed, other = reduced_parts[layer]
        depth = summed.shape[0]
        block = pl.BlockSpec((depth, half), lambda tap: (0, tap))
        aliased = weight_grads is not None
        weight_grads = pl.pallas_call(
            functools.partial(finish_kernel, aliased),
            grid=(taps,),
            in_specs=([pl.BlockSpec(memory_space=pl.ANY)] if aliased else []) + [block, block],
            out_specs=pl.BlockSpec((1, 1, depth, half), lambda tap, layer=layer: (layer, tap, 0, 0)),
            out_shape=struct((layers, taps, depth, half), F32),
            input_output_aliases={0: 0} if aliased else {},
            compiler_params=PARAMS,
            cost_estimate=cost(taps * depth * half, 8 * taps * depth * half),
            name="finish",
        )(*(([weight_grads] if aliased else []) + [summed, other]))
    return (residual_out, weight_grads, alpha_grads)


def solution(mesh):
    return jax.shard_map(
        on_device,
        mesh=mesh,
        in_specs=(
            P(("groups", "dp", "replica"), "chan"),
            P(("groups", "dp", "replica"), "chan"),
            P(None, None, None, "chan"),
            P(None, "chan"),
            P("groups"),
            P("groups"),
            P("groups"),
        ),
        out_specs=(
            P(("groups", "dp", "replica"), "chan"),
            P("groups", None, "dp", "chan"),
            P("groups", "chan"),
        ),
        check_vma=False,
    )
```

```python
import functools
import math

import jax
import jax.numpy as jnp
from jax import lax
from jax.experimental import pallas as pl
from jax.experimental.pallas import tpu as pltpu
from jax.sharding import PartitionSpec as P

dilations = (1, 3, 5)
F32, BF16 = jnp.float32, jnp.bfloat16
ANY_HBM = pl.BlockSpec(memory_space=pltpu.HBM)
IN_VMEM = pl.BlockSpec(memory_space=pltpu.VMEM)
DMA = pltpu.SemaphoreType.DMA
PI_PARTS = (3.140625, 9.67502593994140625e-4, 1.509957990978376432e-7)
SIN_TERMS = (-1.0 / 39916800, 1.0 / 362880, -1.0 / 5040, 1.0 / 120, -1.0 / 6)
COS_TERMS = (1.0 / 479001600, -1.0 / 3628800, 1.0 / 40320, -1.0 / 720, 1.0 / 24, -0.5)
RANGE = 8192.0
CHUNK = 64


def horner(terms, x):
    total = jnp.full_like(x, terms[0])
    for term in terms[1:]:
        total = total * x + term
    return total


def reduced(angle):
    turns = jnp.round(angle * (1.0 / 3.14159265358979))
    for part in PI_PARTS:
        angle = angle - turns * part
    return angle


def sine(angle, exact_range):
    if not exact_range:
        return jnp.sin(angle)
    rest = reduced(angle)
    square = rest * rest
    return rest + rest * (square * horner(SIN_TERMS, square))


def sine_cosine(angle, exact_range):
    if not exact_range:
        return jnp.sin(angle), jnp.cos(angle)
    rest = reduced(angle)
    square = rest * rest
    return (
        rest + rest * (square * horner(SIN_TERMS, square)),
        1.0 + square * horner(COS_TERMS, square),
    )


def by_range(bound, body):
    @pl.when(bound < RANGE)
    def _():
        body(True)

    @pl.when(bound >= RANGE)
    def _():
        body(False)


def write_snake(stream_ref, alpha, out_ref):
    inverse = 1.0 / alpha
    bound = jnp.max(jnp.abs(stream_ref[...])) * jnp.max(alpha)

    def body(exact_range):
        @pl.loop(0, stream_ref.shape[0] // CHUNK)
        def _(step):
            rows = pl.ds(pl.multiple_of(step * CHUNK, CHUNK), CHUNK)
            stream = stream_ref[rows, :]
            wave = sine(alpha * stream, exact_range)
            out_ref[rows, :] = (stream + wave * wave * inverse).astype(BF16)

    by_range(bound, body)


def moved(values, offset):
    if offset == 0:
        return values
    rows = values.shape[0]
    place = lax.broadcasted_iota(jnp.int32, values.shape, 0)
    turned = pltpu.roll(values, (-offset) % rows, 0)
    inside = place < rows - offset if offset > 0 else place >= -offset
    return jnp.where(inside, turned, 0.0)


def write_shifts(values_ref, out_ref, dilation):
    width = values_ref.shape[1]
    values = values_ref[...].astype(F32)
    for tap in range(3):
        out_ref[:, tap * width : (tap + 1) * width] = moved(values, (tap - 1) * dilation).astype(BF16)


def chan_begin(side, half):
    chan = lax.axis_index("chan")
    return pl.multiple_of((chan if side == 0 else 1 - chan) * half, half)


def prep_kernel(
    len_hbm, own_hbm, start_hbm, act_hbm, cot_hbm, alpha_hbm,
    stream_ref, snake_ref, grad_ref, live_ref, alpha_ref,
    len_ref, own_ref, start_ref, act_ref, cot_ref, sems,
):
    pairs = (
        (len_hbm, len_ref), (own_hbm, own_ref), (start_hbm, start_ref),
        (alpha_hbm, alpha_ref), (act_hbm, act_ref), (cot_hbm, cot_ref),
    )
    copies = [pltpu.make_async_copy(a, b, sems.at[i]) for i, (a, b) in enumerate(pairs)]
    for copy in copies:
        copy.start()
    replicas = lax.axis_size("replica")
    device = lax.axis_index("dp") * replicas + lax.axis_index("replica")
    rows, width = act_ref.shape
    place = lax.broadcasted_iota(jnp.int32, (rows, 128), 0)
    live_ref[...] = jnp.zeros((rows, 128), F32)
    for copy in copies[:3]:
        copy.wait()

    @pl.loop(0, len_ref.shape[0])
    def _(clip):
        @pl.when(own_ref[clip] == device)
        def _():
            first = start_ref[clip]
            inside = (place >= first) & (place < first + len_ref[clip])
            live_ref[...] = jnp.where(inside, 1.0, live_ref[...])

    live = jnp.tile(live_ref[...], (1, width // 128))
    for copy in copies[3:5]:
        copy.wait()
    stream_ref[...] = act_ref[...].astype(F32) * live
    write_snake(stream_ref, alpha_ref[0:1, :], snake_ref)
    copies[5].wait()
    grad_ref[...] = (cot_ref[...].astype(F32) * live).astype(BF16)


def fetch(layer, side, weight_hbm, held, sems, beside):
    half = weight_hbm.shape[3]
    begin = chan_begin(side, half)
    copies = []
    for tap in range(3):
        span = pl.ds(tap * half, half)
        target = held.at[:, span] if beside else held.at[span, :]
        copies.append(
            pltpu.make_async_copy(weight_hbm.at[layer, tap, pl.ds(begin, half), :], target, sems.at[tap])
        )
    for copy in copies:
        copy.start()
    return copies


def forward_own_kernel(layer, snake_ref, weight_hbm, out_ref, shifts_ref, held, sems):
    copies = fetch(layer, 0, weight_hbm, held, sems, False)
    write_shifts(snake_ref, shifts_ref, dilations[layer])
    for copy in copies:
        copy.wait()
    out_ref[...] = jnp.dot(shifts_ref[...], held[...], preferred_element_type=F32)


def forward_partner_kernel(layer, last, snake_ref, weight_hbm, own_ref, old_ref, live_ref, *rest):
    if last:
        result_ref, shifts_ref, held, sems = rest
    else:
        alpha_ref, result_ref, next_ref, shifts_ref, held, sems = rest
    copies = fetch(layer, 1, weight_hbm, held, sems, False)
    write_shifts(snake_ref, shifts_ref, dilations[layer])
    for copy in copies:
        copy.wait()
    part = jnp.dot(shifts_ref[...], held[...], preferred_element_type=F32)
    live = jnp.tile(live_ref[...], (1, old_ref.shape[1] // 128))
    new = (old_ref[...] + (own_ref[...] + part)) * live
    result_ref[...] = new.astype(result_ref.dtype)
    if not last:
        write_snake(result_ref, alpha_ref[layer + 1 : layer + 2, :], next_ref)


def back_partner_kernel(layer, grad_ref, weight_hbm, shifted_ref, out_ref, held, sems):
    copies = fetch(layer, 1, weight_hbm, held, sems, True)
    write_shifts(grad_ref, shifted_ref, -dilations[layer])
    for copy in copies:
        copy.wait()
    out_ref[...] = lax.dot_general(
        shifted_ref[...], held[...], (((1,), (1,)), ((), ())), preferred_element_type=F32
    ).astype(BF16)


def back_own_kernel(layer, shifted_ref, weight_hbm, out_ref, held, sems):
    for copy in fetch(layer, 0, weight_hbm, held, sems, True):
        copy.wait()
    out_ref[...] = lax.dot_general(
        shifted_ref[...], held[...], (((1,), (1,)), ((), ())), preferred_element_type=F32
    )


def combine_kernel(layer, own_ref, partner_ref, stream_ref, alphas_ref, *rest):
    if layer == 0:
        (alpha_grad_ref,) = rest
    elif len(rest) == 5:
        old_ref, live_ref, alpha_grad_ref, grad_ref, rounded_ref = rest
    else:
        old_ref, live_ref, alpha_grad_ref, rounded_ref = rest
        grad_ref = None
    alpha = alphas_ref[layer : layer + 1, :]
    inverse = 1.0 / alpha
    bound = jnp.max(jnp.abs(stream_ref[...])) * jnp.max(alpha)
    width = stream_ref.shape[1]

    def body(exact_range):
        def step_body(step, total):
            rows = pl.ds(pl.multiple_of(step * CHUNK, CHUNK), CHUNK)
            stream = stream_ref[rows, :]
            back = own_ref[rows, :] + partner_ref[rows, :].astype(F32)
            sin, cos = sine_cosine(alpha * stream, exact_range)
            double = 2.0 * sin * cos
            ratio = sin * inverse
            term = back * (stream * double * inverse - ratio * ratio)
            if layer > 0:
                live = jnp.tile(live_ref[rows, :], (1, width // 128))
                grad = (old_ref[rows, :].astype(F32) + back * (1.0 + double)) * live
                if grad_ref is not None:
                    grad_ref[rows, :] = grad
                rounded_ref[rows, :] = grad.astype(BF16)
            return total + jnp.sum(term.reshape(CHUNK // 8, 8, width), axis=0)

        total = lax.fori_loop(0, stream_ref.shape[0] // CHUNK, step_body, jnp.zeros((8, width), F32))
        alpha_grad_ref[...] = jnp.sum(total, axis=0, keepdims=True)

    by_range(bound, body)


def block_place(fast, slice_index, part):
    if not fast:
        return slice_index * 2 + part
    apart = jnp.bitwise_xor(slice_index, lax.axis_index("dp"))
    order = (4, 0, 1, 5) if part == 0 else (6, 7, 3, 2)
    return jnp.where(
        apart == 0, order[0], jnp.where(apart == 1, order[1], jnp.where(apart == 2, order[2], order[3]))
    )


def place_rows(fast, turned, side, size, target_ref, columns):
    for local in range(2):
        for part in range(2):
            begin = pl.multiple_of(block_place(fast, side * 2 + local, part) * size, size)
            low = (local * 2 + part) * size
            target_ref[pl.ds(begin, size), columns] = turned[low : low + size, :]


def weight_kernel(fast, own_ref, partner_ref, shifted_ref, *rest):
    outs, turned_ref = rest[:-1], rest[-1]
    rows, half = own_ref.shape
    chan = lax.axis_index("chan")
    for ref, side in ((own_ref, chan), (partner_ref, 1 - chan)):
        place_rows(fast, ref[...].T, side, half // 4, turned_ref, slice(0, rows))
    for tap in range(3):
        span = slice(tap * half, (tap + 1) * half)
        product = jnp.dot(turned_ref[...], shifted_ref[:, span], preferred_element_type=F32).astype(BF16)
        size = product.shape[0] // len(outs)
        for index, ref in enumerate(outs):
            ref[:, span] = product[index * size : (index + 1) * size, :]


def pick_parts(turned_ref, part, size):
    begin = pl.multiple_of(part * size, size)
    return [turned_ref[pl.ds(local * 2 * size + begin, size), :] for local in range(2)]


def turn_kernel(*refs):
    ins, out_ref, turned_ref = refs[:-2], refs[-2], refs[-1]
    size = ins[0].shape[1] // 4
    for index, ref in enumerate(ins):
        turned_ref[...] = ref[...].T
        low = index * 2 * size
        for local, piece in enumerate(pick_parts(turned_ref, 1 - lax.axis_index("replica"), size)):
            out_ref[low + local * size : low + (local + 1) * size, :] = piece


def paired_weight_kernel(
    layer, index, own_ref, partner_ref, shifted_ref, across_ref, across_other_ref, grad_ref, *rest
):
    outs, (turned_ref, half_ref, far_ref) = rest[:-3], rest[-3:]
    rows, half = own_ref.shape
    size = half // 4
    chan = lax.axis_index("chan")
    mine = lax.axis_index("replica")
    low = index * 2 * size
    for ref, side in ((own_ref, chan), (partner_ref, 1 - chan)):
        half_ref[...] = ref[...].T
        both = jnp.concatenate(pick_parts(half_ref, mine, size), 0)
        place_rows(True, both, side, size // 2, turned_ref, slice(0, rows))
    for ref, side in ((across_ref, chan), (across_other_ref, 1 - chan)):
        place_rows(True, ref[low : low + 2 * size, :], side, size // 2, turned_ref, slice(rows, 2 * rows))
    write_shifts(grad_ref, far_ref, -dilations[layer])
    for tap in range(3):
        span = slice(tap * half, (tap + 1) * half)
        product = jnp.dot(turned_ref[:, 0:rows], shifted_ref[:, span], preferred_element_type=F32)
        product += jnp.dot(turned_ref[:, rows:], far_ref[:, span], preferred_element_type=F32)
        product = product.astype(BF16)
        size_out = product.shape[0] // len(outs)
        for place, ref in enumerate(outs):
            ref[:, span] = product[place * size_out : (place + 1) * size_out, :]


def finish_kernel(modes, *refs):
    out_ref = refs[-1]
    half = out_ref.shape[3]
    for layer, paired in enumerate(modes):
        mine_ref, other_ref = refs[2 * layer], refs[2 * layer + 1]
        for tap in range(3):
            span = slice(tap * half, (tap + 1) * half)
            mine, other = mine_ref[:, span].astype(F32), other_ref[:, span].astype(F32)
            if paired:
                size = mine.shape[0]
                begin = lax.axis_index("replica") * size
                out_ref[layer, tap, pl.ds(pl.multiple_of(begin, size), size), :] = mine
                out_ref[layer, tap, pl.ds(pl.multiple_of(size - begin, size), size), :] = other
            else:
                out_ref[layer, tap] = mine + other


def struct(shape, dtype):
    return jax.ShapeDtypeStruct(shape, dtype)


def call(kernel, name, ins, outs, scratch, flops, *args):
    single = not isinstance(outs, list)
    size = sum(a.size * a.dtype.itemsize for a in args if a.size < 2000000)
    size += sum(math.prod(o.shape) * o.dtype.itemsize for o in ([outs] if single else outs))
    return pl.pallas_call(
        kernel,
        in_specs=[ANY_HBM if i else IN_VMEM for i in ins],
        out_specs=IN_VMEM if single else [IN_VMEM] * len(outs),
        out_shape=outs,
        scratch_shapes=scratch,
        compiler_params=pltpu.CompilerParams(vmem_limit_bytes=24 * 1024 * 1024),
        cost_estimate=pl.CostEstimate(flops=int(flops), bytes_accessed=int(size), transcendentals=0),
        name=name,
    )(*args)


def swap(x, axis, other):
    return lax.ppermute(x, axis, [(i, other(i)) for i in range(lax.axis_size(axis))])


def after(value, *others):
    return lax.optimization_barrier((value,) + others)[0]


def reduce_weights(parts, fast):
    if not fast:
        return lax.psum(lax.psum_scatter(parts[0], "dp", scatter_dimension=0, tiled=True), "replica")
    send_a, send_b, keep_a, keep_b = parts
    rows = keep_a.shape[0] // 2
    got_a = swap(send_a, "dp", lambda i: i ^ 1)
    got_b = swap(send_b, "dp", lambda i: i ^ 3)
    late_a = swap(keep_a[rows:] + got_a[rows:], "dp", lambda i: i ^ 3)
    late_b = swap(keep_b[rows:] + got_b[rows:], "dp", lambda i: i ^ 1)

    def total(keep, got, late):
        return (keep[:rows].astype(F32) + got[:rows].astype(F32) + late.astype(F32)).astype(BF16)

    return jnp.concatenate([total(keep_a, got_a, late_a), total(keep_b, got_b, late_b)])


def sum_over(values, axis):
    size = lax.axis_size(axis)
    if size & (size - 1):
        return lax.psum(values, axis)
    apart = 1
    while apart < size:
        values = values + swap(values, axis, lambda i, apart=apart: i ^ apart)
        apart *= 2
    return values


def on_device(activations, cotangent, conv_weights, snake_alpha, seg_lengths, seg_owner, seg_start):
    rows, half = activations.shape
    layers, taps, channels, _ = conv_weights.shape
    fast = lax.axis_size("dp") == 4 and lax.axis_size("replica") == 2
    paired = [fast and layer < layers - 1 for layer in range(layers)]
    tile, triple = (rows, half), (rows, taps * half)
    flops = 2 * rows * half * half * taps
    clips = seg_lengths.shape
    by_rows = [pltpu.VMEM((taps * half, half), BF16), DMA((3,))]
    by_columns = [pltpu.VMEM((half, taps * half), BF16), DMA((3,))]

    stream, snaked, grad, live, alphas = call(
        prep_kernel, "prep", [1] * 6,
        [struct(tile, F32), struct(tile, BF16), struct(tile, BF16), struct((rows, 128), F32), struct(snake_alpha.shape, F32)],
        [pltpu.SMEM(clips, jnp.int32)] * 3 + [pltpu.VMEM(tile, BF16)] * 2 + [DMA((6,))],
        40 * rows * half,
        seg_lengths, seg_owner, seg_start, activations, cotangent, snake_alpha,
    )

    streams, mine, partners = [], [], []
    for layer in range(layers):
        last = layer == layers - 1
        other = swap(snaked, "chan", lambda i: i ^ 1)
        streams.append(stream)
        mine.append(snaked)
        partners.append(other)
        own = call(
            functools.partial(forward_own_kernel, layer), "forward_own", [0, 1], struct(tile, F32),
            [pltpu.VMEM(triple, BF16)] + by_rows, flops, snaked, conv_weights,
        )
        outs = struct(tile, BF16) if last else [struct(tile, F32), struct(tile, BF16)]
        result = call(
            functools.partial(forward_partner_kernel, layer, last), "forward_partner",
            [0, 1, 0, 0, 0] + ([] if last else [0]), outs,
            [pltpu.VMEM(triple, BF16)] + by_rows, flops,
            other, conv_weights, own, stream, live, *([] if last else [alphas]),
        )
        if last:
            residual_out = result
        else:
            stream, snaked = result

    if any(paired):
        sources = [layer for layer in range(layers) if paired[layer]]
        turned = call(
            turn_kernel, "turn", [0] * len(sources), struct((len(sources) * half // 2, rows), BF16),
            [pltpu.VMEM((half, rows), BF16)], 10 * rows * half, *[mine[layer] for layer in sources],
        )
        across = swap(turned, "replica", lambda i: i ^ 1)
        across_other = swap(across, "chan", lambda i: i ^ 1)

    alpha_parts = [None] * layers
    summed = [None] * layers
    rounded = grad
    for layer in reversed(range(layers)):
        shifted, partner_part = call(
            functools.partial(back_partner_kernel, layer), "back_partner", [0, 1],
            [struct(triple, BF16), struct(tile, BF16)], by_columns, flops, rounded, conv_weights,
        )
        arrived = swap(partner_part, "chan", lambda i: i ^ 1)
        own_part = call(
            functools.partial(back_own_kernel, layer), "back_own", [0, 1], struct(tile, F32),
            by_columns, flops, shifted, conv_weights,
        )
        pieces = 4 if fast else 1
        if paired[layer]:
            far = swap(rounded, "replica", lambda i: i ^ 1)
            piece = struct((channels // 2 // pieces, taps * half), BF16)
            parts = call(
                functools.partial(paired_weight_kernel, layer, sources.index(layer)), "paired_weight", [0] * 6,
                [piece] * pieces,
                [pltpu.VMEM((half, 2 * rows), BF16), pltpu.VMEM((half, rows), BF16), pltpu.VMEM(triple, BF16)],
                2 * flops, mine[layer], partners[layer], shifted, across, across_other, far,
            )
        else:
            piece = struct((channels // pieces, taps * half), BF16)
            parts = call(
                functools.partial(weight_kernel, fast), "weight", [0] * 3, [piece] * pieces,
                [pltpu.VMEM((channels, rows), BF16)], 2 * flops, mine[layer], partners[layer], shifted,
            )
        summed[layer] = reduce_weights(parts, fast)
        args = [own_part, arrived, streams[layer], alphas]
        outs = [struct((1, half), F32)]
        if layer > 0:
            args += [grad, live]
            outs += [struct(tile, F32)] * (layer > 1) + [struct(tile, BF16)]
        result = call(
            functools.partial(combine_kernel, layer), "combine", [0] * len(args), outs, [], 60 * rows * half, *args
        )
        alpha_parts[layer] = result[0]
        if layer > 0:
            grad, rounded = result[1], result[-1]

    alpha_grads = sum_over(sum_over(jnp.concatenate(alpha_parts), "replica"), "dp")
    pairs = []
    for values in summed:
        pairs += [values, swap(values, "replica", lambda i: i ^ 1) if fast else jnp.zeros_like(values)]
    depth = channels // lax.axis_size("dp")
    weight_grads = call(
        functools.partial(finish_kernel, tuple(paired)), "finish", [0] * len(pairs),
        struct((layers, taps, depth, half), F32), [], layers * taps * depth * half, *pairs,
    )
    return (residual_out, weight_grads, alpha_grads)


def solution(mesh):
    return jax.shard_map(
        on_device,
        mesh=mesh,
        in_specs=(
            P(("groups", "dp", "replica"), "chan"),
            P(("groups", "dp", "replica"), "chan"),
            P(None, None, None, "chan"),
            P(None, "chan"),
            P("groups"),
            P("groups"),
            P("groups"),
        ),
        out_specs=(
            P(("groups", "dp", "replica"), "chan"),
            P("groups", None, "dp", "chan"),
            P("groups", "chan"),
        ),
        check_vma=False,
    )
```

```python
import functools
import math

import jax
import jax.numpy as jnp
from jax import lax
from jax.experimental import pallas as pl
from jax.experimental.pallas import tpu as pltpu
from jax.sharding import PartitionSpec as P

dilations = (1, 3, 5)
F32, BF16 = jnp.float32, jnp.bfloat16
ANY_HBM = pl.BlockSpec(memory_space=pltpu.HBM)
IN_VMEM = pl.BlockSpec(memory_space=pltpu.VMEM)
DMA = pltpu.SemaphoreType.DMA
PI_PARTS = (3.140625, 9.67502593994140625e-4, 1.509957990978376432e-7)
SIN_TERMS = (-1.0 / 39916800, 1.0 / 362880, -1.0 / 5040, 1.0 / 120, -1.0 / 6)
COS_TERMS = (1.0 / 479001600, -1.0 / 3628800, 1.0 / 40320, -1.0 / 720, 1.0 / 24, -0.5)
RANGE = 8192.0
CHUNK = 64


def horner(terms, x):
    total = jnp.full_like(x, terms[0])
    for term in terms[1:]:
        total = total * x + term
    return total


def reduced(angle):
    turns = jnp.round(angle * (1.0 / 3.14159265358979))
    for part in PI_PARTS:
        angle = angle - turns * part
    return angle


def sine(angle, exact_range):
    if not exact_range:
        return jnp.sin(angle)
    rest = reduced(angle)
    square = rest * rest
    return rest + rest * (square * horner(SIN_TERMS, square))


def sine_cosine(angle, exact_range):
    if not exact_range:
        return jnp.sin(angle), jnp.cos(angle)
    rest = reduced(angle)
    square = rest * rest
    return (
        rest + rest * (square * horner(SIN_TERMS, square)),
        1.0 + square * horner(COS_TERMS, square),
    )


def by_range(bound, body):
    @pl.when(bound < RANGE)
    def _():
        body(True)

    @pl.when(bound >= RANGE)
    def _():
        body(False)


def write_snake(stream_ref, alpha, out_ref):
    inverse = 1.0 / alpha
    bound = jnp.max(jnp.abs(stream_ref[...])) * jnp.max(alpha)

    def body(exact_range):
        @pl.loop(0, stream_ref.shape[0] // CHUNK)
        def _(step):
            rows = pl.ds(pl.multiple_of(step * CHUNK, CHUNK), CHUNK)
            stream = stream_ref[rows, :]
            wave = sine(alpha * stream, exact_range)
            out_ref[rows, :] = (stream + wave * wave * inverse).astype(BF16)

    by_range(bound, body)


def moved(values, offset):
    if offset == 0:
        return values
    rows = values.shape[0]
    place = lax.broadcasted_iota(jnp.int32, values.shape, 0)
    turned = pltpu.roll(values, (-offset) % rows, 0)
    inside = place < rows - offset if offset > 0 else place >= -offset
    return jnp.where(inside, turned, 0.0)


def write_shifts(values_ref, out_ref, dilation):
    width = values_ref.shape[1]
    values = values_ref[...].astype(F32)
    for tap in range(3):
        out_ref[:, tap * width : (tap + 1) * width] = moved(values, (tap - 1) * dilation).astype(BF16)


def chan_begin(side, half):
    chan = lax.axis_index("chan")
    return pl.multiple_of((chan if side == 0 else 1 - chan) * half, half)


def prep_kernel(
    len_hbm, own_hbm, start_hbm, act_hbm, cot_hbm, alpha_hbm,
    stream_ref, snake_ref, grad_ref, live_ref, alpha_ref,
    len_ref, own_ref, start_ref, act_ref, cot_ref, sems,
):
    pairs = (
        (len_hbm, len_ref), (own_hbm, own_ref), (start_hbm, start_ref),
        (alpha_hbm, alpha_ref), (act_hbm, act_ref), (cot_hbm, cot_ref),
    )
    copies = [pltpu.make_async_copy(a, b, sems.at[i]) for i, (a, b) in enumerate(pairs)]
    for copy in copies:
        copy.start()
    replicas = lax.axis_size("replica")
    device = lax.axis_index("dp") * replicas + lax.axis_index("replica")
    rows, width = act_ref.shape
    place = lax.broadcasted_iota(jnp.int32, (rows, 128), 0)
    live_ref[...] = jnp.zeros((rows, 128), F32)
    for copy in copies[:3]:
        copy.wait()

    @pl.loop(0, len_ref.shape[0])
    def _(clip):
        @pl.when(own_ref[clip] == device)
        def _():
            first = start_ref[clip]
            inside = (place >= first) & (place < first + len_ref[clip])
            live_ref[...] = jnp.where(inside, 1.0, live_ref[...])

    live = jnp.tile(live_ref[...], (1, width // 128))
    for copy in copies[3:5]:
        copy.wait()
    stream_ref[...] = act_ref[...].astype(F32) * live
    write_snake(stream_ref, alpha_ref[0:1, :], snake_ref)
    copies[5].wait()
    grad_ref[...] = (cot_ref[...].astype(F32) * live).astype(BF16)


def fetch(layer, side, weight_hbm, held, sems, beside):
    half = weight_hbm.shape[3]
    begin = chan_begin(side, half)
    copies = []
    for tap in range(3):
        span = pl.ds(tap * half, half)
        target = held.at[:, span] if beside else held.at[span, :]
        copies.append(
            pltpu.make_async_copy(weight_hbm.at[layer, tap, pl.ds(begin, half), :], target, sems.at[tap])
        )
    for copy in copies:
        copy.start()
    return copies


def forward_own_kernel(layer, snake_ref, weight_hbm, out_ref, shifts_ref, held, sems):
    copies = fetch(layer, 0, weight_hbm, held, sems, False)
    write_shifts(snake_ref, shifts_ref, dilations[layer])
    for copy in copies:
        copy.wait()
    out_ref[...] = jnp.dot(shifts_ref[...], held[...], preferred_element_type=F32)


def forward_partner_kernel(layer, last, snake_ref, weight_hbm, own_ref, old_ref, live_ref, *rest):
    if last:
        result_ref, shifts_ref, held, sems = rest
    else:
        alpha_ref, result_ref, next_ref, shifts_ref, held, sems = rest
    copies = fetch(layer, 1, weight_hbm, held, sems, False)
    write_shifts(snake_ref, shifts_ref, dilations[layer])
    for copy in copies:
        copy.wait()
    part = jnp.dot(shifts_ref[...], held[...], preferred_element_type=F32)
    live = jnp.tile(live_ref[...], (1, old_ref.shape[1] // 128))
    new = (old_ref[...] + (own_ref[...] + part)) * live
    result_ref[...] = new.astype(result_ref.dtype)
    if not last:
        write_snake(result_ref, alpha_ref[layer + 1 : layer + 2, :], next_ref)


def back_partner_kernel(layer, grad_ref, weight_hbm, shifted_ref, out_ref, held, sems):
    copies = fetch(layer, 1, weight_hbm, held, sems, True)
    write_shifts(grad_ref, shifted_ref, -dilations[layer])
    for copy in copies:
        copy.wait()
    out_ref[...] = lax.dot_general(
        shifted_ref[...], held[...], (((1,), (1,)), ((), ())), preferred_element_type=F32
    ).astype(BF16)


def back_own_kernel(layer, shifted_ref, weight_hbm, out_ref, held, sems):
    for copy in fetch(layer, 0, weight_hbm, held, sems, True):
        copy.wait()
    out_ref[...] = lax.dot_general(
        shifted_ref[...], held[...], (((1,), (1,)), ((), ())), preferred_element_type=F32
    )


def combine_kernel(layer, own_ref, partner_ref, stream_ref, alphas_ref, *rest):
    if layer == 0:
        (alpha_grad_ref,) = rest
    elif len(rest) == 5:
        old_ref, live_ref, alpha_grad_ref, grad_ref, rounded_ref = rest
    else:
        old_ref, live_ref, alpha_grad_ref, rounded_ref = rest
        grad_ref = None
    alpha = alphas_ref[layer : layer + 1, :]
    inverse = 1.0 / alpha
    bound = jnp.max(jnp.abs(stream_ref[...])) * jnp.max(alpha)
    width = stream_ref.shape[1]

    def body(exact_range):
        def step_body(step, total):
            rows = pl.ds(pl.multiple_of(step * CHUNK, CHUNK), CHUNK)
            stream = stream_ref[rows, :]
            back = own_ref[rows, :] + partner_ref[rows, :].astype(F32)
            sin, cos = sine_cosine(alpha * stream, exact_range)
            double = 2.0 * sin * cos
            ratio = sin * inverse
            term = back * (stream * double * inverse - ratio * ratio)
            if layer > 0:
                live = jnp.tile(live_ref[rows, :], (1, width // 128))
                grad = (old_ref[rows, :].astype(F32) + back * (1.0 + double)) * live
                if grad_ref is not None:
                    grad_ref[rows, :] = grad
                rounded_ref[rows, :] = grad.astype(BF16)
            return total + jnp.sum(term.reshape(CHUNK // 8, 8, width), axis=0)

        total = lax.fori_loop(0, stream_ref.shape[0] // CHUNK, step_body, jnp.zeros((8, width), F32))
        alpha_grad_ref[...] = jnp.sum(total, axis=0, keepdims=True)

    by_range(bound, body)


def block_place(fast, slice_index, part):
    if not fast:
        return slice_index * 2 + part
    apart = jnp.bitwise_xor(slice_index, lax.axis_index("dp"))
    order = (4, 0, 1, 5) if part == 0 else (6, 7, 3, 2)
    return jnp.where(
        apart == 0, order[0], jnp.where(apart == 1, order[1], jnp.where(apart == 2, order[2], order[3]))
    )


def place_rows(fast, turned, side, size, target_ref, columns):
    for local in range(2):
        for part in range(2):
            begin = pl.multiple_of(block_place(fast, side * 2 + local, part) * size, size)
            low = (local * 2 + part) * size
            target_ref[pl.ds(begin, size), columns] = turned[low : low + size, :]


def weight_kernel(fast, own_ref, partner_ref, shifted_ref, *rest):
    outs, turned_ref = rest[:-1], rest[-1]
    rows, half = own_ref.shape
    chan = lax.axis_index("chan")
    for ref, side in ((own_ref, chan), (partner_ref, 1 - chan)):
        place_rows(fast, ref[...].T, side, half // 4, turned_ref, slice(0, rows))
    for tap in range(3):
        span = slice(tap * half, (tap + 1) * half)
        product = jnp.dot(turned_ref[...], shifted_ref[:, span], preferred_element_type=F32).astype(BF16)
        size = product.shape[0] // len(outs)
        for index, ref in enumerate(outs):
            ref[:, span] = product[index * size : (index + 1) * size, :]


def pick_parts(turned_ref, part, size):
    begin = pl.multiple_of(part * size, size)
    return [turned_ref[pl.ds(local * 2 * size + begin, size), :] for local in range(2)]


def turn_kernel(*refs):
    ins, out_ref, turned_ref = refs[:-2], refs[-2], refs[-1]
    size = ins[0].shape[1] // 4
    for index, ref in enumerate(ins):
        turned_ref[...] = ref[...].T
        low = index * 2 * size
        for local, piece in enumerate(pick_parts(turned_ref, 1 - lax.axis_index("replica"), size)):
            out_ref[low + local * size : low + (local + 1) * size, :] = piece


def paired_weight_kernel(
    layer, index, own_ref, partner_ref, shifted_ref, across_ref, across_other_ref, grad_ref, *rest
):
    outs, (turned_ref, half_ref, far_ref) = rest[:-3], rest[-3:]
    rows, half = own_ref.shape
    size = half // 4
    chan = lax.axis_index("chan")
    mine = lax.axis_index("replica")
    low = index * 2 * size
    for ref, side in ((own_ref, chan), (partner_ref, 1 - chan)):
        half_ref[...] = ref[...].T
        both = jnp.concatenate(pick_parts(half_ref, mine, size), 0)
        place_rows(True, both, side, size // 2, turned_ref, slice(0, rows))
    for ref, side in ((across_ref, chan), (across_other_ref, 1 - chan)):
        place_rows(True, ref[low : low + 2 * size, :], side, size // 2, turned_ref, slice(rows, 2 * rows))
    write_shifts(grad_ref, far_ref, -dilations[layer])
    for tap in range(3):
        span = slice(tap * half, (tap + 1) * half)
        product = jnp.dot(turned_ref[:, 0:rows], shifted_ref[:, span], preferred_element_type=F32)
        product += jnp.dot(turned_ref[:, rows:], far_ref[:, span], preferred_element_type=F32)
        product = product.astype(BF16)
        size_out = product.shape[0] // len(outs)
        for place, ref in enumerate(outs):
            ref[:, span] = product[place * size_out : (place + 1) * size_out, :]


def finish_kernel(modes, *refs):
    out_ref = refs[-1]
    half = out_ref.shape[3]
    for layer, paired in enumerate(modes):
        mine_ref, other_ref = refs[2 * layer], refs[2 * layer + 1]
        for tap in range(3):
            span = slice(tap * half, (tap + 1) * half)
            mine, other = mine_ref[:, span].astype(F32), other_ref[:, span].astype(F32)
            if paired:
                size = mine.shape[0]
                begin = lax.axis_index("replica") * size
                out_ref[layer, tap, pl.ds(pl.multiple_of(begin, size), size), :] = mine
                out_ref[layer, tap, pl.ds(pl.multiple_of(size - begin, size), size), :] = other
            else:
                out_ref[layer, tap] = mine + other


def fold_kernel(keep_a, got_a, keep_b, got_b, send_a, send_b):
    rows = send_a.shape[0]
    for keep, got, send in ((keep_a, got_a, send_a), (keep_b, got_b, send_b)):
        send[...] = (keep[rows:, :].astype(F32) + got[rows:, :].astype(F32)).astype(BF16)


def total_kernel(keep_a, got_a, late_a, keep_b, got_b, late_b, out_ref):
    rows = late_a.shape[0]
    for index, (keep, got, late) in enumerate(((keep_a, got_a, late_a), (keep_b, got_b, late_b))):
        total = keep[0:rows, :].astype(F32) + got[0:rows, :].astype(F32) + late[...].astype(F32)
        out_ref[index * rows : (index + 1) * rows, :] = total.astype(BF16)


def struct(shape, dtype):
    return jax.ShapeDtypeStruct(shape, dtype)


def after(value, other):
    return value if other is None else lax.optimization_barrier((value, other))[0]


class Sequence:
    def __init__(self):
        self.latest = None

    def hold(self, value):
        return after(value, self.latest)

    def call(self, kernel, name, ins, outs, scratch, flops, *args):
        single = not isinstance(outs, list)
        size = sum(a.size * a.dtype.itemsize for a in args if a.size < 2000000)
        size += sum(math.prod(o.shape) * o.dtype.itemsize for o in ([outs] if single else outs))
        args = [pltpu.with_memory_space_constraint(a, pltpu.HBM) if i else a for i, a in zip(ins, args)]
        if self.latest is not None:
            held = ins.index(0)
            args[held] = self.hold(args[held])
        result = pl.pallas_call(
            kernel,
            in_specs=[ANY_HBM if i else IN_VMEM for i in ins],
            out_specs=IN_VMEM if single else [IN_VMEM] * len(outs),
            out_shape=outs,
            scratch_shapes=scratch,
            compiler_params=pltpu.CompilerParams(vmem_limit_bytes=24 * 1024 * 1024),
            cost_estimate=pl.CostEstimate(flops=int(flops) * 10, bytes_accessed=int(size) * 10, transcendentals=0),
            name=name,
        )(*args)
        self.latest = result if single else result[0]
        return result


def swap(x, axis, other):
    return lax.ppermute(x, axis, [(i, other(i)) for i in range(lax.axis_size(axis))])


def across_chan(x):
    return swap(x, "chan", lambda i: i ^ 1)


def across_replica(x):
    return swap(x, "replica", lambda i: i ^ 1)


def sum_rounds(values, axis, sequence):
    size = lax.axis_size(axis)
    if size & (size - 1):
        return lax.psum(values, axis)
    apart = 1
    while apart < size:
        values = values + swap(sequence.hold(values), axis, lambda i, apart=apart: i ^ apart)
        apart *= 2
    return values


def on_device(activations, cotangent, conv_weights, snake_alpha, seg_lengths, seg_owner, seg_start):
    rows, half = activations.shape
    layers, taps, channels, _ = conv_weights.shape
    top = layers - 1
    fast = lax.axis_size("dp") == 4 and lax.axis_size("replica") == 2
    paired = [fast and layer < top for layer in range(layers)]
    sources = [layer for layer in range(layers) if paired[layer]]
    tile, triple = (rows, half), (rows, taps * half)
    flops = 2 * rows * half * half * taps
    by_rows = [pltpu.VMEM((taps * half, half), BF16), DMA((3,))]
    by_columns = [pltpu.VMEM((half, taps * half), BF16), DMA((3,))]
    sequence = Sequence()
    streams, mine, partners, owns = [], [], {}, {}
    rounded, shifted, arrived, back_owns, far = {}, {}, {}, {}, {}
    alpha_parts = [None] * layers
    parts, got, late, summed, crossed = {}, {}, {}, {}, {}

    def forward_own(layer):
        owns[layer] = sequence.call(
            functools.partial(forward_own_kernel, layer), "forward_own", [0, 1], struct(tile, F32),
            [pltpu.VMEM(triple, BF16)] + by_rows, flops, mine[layer], conv_weights,
        )

    def forward_partner(layer):
        last = layer == top
        result = sequence.call(
            functools.partial(forward_partner_kernel, layer, last), "forward_partner",
            [0, 1, 0, 0, 0] + ([] if last else [0]),
            struct(tile, BF16) if last else [struct(tile, F32), struct(tile, BF16)],
            [pltpu.VMEM(triple, BF16)] + by_rows, flops,
            partners[layer], conv_weights, owns[layer], streams[layer], live, *([] if last else [alphas]),
        )
        if last:
            return result
        streams.append(result[0])
        mine.append(result[1])
        partners[layer + 1] = across_chan(result[1])

    def back_partner(layer):
        shifted[layer], part = sequence.call(
            functools.partial(back_partner_kernel, layer), "back_partner", [0, 1],
            [struct(triple, BF16), struct(tile, BF16)], by_columns, flops, rounded[layer + 1], conv_weights,
        )
        arrived[layer] = across_chan(part)

    def back_own(layer):
        back_owns[layer] = sequence.call(
            functools.partial(back_own_kernel, layer), "back_own", [0, 1], struct(tile, F32),
            by_columns, flops, shifted[layer], conv_weights,
        )

    def combine(layer, grad):
        args = [back_owns[layer], arrived[layer], streams[layer], alphas]
        outs = [struct((1, half), F32)]
        if layer > 0:
            args += [grad, live]
            outs += [struct(tile, F32)] * (layer > 1) + [struct(tile, BF16)]
        result = sequence.call(
            functools.partial(combine_kernel, layer), "combine", [0] * len(args), outs, [], 60 * rows * half, *args
        )
        alpha_parts[layer] = result[0]
        if layer > 0:
            rounded[layer] = result[-1]
            if paired[layer - 1]:
                far[layer - 1] = across_replica(result[-1])
            return result[1]

    def weights(layer):
        pieces = 4 if fast else 1
        if paired[layer]:
            piece = struct((channels // 2 // pieces, taps * half), BF16)
            out = sequence.call(
                functools.partial(paired_weight_kernel, layer, sources.index(layer)), "paired_weight", [0] * 6,
                [piece] * pieces,
                [pltpu.VMEM((half, 2 * rows), BF16), pltpu.VMEM((half, rows), BF16), pltpu.VMEM(triple, BF16)],
                2 * flops, mine[layer], partners[layer], shifted[layer], across, across_other, far[layer],
            )
        else:
            piece = struct((channels // pieces, taps * half), BF16)
            out = sequence.call(
                functools.partial(weight_kernel, fast), "weight", [0] * 3, [piece] * pieces,
                [pltpu.VMEM((channels, rows), BF16)], 2 * flops, mine[layer], partners[layer], shifted[layer],
            )
        if not fast:
            part = lax.psum_scatter(out[0], "dp", scatter_dimension=0, tiled=True)
            summed[layer] = lax.psum(part, "replica")
            crossed[layer] = jnp.zeros_like(part)
            return
        send_a, send_b, keep_a, keep_b = out
        parts[layer] = (keep_a, keep_b)
        got[layer] = (swap(send_a, "dp", lambda i: i ^ 1), swap(send_b, "dp", lambda i: i ^ 3))

    def fold(layer):
        if not fast:
            return
        (keep_a, keep_b), (got_a, got_b) = parts[layer], got[layer]
        piece = struct((keep_a.shape[0] // 2, keep_a.shape[1]), BF16)
        send_a, send_b = sequence.call(
            fold_kernel, "fold", [0] * 4, [piece, piece], [], keep_a.size, keep_a, got_a, keep_b, got_b
        )
        late[layer] = (swap(send_a, "dp", lambda i: i ^ 3), swap(send_b, "dp", lambda i: i ^ 1))

    def total(layer):
        if not fast:
            return
        (keep_a, keep_b), (got_a, got_b), (late_a, late_b) = parts[layer], got[layer], late[layer]
        summed[layer] = sequence.call(
            total_kernel, "total", [0] * 6, struct(keep_a.shape, BF16), [], keep_a.size,
            keep_a, got_a, late_a, keep_b, got_b, late_b,
        )
        crossed[layer] = across_replica(summed[layer])

    stream, snaked, grad, live, alphas = sequence.call(
        prep_kernel, "prep", [1] * 6,
        [struct(tile, F32), struct(tile, BF16), struct(tile, BF16), struct((rows, 128), F32), struct(snake_alpha.shape, F32)],
        [pltpu.SMEM(seg_lengths.shape, jnp.int32)] * 3 + [pltpu.VMEM(tile, BF16)] * 2 + [DMA((6,))],
        40 * rows * half,
        seg_lengths, seg_owner, seg_start, activations, cotangent, snake_alpha,
    )
    streams.append(stream)
    mine.append(snaked)
    partners[0] = across_chan(snaked)
    rounded[layers] = grad
    back_partner(2)
    forward_own(0)
    forward_partner(0)
    if sources:
        turned = sequence.call(
            turn_kernel, "turn", [0] * len(sources), struct((len(sources) * half // 2, rows), BF16),
            [pltpu.VMEM((half, rows), BF16)], 10 * rows * half, *[mine[layer] for layer in sources],
        )
        across = across_replica(turned)
    back_own(2)
    forward_own(1)
    forward_partner(1)
    grad = combine(2, grad)
    back_partner(1)
    weights(2)
    back_own(1)
    combine(1, grad)
    back_partner(0)
    forward_own(2)
    if sources:
        across_other = across_chan(sequence.hold(across))
    back_own(0)
    combine(0, None)
    alpha_grads = sum_rounds(jnp.concatenate(alpha_parts), "replica", sequence)
    residual_out = forward_partner(2)
    weights(1)
    fold(2)
    weights(0)
    total(2)
    alpha_grads = sum_rounds(alpha_grads, "dp", sequence)
    fold(1)
    fold(0)
    total(1)
    total(0)
    pairs = []
    for layer in range(layers):
        pairs += [summed[layer], crossed[layer]]
    depth = channels // lax.axis_size("dp")
    weight_grads = sequence.call(
        functools.partial(finish_kernel, tuple(paired)), "finish", [0] * len(pairs),
        struct((layers, taps, depth, half), F32), [], layers * taps * depth * half, *pairs,
    )
    return (residual_out, weight_grads, alpha_grads)


def solution(mesh):
    return jax.shard_map(
        on_device,
        mesh=mesh,
        in_specs=(
            P(("groups", "dp", "replica"), "chan"),
            P(("groups", "dp", "replica"), "chan"),
            P(None, None, None, "chan"),
            P(None, "chan"),
            P("groups"),
            P("groups"),
            P("groups"),
        ),
        out_specs=(
            P(("groups", "dp", "replica"), "chan"),
            P("groups", None, "dp", "chan"),
            P("groups", "chan"),
        ),
        check_vma=False,
    )
```

```python
import functools
import math

import jax
import jax.numpy as jnp
from jax import lax
from jax.experimental import pallas as pl
from jax.experimental.pallas import tpu as pltpu
from jax.sharding import PartitionSpec as P

dilations = (1, 3, 5)
F32, BF16 = jnp.float32, jnp.bfloat16
ANY_HBM = pl.BlockSpec(memory_space=pltpu.HBM)
IN_VMEM = pl.BlockSpec(memory_space=pltpu.VMEM)
DMA = pltpu.SemaphoreType.DMA
PI_PARTS = (3.140625, 9.67502593994140625e-4, 1.509957990978376432e-7)
SIN_TERMS = (-1.0 / 39916800, 1.0 / 362880, -1.0 / 5040, 1.0 / 120, -1.0 / 6)
COS_TERMS = (1.0 / 479001600, -1.0 / 3628800, 1.0 / 40320, -1.0 / 720, 1.0 / 24, -0.5)
RANGE = 8192.0
CHUNK = 64


def horner(terms, x):
    total = jnp.full_like(x, terms[0])
    for term in terms[1:]:
        total = total * x + term
    return total


def reduced(angle):
    turns = jnp.round(angle * (1.0 / 3.14159265358979))
    for part in PI_PARTS:
        angle = angle - turns * part
    return angle


def sine(angle, exact_range):
    if not exact_range:
        return jnp.sin(angle)
    rest = reduced(angle)
    square = rest * rest
    return rest + rest * (square * horner(SIN_TERMS, square))


def sine_cosine(angle, exact_range):
    if not exact_range:
        return jnp.sin(angle), jnp.cos(angle)
    rest = reduced(angle)
    square = rest * rest
    return (
        rest + rest * (square * horner(SIN_TERMS, square)),
        1.0 + square * horner(COS_TERMS, square),
    )


def by_range(bound, body):
    @pl.when(bound < RANGE)
    def _():
        body(True)

    @pl.when(bound >= RANGE)
    def _():
        body(False)


def write_snake(stream_ref, alpha, out_ref):
    inverse = 1.0 / alpha
    bound = jnp.max(jnp.abs(stream_ref[...])) * jnp.max(alpha)

    def body(exact_range):
        @pl.loop(0, stream_ref.shape[0] // CHUNK)
        def _(step):
            rows = pl.ds(pl.multiple_of(step * CHUNK, CHUNK), CHUNK)
            stream = stream_ref[rows, :]
            wave = sine(alpha * stream, exact_range)
            out_ref[rows, :] = (stream + wave * wave * inverse).astype(BF16)

    by_range(bound, body)


def moved(values, offset):
    if offset == 0:
        return values
    rows = values.shape[0]
    place = lax.broadcasted_iota(jnp.int32, values.shape, 0)
    turned = pltpu.roll(values, (-offset) % rows, 0)
    inside = place < rows - offset if offset > 0 else place >= -offset
    return jnp.where(inside, turned, 0.0)


def write_shifts(values_ref, out_ref, dilation):
    width = values_ref.shape[1]
    values = values_ref[...].astype(F32)
    for tap in range(3):
        out_ref[:, tap * width : (tap + 1) * width] = moved(values, (tap - 1) * dilation).astype(BF16)


def chan_begin(side, half):
    chan = lax.axis_index("chan")
    return pl.multiple_of((chan if side == 0 else 1 - chan) * half, half)


def prep_kernel(
    len_hbm, own_hbm, start_hbm, act_hbm, cot_hbm, alpha_hbm, weight_hbm,
    stream_ref, snake_ref, grad_ref, live_ref, alpha_ref, weight_ref,
    len_ref, own_ref, start_ref, act_ref, cot_ref, sems, weight_sems,
):
    pairs = (
        (len_hbm, len_ref), (own_hbm, own_ref), (start_hbm, start_ref),
        (alpha_hbm, alpha_ref), (act_hbm, act_ref), (cot_hbm, cot_ref),
    )
    copies = [pltpu.make_async_copy(a, b, sems.at[i]) for i, (a, b) in enumerate(pairs)]
    layers, taps, _, half = weight_hbm.shape
    loads = []
    for layer in range(layers):
        for side in range(2):
            for tap in range(taps):
                source = weight_hbm.at[layer, tap, pl.ds(chan_begin(side, half), half), :]
                target = weight_ref.at[layer, side, pl.ds(tap * half, half), :]
                loads.append(pltpu.make_async_copy(source, target, weight_sems.at[len(loads)]))
    for copy in copies + loads:
        copy.start()
    replicas = lax.axis_size("replica")
    device = lax.axis_index("dp") * replicas + lax.axis_index("replica")
    rows, width = act_ref.shape
    place = lax.broadcasted_iota(jnp.int32, (rows, 128), 0)
    live_ref[...] = jnp.zeros((rows, 128), F32)
    for copy in copies[:3]:
        copy.wait()

    @pl.loop(0, len_ref.shape[0])
    def _(clip):
        @pl.when(own_ref[clip] == device)
        def _():
            first = start_ref[clip]
            inside = (place >= first) & (place < first + len_ref[clip])
            live_ref[...] = jnp.where(inside, 1.0, live_ref[...])

    live = jnp.tile(live_ref[...], (1, width // 128))
    for copy in copies[3:5]:
        copy.wait()
    stream_ref[...] = act_ref[...].astype(F32) * live
    write_snake(stream_ref, alpha_ref[0:1, :], snake_ref)
    copies[5].wait()
    grad_ref[...] = (cot_ref[...].astype(F32) * live).astype(BF16)
    for copy in loads:
        copy.wait()


def forward_own_kernel(layer, snake_ref, weight_ref, out_ref, shifts_ref):
    write_shifts(snake_ref, shifts_ref, dilations[layer])
    out_ref[...] = jnp.dot(shifts_ref[...], weight_ref[layer, 0], preferred_element_type=F32)


def forward_partner_kernel(layer, last, snake_ref, weight_ref, own_ref, old_ref, live_ref, *rest):
    if last:
        result_ref, shifts_ref = rest
    else:
        alpha_ref, result_ref, next_ref, shifts_ref = rest
    write_shifts(snake_ref, shifts_ref, dilations[layer])
    part = jnp.dot(shifts_ref[...], weight_ref[layer, 1], preferred_element_type=F32)
    live = jnp.tile(live_ref[...], (1, old_ref.shape[1] // 128))
    new = (old_ref[...] + (own_ref[...] + part)) * live
    result_ref[...] = new.astype(result_ref.dtype)
    if not last:
        write_snake(result_ref, alpha_ref[layer + 1 : layer + 2, :], next_ref)


def back_product(shifted_ref, weight_ref, layer, side):
    half = weight_ref.shape[3]
    total = None
    for tap in range(3):
        span = slice(tap * half, (tap + 1) * half)
        part = lax.dot_general(
            shifted_ref[:, span], weight_ref[layer, side, span, :], (((1,), (1,)), ((), ())),
            preferred_element_type=F32,
        )
        total = part if total is None else total + part
    return total


def back_partner_kernel(layer, grad_ref, weight_ref, shifted_ref, out_ref):
    write_shifts(grad_ref, shifted_ref, -dilations[layer])
    out_ref[...] = back_product(shifted_ref, weight_ref, layer, 1).astype(BF16)


def back_own_kernel(layer, shifted_ref, weight_ref, out_ref):
    out_ref[...] = back_product(shifted_ref, weight_ref, layer, 0)


def combine_kernel(layer, own_ref, partner_ref, stream_ref, alphas_ref, *rest):
    if layer == 0:
        (alpha_grad_ref,) = rest
    elif len(rest) == 5:
        old_ref, live_ref, alpha_grad_ref, grad_ref, rounded_ref = rest
    else:
        old_ref, live_ref, alpha_grad_ref, rounded_ref = rest
        grad_ref = None
    alpha = alphas_ref[layer : layer + 1, :]
    inverse = 1.0 / alpha
    bound = jnp.max(jnp.abs(stream_ref[...])) * jnp.max(alpha)
    width = stream_ref.shape[1]

    def body(exact_range):
        def step_body(step, total):
            rows = pl.ds(pl.multiple_of(step * CHUNK, CHUNK), CHUNK)
            stream = stream_ref[rows, :]
            back = own_ref[rows, :] + partner_ref[rows, :].astype(F32)
            sin, cos = sine_cosine(alpha * stream, exact_range)
            double = 2.0 * sin * cos
            ratio = sin * inverse
            term = back * (stream * double * inverse - ratio * ratio)
            if layer > 0:
                live = jnp.tile(live_ref[rows, :], (1, width // 128))
                grad = (old_ref[rows, :].astype(F32) + back * (1.0 + double)) * live
                if grad_ref is not None:
                    grad_ref[rows, :] = grad
                rounded_ref[rows, :] = grad.astype(BF16)
            return total + jnp.sum(term.reshape(CHUNK // 8, 8, width), axis=0)

        total = lax.fori_loop(0, stream_ref.shape[0] // CHUNK, step_body, jnp.zeros((8, width), F32))
        alpha_grad_ref[...] = jnp.sum(total, axis=0, keepdims=True)

    by_range(bound, body)


def block_place(pieces, slice_index, part):
    apart = jnp.bitwise_xor(slice_index, lax.axis_index("dp"))
    order = (2 * pieces, 0, 1, 2 * pieces + 1)
    return 2 * part + jnp.where(
        apart == 0, order[0], jnp.where(apart == 1, order[1], jnp.where(apart == 2, order[2], order[3]))
    )


def weight_kernel(own_ref, partner_ref, shifted_ref, out_ref, turned_ref):
    half = own_ref.shape[1]
    chan = lax.axis_index("chan")
    for ref, side in ((own_ref, chan), (partner_ref, 1 - chan)):
        turned_ref[pl.ds(pl.multiple_of(side * half, half), half), :] = ref[...].T
    for tap in range(3):
        span = slice(tap * half, (tap + 1) * half)
        out_ref[:, span] = jnp.dot(turned_ref[...], shifted_ref[:, span], preferred_element_type=F32).astype(BF16)


def place_rows(pieces, rows_of, side, target_ref, columns):
    size = rows_of.shape[0] // (2 * pieces)
    for local in range(2):
        for part in range(pieces):
            begin = pl.multiple_of(block_place(pieces, side * 2 + local, part) * size, size)
            low = (local * pieces + part) * size
            target_ref[pl.ds(begin, size), columns] = rows_of[low : low + size, :]


def pick_parts(turned_ref, part, size):
    begin = pl.multiple_of(part * size, size)
    return [turned_ref[pl.ds(local * 2 * size + begin, size), :] for local in range(2)]


def turn_kernel(snake_ref, out_ref, turned_ref):
    size = snake_ref.shape[1] // 4
    turned_ref[...] = snake_ref[...].T
    for local, piece in enumerate(pick_parts(turned_ref, 1 - lax.axis_index("replica"), size)):
        out_ref[local * size : (local + 1) * size, :] = piece


def paired_weight_kernel(
    layer, pieces, own_ref, partner_ref, shifted_ref, across_ref, across_other_ref, grad_ref, *rest
):
    outs, (turned_ref, half_ref, far_ref) = rest[:-3], rest[-3:]
    rows, half = own_ref.shape
    chan = lax.axis_index("chan")
    mine = lax.axis_index("replica")
    for ref, side in ((own_ref, chan), (partner_ref, 1 - chan)):
        half_ref[...] = ref[...].T
        both = jnp.concatenate(pick_parts(half_ref, mine, half // 4), 0)
        place_rows(pieces, both, side, turned_ref, slice(0, rows))
    for ref, side in ((across_ref, chan), (across_other_ref, 1 - chan)):
        place_rows(pieces, ref[...], side, turned_ref, slice(rows, 2 * rows))
    write_shifts(grad_ref, far_ref, -dilations[layer])
    for tap in range(3):
        span = slice(tap * half, (tap + 1) * half)
        product = jnp.dot(turned_ref[:, 0:rows], shifted_ref[:, span], preferred_element_type=F32)
        product += jnp.dot(turned_ref[:, rows:], far_ref[:, span], preferred_element_type=F32)
        product = product.astype(BF16)
        size = product.shape[0] // len(outs)
        for place, ref in enumerate(outs):
            ref[:, span] = product[place * size : (place + 1) * size, :]


def finish_kernel(paired, counts, *refs):
    out_ref, refs = refs[-1], list(refs[:-1])
    half = out_ref.shape[3]
    for layer, pieces in enumerate(counts):
        for part in range(pieces):
            mine_ref, other_ref = refs.pop(0), refs.pop(0)
            size = mine_ref.shape[0]
            for tap in range(3):
                span = slice(tap * half, (tap + 1) * half)
                mine, other = mine_ref[:, span].astype(F32), other_ref[:, span].astype(F32)
                if paired:
                    begin = lax.axis_index("replica") * (size * pieces)
                    for values, start in ((mine, begin), (other, size * pieces - begin)):
                        place = pl.multiple_of(start + part * size, size)
                        out_ref[layer, tap, pl.ds(place, size), :] = values
                else:
                    out_ref[layer, tap] = mine + other


def fold_kernel(keep, got, send):
    rows = send.shape[0]
    send[...] = (keep[rows:, :].astype(F32) + got[rows:, :].astype(F32)).astype(BF16)


def total_kernel(keep, got, late, out_ref):
    rows = late.shape[0]
    total = keep[0:rows, :].astype(F32) + got[0:rows, :].astype(F32) + late[...].astype(F32)
    out_ref[...] = total.astype(BF16)


def struct(shape, dtype):
    return jax.ShapeDtypeStruct(shape, dtype)


def after(value, other):
    return value if other is None else lax.optimization_barrier((value, other))[0]


class Sequence:
    def __init__(self):
        self.latest = None

    def hold(self, value):
        return after(value, self.latest)

    def call(self, kernel, name, ins, outs, scratch, flops, *args):
        single = not isinstance(outs, list)
        size = sum(a.size * a.dtype.itemsize for a in args if a.size < 2000000)
        size += sum(math.prod(o.shape) * o.dtype.itemsize for o in ([outs] if single else outs))
        args = [pltpu.with_memory_space_constraint(a, pltpu.HBM) if i else a for i, a in zip(ins, args)]
        if self.latest is not None:
            args[0] = self.hold(args[0])
        result = pl.pallas_call(
            kernel,
            in_specs=[ANY_HBM if i else IN_VMEM for i in ins],
            out_specs=IN_VMEM if single else [IN_VMEM] * len(outs),
            out_shape=outs,
            scratch_shapes=scratch,
            compiler_params=pltpu.CompilerParams(vmem_limit_bytes=24 * 1024 * 1024),
            cost_estimate=pl.CostEstimate(flops=int(flops) * 10, bytes_accessed=int(size) * 10, transcendentals=0),
            name=name,
        )(*args)
        self.latest = result if single else result[0]
        return result


def swap(x, axis, other):
    return lax.ppermute(x, axis, [(i, other(i)) for i in range(lax.axis_size(axis))])


def across_chan(x):
    return swap(x, "chan", lambda i: i ^ 1)


def across_replica(x):
    return swap(x, "replica", lambda i: i ^ 1)


def sum_rounds(values, axis, sequence):
    size = lax.axis_size(axis)
    if size & (size - 1):
        return lax.psum(values, axis)
    apart = 1
    while apart < size:
        values = values + swap(sequence.hold(values), axis, lambda i, apart=apart: i ^ apart)
        apart *= 2
    return values


def on_device(activations, cotangent, conv_weights, snake_alpha, seg_lengths, seg_owner, seg_start):
    rows, half = activations.shape
    layers, taps, channels, _ = conv_weights.shape
    top = layers - 1
    fast = lax.axis_size("dp") == 4 and lax.axis_size("replica") == 2
    counts = [2, 1, 1] if fast else [1, 1, 1]
    tile, triple = (rows, half), (rows, taps * half)
    flops = 2 * rows * half * half * taps
    sequence = Sequence()
    streams, mine, partners, owns = [], [], {}, {}
    rounded, shifted, arrived, back_owns, far = {}, {}, {}, {}, {}
    across, across_other = {}, {}
    alpha_parts = [None] * layers
    kept, got, late, summed, crossed = {}, {}, {}, {}, {}

    def forward_own(layer):
        owns[layer] = sequence.call(
            functools.partial(forward_own_kernel, layer), "forward_own", [0, 0], struct(tile, F32),
            [pltpu.VMEM(triple, BF16)], flops, mine[layer], weight,
        )

    def forward_partner(layer):
        last = layer == top
        result = sequence.call(
            functools.partial(forward_partner_kernel, layer, last), "forward_partner",
            [0, 0, 0, 0, 0] + ([] if last else [0]),
            struct(tile, BF16) if last else [struct(tile, F32), struct(tile, BF16)],
            [pltpu.VMEM(triple, BF16)], flops,
            partners[layer], weight, owns[layer], streams[layer], live, *([] if last else [alphas]),
        )
        if last:
            return result
        streams.append(result[0])
        mine.append(result[1])
        partners[layer + 1] = across_chan(result[1])

    def back_partner(layer):
        shifted[layer], part = sequence.call(
            functools.partial(back_partner_kernel, layer), "back_partner", [0, 0],
            [struct(triple, BF16), struct(tile, BF16)], [], flops, rounded[layer + 1], weight,
        )
        arrived[layer] = across_chan(part)

    def back_own(layer):
        back_owns[layer] = sequence.call(
            functools.partial(back_own_kernel, layer), "back_own", [0, 0], struct(tile, F32),
            [], flops, shifted[layer], weight,
        )

    def send_gradient(layer):
        if fast:
            far[layer] = across_replica(sequence.hold(rounded[layer + 1]))

    def combine(layer, grad):
        args = [back_owns[layer], arrived[layer], streams[layer], alphas]
        outs = [struct((1, half), F32)]
        if layer > 0:
            args += [grad, live]
            outs += [struct(tile, F32)] * (layer > 1) + [struct(tile, BF16)]
        result = sequence.call(
            functools.partial(combine_kernel, layer), "combine", [0] * len(args), outs, [], 60 * rows * half, *args
        )
        alpha_parts[layer] = result[0]
        if layer > 0:
            rounded[layer] = result[-1]
            return result[1]

    def turn(layer):
        if fast:
            across[layer] = across_replica(sequence.call(
                turn_kernel, "turn", [0], struct((half // 2, rows), BF16),
                [pltpu.VMEM((half, rows), BF16)], 10 * rows * half, mine[layer],
            ))

    def share(layer):
        if fast:
            across_other[layer] = across_chan(sequence.hold(across[layer]))

    def weights(layer):
        if not fast:
            out = sequence.call(
                weight_kernel, "weight", [0] * 3, struct((channels, taps * half), BF16),
                [pltpu.VMEM((channels, rows), BF16)], 2 * flops, mine[layer], partners[layer], shifted[layer],
            )
            part = lax.psum_scatter(out, "dp", scatter_dimension=0, tiled=True)
            summed[layer, 0] = lax.psum(part, "replica")
            crossed[layer, 0] = jnp.zeros_like(part)
            return
        pieces = counts[layer]
        piece = struct((channels // 4 // pieces, taps * half), BF16)
        out = sequence.call(
            functools.partial(paired_weight_kernel, layer, pieces), "paired_weight", [0] * 6,
            [piece] * (2 * pieces),
            [pltpu.VMEM((half, 2 * rows), BF16), pltpu.VMEM((half, rows), BF16), pltpu.VMEM(triple, BF16)],
            2 * flops, mine[layer], partners[layer], shifted[layer], across[layer], across_other[layer], far[layer],
        )
        for part in range(pieces):
            got[layer, part] = swap(out[part], "dp", lambda i: i ^ 1)
            kept[layer, part] = out[pieces + part]

    def fold(layer, part=0):
        if not fast:
            return
        keep, came = kept[layer, part], got[layer, part]
        send = sequence.call(
            fold_kernel, "fold", [0] * 2, struct((keep.shape[0] // 2, keep.shape[1]), BF16), [], keep.size, keep, came
        )
        late[layer, part] = swap(send, "dp", lambda i: i ^ 3)

    def total(layer, part=0):
        if not fast:
            return
        keep, came, last = kept[layer, part], got[layer, part], late[layer, part]
        summed[layer, part] = sequence.call(
            total_kernel, "total", [0] * 3, struct(last.shape, BF16), [], keep.size, keep, came, last
        )
        crossed[layer, part] = across_replica(summed[layer, part])

    stream, snaked, grad, live, alphas, weight = sequence.call(
        prep_kernel, "prep", [1] * 7,
        [struct(tile, F32), struct(tile, BF16), struct(tile, BF16), struct((rows, 128), F32),
         struct(snake_alpha.shape, F32), struct((layers, 2, taps * half, half), BF16)],
        [pltpu.SMEM(seg_lengths.shape, jnp.int32)] * 3 + [pltpu.VMEM(tile, BF16)] * 2 + [DMA((6,)), DMA((2 * layers * taps,))],
        40 * rows * half,
        seg_lengths, seg_owner, seg_start, activations, cotangent, snake_alpha, conv_weights,
    )
    streams.append(stream)
    mine.append(snaked)
    partners[0] = across_chan(snaked)
    rounded[layers] = grad
    send_gradient(2)
    back_partner(2)
    forward_own(0)
    forward_partner(0)
    back_own(2)
    forward_own(1)
    forward_partner(1)
    turn(2)
    grad = combine(2, grad)
    send_gradient(1)
    turn(1)
    back_partner(1)
    back_own(1)
    share(2)
    combine(1, grad)
    weights(2)
    back_partner(0)
    forward_own(2)
    back_own(0)
    share(1)
    combine(0, None)
    alpha_grads = sum_rounds(jnp.concatenate(alpha_parts), "replica", sequence)
    residual_out = forward_partner(2)
    weights(1)
    send_gradient(0)
    turn(0)
    fold(2)
    share(0)
    weights(0)
    total(2)
    alpha_grads = sum_rounds(alpha_grads, "dp", sequence)
    fold(1)
    for part in range(counts[0]):
        fold(0, part)
    total(1)
    for part in range(counts[0]):
        total(0, part)
    pairs = []
    for layer in range(layers):
        for part in range(counts[layer]):
            pairs += [summed[layer, part], crossed[layer, part]]
    depth = channels // lax.axis_size("dp")
    weight_grads = sequence.call(
        functools.partial(finish_kernel, fast, tuple(counts)), "finish", [0] * len(pairs),
        struct((layers, taps, depth, half), F32), [], layers * taps * depth * half, *pairs,
    )
    return (residual_out, weight_grads, alpha_grads)


def solution(mesh):
    return jax.shard_map(
        on_device,
        mesh=mesh,
        in_specs=(
            P(("groups", "dp", "replica"), "chan"),
            P(("groups", "dp", "replica"), "chan"),
            P(None, None, None, "chan"),
            P(None, "chan"),
            P("groups"),
            P("groups"),
            P("groups"),
        ),
        out_specs=(
            P(("groups", "dp", "replica"), "chan"),
            P("groups", None, "dp", "chan"),
            P("groups", "chan"),
        ),
        check_vma=False,
    )
```

```python
import functools
import math

import jax
import jax.numpy as jnp
from jax import lax
from jax.experimental import pallas as pl
from jax.experimental.pallas import tpu as pltpu
from jax.sharding import PartitionSpec as P

dilations = (1, 3, 5)
F32, BF16 = jnp.float32, jnp.bfloat16
ANY_HBM = pl.BlockSpec(memory_space=pltpu.HBM)
IN_VMEM = pl.BlockSpec(memory_space=pltpu.VMEM)
DMA = pltpu.SemaphoreType.DMA
PI_PARTS = (3.140625, 9.67502593994140625e-4, 1.509957990978376432e-7)
SIN_TERMS = (-1.0 / 39916800, 1.0 / 362880, -1.0 / 5040, 1.0 / 120, -1.0 / 6)
COS_TERMS = (1.0 / 479001600, -1.0 / 3628800, 1.0 / 40320, -1.0 / 720, 1.0 / 24, -0.5)
RANGE = 8192.0
CHUNK = 64


def horner(terms, x):
    total = jnp.full_like(x, terms[0])
    for term in terms[1:]:
        total = total * x + term
    return total


def reduced(angle):
    turns = jnp.round(angle * (1.0 / 3.14159265358979))
    for part in PI_PARTS:
        angle = angle - turns * part
    return angle


def sine(angle, exact_range):
    if not exact_range:
        return jnp.sin(angle)
    rest = reduced(angle)
    square = rest * rest
    return rest + rest * (square * horner(SIN_TERMS, square))


def sine_cosine(angle, exact_range):
    if not exact_range:
        return jnp.sin(angle), jnp.cos(angle)
    rest = reduced(angle)
    square = rest * rest
    return (
        rest + rest * (square * horner(SIN_TERMS, square)),
        1.0 + square * horner(COS_TERMS, square),
    )


def by_range(bound, body):
    @pl.when(bound < RANGE)
    def _():
        body(True)

    @pl.when(bound >= RANGE)
    def _():
        body(False)


def write_snake(stream_ref, alpha, out_ref):
    inverse = 1.0 / alpha
    bound = jnp.max(jnp.abs(stream_ref[...])) * jnp.max(alpha)

    def body(exact_range):
        @pl.loop(0, stream_ref.shape[0] // CHUNK)
        def _(step):
            rows = pl.ds(pl.multiple_of(step * CHUNK, CHUNK), CHUNK)
            stream = stream_ref[rows, :]
            wave = sine(alpha * stream, exact_range)
            out_ref[rows, :] = (stream + wave * wave * inverse).astype(BF16)

    by_range(bound, body)


def moved(values, offset):
    if offset == 0:
        return values
    rows = values.shape[0]
    place = lax.broadcasted_iota(jnp.int32, values.shape, 0)
    turned = pltpu.roll(values, (-offset) % rows, 0)
    inside = place < rows - offset if offset > 0 else place >= -offset
    return jnp.where(inside, turned, 0.0)


def write_shifts(values_ref, out_ref, dilation):
    width = values_ref.shape[1]
    values = values_ref[...].astype(F32)
    for tap in range(3):
        out_ref[:, tap * width : (tap + 1) * width] = moved(values, (tap - 1) * dilation).astype(BF16)


def chan_begin(side, half):
    chan = lax.axis_index("chan")
    return pl.multiple_of((chan if side == 0 else 1 - chan) * half, half)


def prep_kernel(
    len_hbm, own_hbm, start_hbm, act_hbm, cot_hbm, alpha_hbm, weight_hbm,
    stream_ref, snake_ref, grad_ref, live_ref, alpha_ref, weight_ref,
    len_ref, own_ref, start_ref, act_ref, cot_ref, sems, weight_sems,
):
    pairs = (
        (len_hbm, len_ref), (own_hbm, own_ref), (start_hbm, start_ref),
        (alpha_hbm, alpha_ref), (act_hbm, act_ref), (cot_hbm, cot_ref),
    )
    copies = [pltpu.make_async_copy(a, b, sems.at[i]) for i, (a, b) in enumerate(pairs)]
    layers, taps, _, half = weight_hbm.shape
    loads = []
    for layer in range(layers):
        for side in range(2):
            for tap in range(taps):
                source = weight_hbm.at[layer, tap, pl.ds(chan_begin(side, half), half), :]
                target = weight_ref.at[layer, side, pl.ds(tap * half, half), :]
                loads.append(pltpu.make_async_copy(source, target, weight_sems.at[len(loads)]))
    for copy in copies + loads:
        copy.start()
    replicas = lax.axis_size("replica")
    device = lax.axis_index("dp") * replicas + lax.axis_index("replica")
    rows, width = act_ref.shape
    place = lax.broadcasted_iota(jnp.int32, (rows, 128), 0)
    live_ref[...] = jnp.zeros((rows, 128), F32)
    for copy in copies[:3]:
        copy.wait()

    @pl.loop(0, len_ref.shape[0])
    def _(clip):
        @pl.when(own_ref[clip] == device)
        def _():
            first = start_ref[clip]
            inside = (place >= first) & (place < first + len_ref[clip])
            live_ref[...] = jnp.where(inside, 1.0, live_ref[...])

    live = jnp.tile(live_ref[...], (1, width // 128))
    for copy in copies[3:5]:
        copy.wait()
    stream_ref[...] = act_ref[...].astype(F32) * live
    write_snake(stream_ref, alpha_ref[0:1, :], snake_ref)
    copies[5].wait()
    grad_ref[...] = (cot_ref[...].astype(F32) * live).astype(BF16)
    for copy in loads:
        copy.wait()


def forward_own_kernel(layer, snake_ref, weight_ref, out_ref, shifts_ref):
    write_shifts(snake_ref, shifts_ref, dilations[layer])
    out_ref[...] = jnp.dot(shifts_ref[...], weight_ref[layer, 0], preferred_element_type=F32)


def forward_partner_kernel(layer, last, snake_ref, weight_ref, own_ref, old_ref, live_ref, *rest):
    if last:
        result_ref, shifts_ref = rest
    else:
        alpha_ref, result_ref, next_ref, shifts_ref = rest
    write_shifts(snake_ref, shifts_ref, dilations[layer])
    part = jnp.dot(shifts_ref[...], weight_ref[layer, 1], preferred_element_type=F32)
    live = jnp.tile(live_ref[...], (1, old_ref.shape[1] // 128))
    new = (old_ref[...] + (own_ref[...] + part)) * live
    result_ref[...] = new.astype(result_ref.dtype)
    if not last:
        write_snake(result_ref, alpha_ref[layer + 1 : layer + 2, :], next_ref)


def back_product(shifted_ref, weight_ref, layer, side):
    half = weight_ref.shape[3]
    total = None
    for tap in range(3):
        span = slice(tap * half, (tap + 1) * half)
        part = lax.dot_general(
            shifted_ref[:, span], weight_ref[layer, side, span, :], (((1,), (1,)), ((), ())),
            preferred_element_type=F32,
        )
        total = part if total is None else total + part
    return total


def back_partner_kernel(layer, grad_ref, weight_ref, shifted_ref, out_ref):
    write_shifts(grad_ref, shifted_ref, -dilations[layer])
    out_ref[...] = back_product(shifted_ref, weight_ref, layer, 1).astype(BF16)


def back_own_kernel(layer, shifted_ref, weight_ref, out_ref):
    out_ref[...] = back_product(shifted_ref, weight_ref, layer, 0)


def combine_kernel(layer, own_ref, partner_ref, stream_ref, alphas_ref, *rest):
    if layer == 0:
        (alpha_grad_ref,) = rest
    elif len(rest) == 5:
        old_ref, live_ref, alpha_grad_ref, grad_ref, rounded_ref = rest
    else:
        old_ref, live_ref, alpha_grad_ref, rounded_ref = rest
        grad_ref = None
    alpha = alphas_ref[layer : layer + 1, :]
    inverse = 1.0 / alpha
    bound = jnp.max(jnp.abs(stream_ref[...])) * jnp.max(alpha)
    width = stream_ref.shape[1]

    def body(exact_range):
        def step_body(step, total):
            rows = pl.ds(pl.multiple_of(step * CHUNK, CHUNK), CHUNK)
            stream = stream_ref[rows, :]
            back = own_ref[rows, :] + partner_ref[rows, :].astype(F32)
            sin, cos = sine_cosine(alpha * stream, exact_range)
            double = 2.0 * sin * cos
            ratio = sin * inverse
            term = back * (stream * double * inverse - ratio * ratio)
            if layer > 0:
                live = jnp.tile(live_ref[rows, :], (1, width // 128))
                grad = (old_ref[rows, :].astype(F32) + back * (1.0 + double)) * live
                if grad_ref is not None:
                    grad_ref[rows, :] = grad
                rounded_ref[rows, :] = grad.astype(BF16)
            return total + jnp.sum(term.reshape(CHUNK // 8, 8, width), axis=0)

        total = lax.fori_loop(0, stream_ref.shape[0] // CHUNK, step_body, jnp.zeros((8, width), F32))
        alpha_grad_ref[...] = jnp.sum(total, axis=0, keepdims=True)

    by_range(bound, body)


def block_place(pieces, slice_index, part):
    apart = jnp.bitwise_xor(slice_index, lax.axis_index("dp"))
    order = (2 * pieces, 0, 1, 2 * pieces + 1)
    return 2 * part + jnp.where(
        apart == 0, order[0], jnp.where(apart == 1, order[1], jnp.where(apart == 2, order[2], order[3]))
    )


def weight_kernel(own_ref, partner_ref, shifted_ref, out_ref, turned_ref):
    half = own_ref.shape[1]
    chan = lax.axis_index("chan")
    for ref, side in ((own_ref, chan), (partner_ref, 1 - chan)):
        turned_ref[pl.ds(pl.multiple_of(side * half, half), half), :] = ref[...].T
    for tap in range(3):
        span = slice(tap * half, (tap + 1) * half)
        out_ref[:, span] = jnp.dot(turned_ref[...], shifted_ref[:, span], preferred_element_type=F32).astype(BF16)


def place_rows(pieces, rows_of, side, target_ref, columns):
    size = rows_of.shape[0] // (2 * pieces)
    for local in range(2):
        for part in range(pieces):
            begin = pl.multiple_of(block_place(pieces, side * 2 + local, part) * size, size)
            low = (local * pieces + part) * size
            target_ref[pl.ds(begin, size), columns] = rows_of[low : low + size, :]


def pick_parts(turned_ref, part, size):
    begin = pl.multiple_of(part * size, size)
    return [turned_ref[pl.ds(local * 2 * size + begin, size), :] for local in range(2)]


def turn_kernel(*refs):
    snakes, out_ref, turned_ref = refs[:-2], refs[-2], refs[-1]
    size = snakes[0].shape[1] // 4
    for index, ref in enumerate(snakes):
        turned_ref[...] = ref[...].T
        for local, piece in enumerate(pick_parts(turned_ref, 1 - lax.axis_index("replica"), size)):
            low = (2 * index + local) * size
            out_ref[low : low + size, :] = piece


def own_rows_kernel(pieces, own_ref, partner_ref, out_ref, half_ref):
    chan = lax.axis_index("chan")
    mine = lax.axis_index("replica")
    for ref, side in ((own_ref, chan), (partner_ref, 1 - chan)):
        half_ref[...] = ref[...].T
        both = jnp.concatenate(pick_parts(half_ref, mine, ref.shape[1] // 4), 0)
        place_rows(pieces, both, side, out_ref, slice(None))


def far_kernel(layer, grad_ref, out_ref):
    write_shifts(grad_ref, out_ref, -dilations[layer])


def paired_weight_kernel(pieces, low, own_ref, shifted_ref, across_ref, across_other_ref, far_ref, *rest):
    outs, turned_ref = rest[:-1], rest[-1]
    half = own_ref.shape[0]
    chan = lax.axis_index("chan")
    for ref, side in ((across_ref, chan), (across_other_ref, 1 - chan)):
        place_rows(pieces, ref[low : low + half // 2, :], side, turned_ref, slice(None))
    for tap in range(3):
        span = slice(tap * half, (tap + 1) * half)
        product = jnp.dot(own_ref[...], shifted_ref[:, span], preferred_element_type=F32)
        product += jnp.dot(turned_ref[...], far_ref[:, span], preferred_element_type=F32)
        product = product.astype(BF16)
        size = product.shape[0] // len(outs)
        for place, ref in enumerate(outs):
            ref[:, span] = product[place * size : (place + 1) * size, :]


def finish_kernel(paired, held, counts, *refs):
    out_ref, total_ref, sems = refs[-3:]
    refs = list(refs[1:-3] if held else refs[:-3])
    half = total_ref.shape[3]
    copies = []
    for index, (layer, pieces) in enumerate(counts):
        for part in range(pieces):
            mine_ref, other_ref = refs.pop(0), refs.pop(0)
            size = mine_ref.shape[0]
            for tap in range(3):
                span = slice(tap * half, (tap + 1) * half)
                mine, other = mine_ref[:, span].astype(F32), other_ref[:, span].astype(F32)
                if paired:
                    begin = lax.axis_index("replica") * (size * pieces)
                    for values, start in ((mine, begin), (other, size * pieces - begin)):
                        place = pl.multiple_of(start + part * size, size)
                        total_ref[index, tap, pl.ds(place, size), :] = values
                else:
                    total_ref[index, tap] = mine + other
        copies.append(pltpu.make_async_copy(total_ref.at[index], out_ref.at[layer], sems.at[index]))
        copies[-1].start()
    for copy in copies:
        copy.wait()


def fold_kernel(keep, got, send):
    rows = send.shape[0]
    send[...] = (keep[rows:, :].astype(F32) + got[rows:, :].astype(F32)).astype(BF16)


def total_kernel(keep, got, late, out_ref):
    rows = late.shape[0]
    total = keep[0:rows, :].astype(F32) + got[0:rows, :].astype(F32) + late[...].astype(F32)
    out_ref[...] = total.astype(BF16)


def stack_kernel(*refs):
    for index, ref in enumerate(refs[:-1]):
        refs[-1][index : index + 1, :] = ref[...]


def add_kernel(left, right, out_ref):
    out_ref[...] = left[...] + right[...]


def struct(shape, dtype):
    return jax.ShapeDtypeStruct(shape, dtype)


def after(value, other):
    return value if other is None else lax.optimization_barrier((value, other))[0]


class Sequence:
    def __init__(self):
        self.latest = None
        self.weight = 10

    def hold(self, value):
        return after(value, self.latest)

    def call(self, kernel, name, ins, outs, scratch, flops, *args, spec=IN_VMEM, aliases=None):
        single = not isinstance(outs, list)
        size = sum(a.size * a.dtype.itemsize for a in args if a.size < 2000000)
        size += sum(math.prod(o.shape) * o.dtype.itemsize for o in ([outs] if single else outs))
        args = [pltpu.with_memory_space_constraint(a, pltpu.HBM) if i == 1 else a for i, a in zip(ins, args)]
        if self.latest is not None:
            held = ins.index(0)
            args[held] = self.hold(args[held])
        result = pl.pallas_call(
            kernel,
            in_specs=[ANY_HBM if i else IN_VMEM for i in ins],
            out_specs=spec if single else [IN_VMEM] * len(outs),
            out_shape=outs,
            scratch_shapes=scratch,
            input_output_aliases=aliases or {},
            compiler_params=pltpu.CompilerParams(vmem_limit_bytes=24 * 1024 * 1024),
            cost_estimate=pl.CostEstimate(flops=int(flops) * self.weight, bytes_accessed=int(size) * self.weight, transcendentals=0),
            name=name,
        )(*args)
        self.latest = result if single else result[0]
        return result


def swap(x, axis, other):
    return lax.ppermute(x, axis, [(i, other(i)) for i in range(lax.axis_size(axis))])


def across_chan(x):
    return swap(x, "chan", lambda i: i ^ 1)


def across_replica(x):
    return swap(x, "replica", lambda i: i ^ 1)


def on_device(activations, cotangent, conv_weights, snake_alpha, seg_lengths, seg_owner, seg_start):
    rows, half = activations.shape
    layers, taps, channels, _ = conv_weights.shape
    top = layers - 1
    fast = lax.axis_size("dp") == 4 and lax.axis_size("replica") == 2
    counts = [1] * layers
    tile, triple = (rows, half), (rows, taps * half)
    flops = 2 * rows * half * half * taps
    sequence = Sequence()
    streams, mine, partners, owns = [], [], {}, {}
    rounded, shifted, arrived, back_owns, far = {}, {}, {}, {}, {}
    across, across_other = {}, {}
    alpha_parts = [None] * layers
    kept, got, late, summed, crossed = {}, {}, {}, {}, {}

    def forward_own(layer):
        owns[layer] = sequence.call(
            functools.partial(forward_own_kernel, layer), "forward_own", [0, 0], struct(tile, F32),
            [pltpu.VMEM(triple, BF16)], flops, mine[layer], weight,
        )

    def forward_partner(layer):
        last = layer == top
        result = sequence.call(
            functools.partial(forward_partner_kernel, layer, last), "forward_partner",
            [0, 0, 0, 0, 0] + ([] if last else [0]),
            struct(tile, BF16) if last else [struct(tile, F32), struct(tile, BF16)],
            [pltpu.VMEM(triple, BF16)], flops,
            partners[layer], weight, owns[layer], streams[layer], live, *([] if last else [alphas]),
        )
        if last:
            return result
        streams.append(result[0])
        mine.append(result[1])
        partners[layer + 1] = across_chan(result[1])

    def back_partner(layer):
        shifted[layer], part = sequence.call(
            functools.partial(back_partner_kernel, layer), "back_partner", [0, 0],
            [struct(triple, BF16), struct(tile, BF16)], [], flops, rounded[layer + 1], weight,
        )
        arrived[layer] = across_chan(part)

    def back_own(layer):
        back_owns[layer] = sequence.call(
            functools.partial(back_own_kernel, layer), "back_own", [0, 0], struct(tile, F32),
            [], flops, shifted[layer], weight,
        )

    def send_gradient(layer):
        if fast:
            far[layer] = across_replica(sequence.hold(rounded[layer + 1]))

    def combine(layer, grad):
        args = [back_owns[layer], arrived[layer], streams[layer], alphas]
        outs = [struct((1, half), F32)]
        if layer > 0:
            args += [grad, live]
            outs += [struct(tile, F32)] * (layer > 1) + [struct(tile, BF16)]
        result = sequence.call(
            functools.partial(combine_kernel, layer), "combine", [0] * len(args), outs, [], 60 * rows * half, *args
        )
        alpha_parts[layer] = result[0]
        if layer > 0:
            rounded[layer] = result[-1]
            return result[1]

    def turn(*chosen):
        if fast:
            moved_rows = across_replica(sequence.call(
                turn_kernel, "turn", [0] * len(chosen), struct((len(chosen) * half // 2, rows), BF16),
                [pltpu.VMEM((half, rows), BF16)], 10 * rows * half, *[mine[layer] for layer in chosen],
            ))
            for index, layer in enumerate(chosen):
                across[layer] = (moved_rows, index * half // 2)

    def share(*chosen):
        if fast:
            shared = across_chan(sequence.hold(across[chosen[0]][0]))
            for layer in chosen:
                across_other[layer] = shared

    own_turned, far_shifted = {}, {}

    def own_rows(layer):
        if fast:
            own_turned[layer] = sequence.call(
                functools.partial(own_rows_kernel, counts[layer]), "own_rows", [0, 0], struct((half, rows), BF16),
                [pltpu.VMEM((half, rows), BF16)], 10 * rows * half, mine[layer], partners[layer],
            )

    def far_rows(layer):
        if fast:
            far_shifted[layer] = sequence.call(
                functools.partial(far_kernel, layer), "far_rows", [0], struct(triple, BF16), [],
                10 * rows * half, far[layer],
            )

    def weights(layer):
        if not fast:
            out = sequence.call(
                weight_kernel, "weight", [0] * 3, struct((channels, taps * half), BF16),
                [pltpu.VMEM((channels, rows), BF16)], 2 * flops, mine[layer], partners[layer], shifted[layer],
            )
            part = lax.psum_scatter(out, "dp", scatter_dimension=0, tiled=True)
            summed[layer, 0] = lax.psum(part, "replica")
            crossed[layer, 0] = jnp.zeros_like(part)
            return
        pieces = counts[layer]
        piece = struct((channels // 4 // pieces, taps * half), BF16)
        out = sequence.call(
            functools.partial(paired_weight_kernel, pieces, across[layer][1]), "paired_weight", [0] * 5,
            [piece] * (2 * pieces), [pltpu.VMEM((half, rows), BF16)], 2 * flops,
            own_turned[layer], shifted[layer], across[layer][0], across_other[layer], far_shifted[layer],
        )
        for part in range(pieces):
            got[layer, part] = swap(out[part], "dp", lambda i: i ^ 1)
            kept[layer, part] = out[pieces + part]

    def fold(layer, part=0):
        if not fast:
            return
        keep, came = kept[layer, part], got[layer, part]
        send = sequence.call(
            fold_kernel, "fold", [0] * 2, struct((keep.shape[0] // 2, keep.shape[1]), BF16), [], keep.size, keep, came
        )
        late[layer, part] = swap(send, "dp", lambda i: i ^ 3)

    def total(layer, part=0):
        if not fast:
            return
        keep, came, last = kept[layer, part], got[layer, part], late[layer, part]
        summed[layer, part] = sequence.call(
            total_kernel, "total", [0] * 3, struct(last.shape, BF16), [], 2 * flops, keep, came, last
        )
        crossed[layer, part] = across_replica(summed[layer, part])

    stream, snaked, grad, live, alphas, weight = sequence.call(
        prep_kernel, "prep", [1] * 7,
        [struct(tile, F32), struct(tile, BF16), struct(tile, BF16), struct((rows, 128), F32),
         struct(snake_alpha.shape, F32), struct((layers, 2, taps * half, half), BF16)],
        [pltpu.SMEM(seg_lengths.shape, jnp.int32)] * 3 + [pltpu.VMEM(tile, BF16)] * 2 + [DMA((6,)), DMA((2 * layers * taps,))],
        40 * rows * half,
        seg_lengths, seg_owner, seg_start, activations, cotangent, snake_alpha, conv_weights,
    )
    streams.append(stream)
    mine.append(snaked)
    partners[0] = across_chan(snaked)
    rounded[layers] = grad
    depth = channels // lax.axis_size("dp")

    def finish(chosen, before=None):
        pairs = [] if before is None else [before]
        for layer in chosen:
            for part in range(counts[layer]):
                pairs += [summed[layer, part], crossed[layer, part]]
        return sequence.call(
            functools.partial(finish_kernel, fast, before is not None, tuple((layer, counts[layer]) for layer in chosen)),
            "finish", [2] * (before is not None) + [0] * (len(pairs) - (before is not None)),
            struct((layers, taps, depth, half), F32),
            [pltpu.VMEM((len(chosen), taps, depth, half), F32), DMA((len(chosen),))],
            layers * taps * depth * half, *pairs, spec=ANY_HBM, aliases={0: 0} if before is not None else None,
        )

    rounds = [("replica", 1 << bit) for bit in range(8) if lax.axis_size("replica") >> (bit + 1)]
    rounds += [("dp", 1 << bit) for bit in range(8) if lax.axis_size("dp") >> (bit + 1)]
    arrivals = []

    def alpha_round():
        if arrivals:
            value = sequence.call(
                add_kernel, "add", [0, 0], struct((layers, half), F32), [], layers * half, *arrivals.pop()
            )
        else:
            value = sequence.call(
                stack_kernel, "stack", [0] * layers, struct((layers, half), F32), [], layers * half, *alpha_parts
            )
        if not rounds:
            return value
        axis, apart = rounds.pop(0)
        arrivals.append((value, swap(value, axis, lambda place: place ^ apart)))

    send_gradient(2)
    back_partner(2)
    forward_own(0)
    forward_partner(0)
    back_own(2)
    forward_own(1)
    forward_partner(1)
    turn(2)
    grad = combine(2, grad)
    send_gradient(1)
    far_rows(2)
    own_rows(2)
    turn(1, 0)
    back_partner(1)
    share(2)
    back_own(1)
    combine(1, grad)
    back_partner(0)
    weights(2)
    own_rows(1)
    back_own(0)
    own_rows(0)
    combine(0, None)
    forward_own(2)
    residual_out = forward_partner(2)
    far_rows(1)
    share(1, 0)
    send_gradient(0)
    fold(2)
    weights(1)
    total(2)
    fold(1)
    far_rows(0)
    alpha_round()
    weights(0)
    total(1)
    alpha_round()
    fold(0)
    weight_grads = finish((2, 1))
    alpha_grads = alpha_round()
    total(0)
    while alpha_grads is None:
        alpha_grads = alpha_round()
    weight_grads = finish((0,), weight_grads)
    return (residual_out, weight_grads, alpha_grads)


def solution(mesh):
    return jax.shard_map(
        on_device,
        mesh=mesh,
        in_specs=(
            P(("groups", "dp", "replica"), "chan"),
            P(("groups", "dp", "replica"), "chan"),
            P(None, None, None, "chan"),
            P(None, "chan"),
            P("groups"),
            P("groups"),
            P("groups"),
        ),
        out_specs=(
            P(("groups", "dp", "replica"), "chan"),
            P("groups", None, "dp", "chan"),
            P("groups", "chan"),
        ),
        check_vma=False,
    )
```

```python
import functools
import math

import jax
import jax.numpy as jnp
from jax import lax
from jax.experimental import pallas as pl
from jax.experimental.pallas import tpu as pltpu
from jax.sharding import PartitionSpec as P

dilations = (1, 3, 5)
F32, BF16 = jnp.float32, jnp.bfloat16
ANY_HBM = pl.BlockSpec(memory_space=pltpu.HBM)
IN_VMEM = pl.BlockSpec(memory_space=pltpu.VMEM)
DMA = pltpu.SemaphoreType.DMA
PI_PARTS = (3.140625, 9.67502593994140625e-4, 1.509957990978376432e-7)
SIN_TERMS = (-1.0 / 39916800, 1.0 / 362880, -1.0 / 5040, 1.0 / 120, -1.0 / 6)
COS_TERMS = (1.0 / 479001600, -1.0 / 3628800, 1.0 / 40320, -1.0 / 720, 1.0 / 24, -0.5)
RANGE = 8192.0
CHUNK = 64
CARRIED = 16


def horner(terms, x):
    total = jnp.full_like(x, terms[0])
    for term in terms[1:]:
        total = total * x + term
    return total


def reduced(angle):
    turns = jnp.round(angle * (1.0 / 3.14159265358979))
    for part in PI_PARTS:
        angle = angle - turns * part
    return angle


def sine(angle, exact_range):
    if not exact_range:
        return jnp.sin(angle)
    rest = reduced(angle)
    square = rest * rest
    return rest + rest * (square * horner(SIN_TERMS, square))


def sine_cosine(angle, exact_range):
    if not exact_range:
        return jnp.sin(angle), jnp.cos(angle)
    rest = reduced(angle)
    square = rest * rest
    return (
        rest + rest * (square * horner(SIN_TERMS, square)),
        1.0 + square * horner(COS_TERMS, square),
    )


def by_range(bound, body):
    @pl.when(bound < RANGE)
    def _():
        body(True)

    @pl.when(bound >= RANGE)
    def _():
        body(False)


def write_snake(stream_ref, alpha, out_ref):
    inverse = 1.0 / alpha
    bound = jnp.max(jnp.abs(stream_ref[...])) * jnp.max(alpha)

    def body(exact_range):
        @pl.loop(0, stream_ref.shape[0] // CHUNK)
        def _(step):
            rows = pl.ds(pl.multiple_of(step * CHUNK, CHUNK), CHUNK)
            stream = stream_ref[rows, :]
            wave = sine(alpha * stream, exact_range)
            out_ref[rows, :] = (stream + wave * wave * inverse).astype(BF16)

    by_range(bound, body)


def moved(values, offset):
    if offset == 0:
        return values
    rows = values.shape[0]
    place = lax.broadcasted_iota(jnp.int32, values.shape, 0)
    turned = pltpu.roll(values, (-offset) % rows, 0)
    inside = place < rows - offset if offset > 0 else place >= -offset
    return jnp.where(inside, turned, 0.0)


def write_shifts(values_ref, out_ref, dilation):
    width = values_ref.shape[1]
    values = values_ref[...].astype(F32)
    for tap in range(3):
        out_ref[:, tap * width : (tap + 1) * width] = moved(values, (tap - 1) * dilation).astype(BF16)


def chan_begin(side, half):
    chan = lax.axis_index("chan")
    return pl.multiple_of((chan if side == 0 else 1 - chan) * half, half)


def load_weights(layer, weight_hbm, weight_ref, sems):
    half = weight_hbm.shape[3]
    loads = []
    for side in range(2):
        for tap in range(3):
            source = weight_hbm.at[layer, tap, pl.ds(chan_begin(side, half), half), :]
            target = weight_ref.at[side, pl.ds(tap * half, half), :]
            loads.append(pltpu.make_async_copy(source, target, sems.at[len(loads)]))
    for copy in loads:
        copy.start()
    return loads


def prep_kernel(
    len_hbm, own_hbm, start_hbm, act_hbm, cot_hbm, alpha_hbm, weight_hbm,
    stream_ref, snake_ref, grad_ref, live_ref, alpha_ref, weight_ref,
    len_ref, own_ref, start_ref, act_ref, cot_ref, sems, weight_sems,
):
    pairs = (
        (len_hbm, len_ref), (own_hbm, own_ref), (start_hbm, start_ref),
        (alpha_hbm, alpha_ref), (act_hbm, act_ref), (cot_hbm, cot_ref),
    )
    copies = [pltpu.make_async_copy(a, b, sems.at[i]) for i, (a, b) in enumerate(pairs)]
    for copy in copies:
        copy.start()
    loads = load_weights(0, weight_hbm, weight_ref, weight_sems)
    replicas = lax.axis_size("replica")
    device = lax.axis_index("dp") * replicas + lax.axis_index("replica")
    rows, width = act_ref.shape
    place = lax.broadcasted_iota(jnp.int32, (rows, 128), 0)
    live_ref[...] = jnp.zeros((rows, 128), F32)
    for copy in copies[:3]:
        copy.wait()

    @pl.loop(0, len_ref.shape[0])
    def _(clip):
        @pl.when(own_ref[clip] == device)
        def _():
            first = start_ref[clip]
            inside = (place >= first) & (place < first + len_ref[clip])
            live_ref[...] = jnp.where(inside, 1.0, live_ref[...])

    live = jnp.tile(live_ref[...], (1, width // 128))
    for copy in copies[3:5]:
        copy.wait()
    stream_ref[...] = act_ref[...].astype(F32) * live
    write_snake(stream_ref, alpha_ref[0:1, :], snake_ref)
    copies[5].wait()
    grad_ref[...] = (cot_ref[...].astype(F32) * live).astype(BF16)
    for copy in loads:
        copy.wait()


def forward_own_kernel(layer, load, snake_ref, weight_ref, *rest):
    if load is None:
        out_ref, shifts_ref = rest
        loads = []
    else:
        weight_hbm, out_ref, loaded_ref, shifts_ref, sems = rest
        loads = load_weights(load, weight_hbm, loaded_ref, sems)
    write_shifts(snake_ref, shifts_ref, dilations[layer])
    out_ref[...] = jnp.dot(shifts_ref[...], weight_ref[0], preferred_element_type=F32)
    for copy in loads:
        copy.wait()


def forward_partner_kernel(layer, last, load, snake_ref, weight_ref, own_ref, old_ref, live_ref, *rest):
    rest = list(rest)
    alpha_ref = None if last else rest.pop(0)
    weight_hbm = None if load is None else rest.pop(0)
    result_ref = rest.pop(0)
    next_ref = None if last else rest.pop(0)
    loads = []
    if load is not None:
        loaded_ref, shifts_ref, sems = rest
        loads = load_weights(load, weight_hbm, loaded_ref, sems)
    else:
        (shifts_ref,) = rest
    write_shifts(snake_ref, shifts_ref, dilations[layer])
    part = jnp.dot(shifts_ref[...], weight_ref[1], preferred_element_type=F32)
    live = jnp.tile(live_ref[...], (1, old_ref.shape[1] // 128))
    new = (old_ref[...] + (own_ref[...] + part)) * live
    result_ref[...] = new.astype(result_ref.dtype)
    if not last:
        write_snake(result_ref, alpha_ref[layer + 1 : layer + 2, :], next_ref)
    for copy in loads:
        copy.wait()


def back_product(shifted_ref, weight_ref, side):
    half = weight_ref.shape[2]
    total = None
    for tap in range(3):
        span = slice(tap * half, (tap + 1) * half)
        part = lax.dot_general(
            shifted_ref[:, span], weight_ref[side, span, :], (((1,), (1,)), ((), ())),
            preferred_element_type=F32,
        )
        total = part if total is None else total + part
    return total


def back_partner_kernel(layer, grad_ref, weight_ref, shifted_ref, out_ref):
    write_shifts(grad_ref, shifted_ref, -dilations[layer])
    out_ref[...] = back_product(shifted_ref, weight_ref, 1).astype(BF16)


def back_own_kernel(shifted_ref, weight_ref, out_ref):
    out_ref[...] = back_product(shifted_ref, weight_ref, 0)


def combine_kernel(layer, own_ref, partner_ref, stream_ref, alphas_ref, *rest):
    if layer == 0:
        (alpha_grad_ref,) = rest
    elif len(rest) == 5:
        old_ref, live_ref, alpha_grad_ref, grad_ref, rounded_ref = rest
    else:
        old_ref, live_ref, alpha_grad_ref, rounded_ref = rest
        grad_ref = None
    alpha = alphas_ref[layer : layer + 1, :]
    inverse = 1.0 / alpha
    bound = jnp.max(jnp.abs(stream_ref[...])) * jnp.max(alpha)
    width = stream_ref.shape[1]

    def body(exact_range):
        def step_body(step, total):
            rows = pl.ds(pl.multiple_of(step * CHUNK, CHUNK), CHUNK)
            stream = stream_ref[rows, :]
            back = own_ref[rows, :] + partner_ref[rows, :].astype(F32)
            sin, cos = sine_cosine(alpha * stream, exact_range)
            double = 2.0 * sin * cos
            ratio = sin * inverse
            term = back * (stream * double * inverse - ratio * ratio)
            if layer > 0:
                live = jnp.tile(live_ref[rows, :], (1, width // 128))
                grad = (old_ref[rows, :].astype(F32) + back * (1.0 + double)) * live
                if grad_ref is not None:
                    grad_ref[rows, :] = grad
                rounded_ref[rows, :] = grad.astype(BF16)
            return total + jnp.sum(term.reshape(CHUNK // 8, 8, width), axis=0)

        total = lax.fori_loop(0, stream_ref.shape[0] // CHUNK, step_body, jnp.zeros((8, width), F32))
        alpha_grad_ref[...] = jnp.sum(total, axis=0, keepdims=True)

    by_range(bound, body)


def block_place(pieces, slice_index, part):
    apart = jnp.bitwise_xor(slice_index, lax.axis_index("dp"))
    order = (2 * pieces, 0, 1, 2 * pieces + 1)
    return 2 * part + jnp.where(
        apart == 0, order[0], jnp.where(apart == 1, order[1], jnp.where(apart == 2, order[2], order[3]))
    )


def weight_kernel(own_ref, partner_ref, shifted_ref, out_ref, turned_ref):
    half = own_ref.shape[1]
    chan = lax.axis_index("chan")
    for ref, side in ((own_ref, chan), (partner_ref, 1 - chan)):
        turned_ref[pl.ds(pl.multiple_of(side * half, half), half), :] = ref[...].T
    for tap in range(3):
        span = slice(tap * half, (tap + 1) * half)
        out_ref[:, span] = jnp.dot(turned_ref[...], shifted_ref[:, span], preferred_element_type=F32).astype(BF16)


def place_rows(pieces, rows_of, side, target_ref, columns):
    size = rows_of.shape[0] // (2 * pieces)
    for local in range(2):
        for part in range(pieces):
            begin = pl.multiple_of(block_place(pieces, side * 2 + local, part) * size, size)
            low = (local * pieces + part) * size
            target_ref[pl.ds(begin, size), columns] = rows_of[low : low + size, :]


def pick_parts(turned_ref, part, size):
    begin = pl.multiple_of(part * size, size)
    return [turned_ref[pl.ds(local * 2 * size + begin, size), :] for local in range(2)]


def turn_kernel(*refs):
    snakes, out_ref, turned_ref = refs[:-2], refs[-2], refs[-1]
    size = snakes[0].shape[1] // 4
    for index, ref in enumerate(snakes):
        turned_ref[...] = ref[...].T
        for local, piece in enumerate(pick_parts(turned_ref, 1 - lax.axis_index("replica"), size)):
            low = (2 * index + local) * size
            out_ref[low : low + size, :] = piece


def own_rows_kernel(pieces, own_ref, partner_ref, out_ref, half_ref):
    chan = lax.axis_index("chan")
    mine = lax.axis_index("replica")
    for ref, side in ((own_ref, chan), (partner_ref, 1 - chan)):
        half_ref[...] = ref[...].T
        both = jnp.concatenate(pick_parts(half_ref, mine, ref.shape[1] // 4), 0)
        place_rows(pieces, both, side, out_ref, slice(None))


def far_kernel(layer, grad_ref, out_ref):
    write_shifts(grad_ref, out_ref, -dilations[layer])


def write_carried(values, out_ref, low):
    first = values.astype(BF16).astype(F32)
    second = (values - first).astype(BF16).astype(F32)
    third = values - first - second
    shape = (CARRIED, values.shape[1])
    row = lax.broadcasted_iota(jnp.int32, shape, 0)
    block = jnp.where(row == 0, first, jnp.where(row == 1, second, jnp.where(row == 2, third, 0.0)))
    out_ref[low : low + CARRIED, :] = block.astype(BF16)


def read_carried(ref, low):
    block = ref[low : low + CARRIED, :].astype(F32)
    return (block[0:1, :] + block[1:2, :]) + block[2:3, :]


def paired_weight_kernel(pieces, low, carry, own_ref, shifted_ref, across_ref, across_other_ref, far_ref, *rest):
    if carry:
        write_carried(jnp.concatenate([ref[...] for ref in rest[:carry]], 1), rest[carry], own_ref.shape[0] // 2)
        rest = rest[carry:]
    outs, turned_ref = rest[:-1], rest[-1]
    half = own_ref.shape[0]
    chan = lax.axis_index("chan")
    for ref, side in ((across_ref, chan), (across_other_ref, 1 - chan)):
        place_rows(pieces, ref[low : low + half // 2, :], side, turned_ref, slice(None))
    for tap in range(3):
        span = slice(tap * half, (tap + 1) * half)
        product = jnp.dot(own_ref[...], shifted_ref[:, span], preferred_element_type=F32)
        product += jnp.dot(turned_ref[...], far_ref[:, span], preferred_element_type=F32)
        product = product.astype(BF16)
        size = product.shape[0] // len(outs)
        for place, ref in enumerate(outs):
            ref[0:size, span] = product[place * size : (place + 1) * size, :]


def finish_kernel(paired, held, carry, counts, *refs):
    total_ref, sems = refs[-2:]
    refs = list(refs[1:-2] if held else refs[:-2])
    if carry:
        alpha_ref = refs.pop()
        alpha_mine = refs.pop(0)
    out_ref = refs.pop()
    half = total_ref.shape[3]
    rows_of = total_ref.shape[2] // (2 if paired else 1)
    copies = []
    for index, (layer, pieces) in enumerate(counts):
        for part in range(pieces):
            mine_ref, other_ref = refs.pop(0), refs.pop(0)
            size = rows_of
            if carry and other_ref.shape[0] > size:
                alpha = alpha_mine[...] + read_carried(other_ref, size)
                for place in range(3):
                    alpha_ref[place : place + 1, :] = alpha[:, place * half : (place + 1) * half]
            for tap in range(3):
                span = slice(tap * half, (tap + 1) * half)
                mine, other = mine_ref[0:size, span].astype(F32), other_ref[0:size, span].astype(F32)
                if paired:
                    begin = lax.axis_index("replica") * (size * pieces)
                    for values, start in ((mine, begin), (other, size * pieces - begin)):
                        place = pl.multiple_of(start + part * size, size)
                        total_ref[index, tap, pl.ds(place, size), :] = values
                else:
                    total_ref[index, tap] = mine + other
        copies.append(pltpu.make_async_copy(total_ref.at[index], out_ref.at[layer], sems.at[index]))
        copies[-1].start()
    for copy in copies:
        copy.wait()


def fold_kernel(carry, keep, got, *rest):
    if carry:
        mine, rest = rest[:carry], rest[carry:]
        send, sum_ref = rest
    else:
        (send,) = rest
    rows = keep.shape[0] // 2
    send[0:rows, :] = (keep[rows:, :].astype(F32) + got[rows : 2 * rows, :].astype(F32)).astype(BF16)
    if carry:
        values = jnp.concatenate([ref[...] for ref in mine], 1) + read_carried(got, 2 * rows)
        sum_ref[...] = values
        write_carried(values, send, rows)


def total_kernel(carry, keep, got, late, *rest):
    if carry:
        mine, out_ref, sum_ref = rest
    else:
        (out_ref,) = rest
    rows = keep.shape[0] // 2
    total = keep[0:rows, :].astype(F32) + got[0:rows, :].astype(F32) + late[0:rows, :].astype(F32)
    out_ref[0:rows, :] = total.astype(BF16)
    if carry:
        values = mine[...] + read_carried(late, rows)
        sum_ref[...] = values
        write_carried(values, out_ref, rows)


def stack_kernel(*refs):
    for index, ref in enumerate(refs[:-1]):
        refs[-1][index : index + 1, :] = ref[...]


def add_kernel(left, right, out_ref):
    out_ref[...] = left[...] + right[...]


def struct(shape, dtype):
    return jax.ShapeDtypeStruct(shape, dtype)


def after(value, other):
    return value if other is None else lax.optimization_barrier((value, other))[0]


class Sequence:
    def __init__(self):
        self.latest = None
        self.weight = 10

    def hold(self, value):
        return after(value, self.latest)

    def call(self, kernel, name, ins, outs, scratch, flops, *args, specs=None, aliases=None):
        single = not isinstance(outs, list)
        size = sum(a.size * a.dtype.itemsize for a in args if a.size < 2000000)
        size += sum(math.prod(o.shape) * o.dtype.itemsize for o in ([outs] if single else outs))
        args = [pltpu.with_memory_space_constraint(a, pltpu.HBM) if i == 1 else a for i, a in zip(ins, args)]
        if self.latest is not None:
            held = ins.index(0)
            args[held] = self.hold(args[held])
        result = pl.pallas_call(
            kernel,
            in_specs=[ANY_HBM if i else IN_VMEM for i in ins],
            out_specs=specs or (IN_VMEM if single else [IN_VMEM] * len(outs)),
            out_shape=outs,
            scratch_shapes=scratch,
            input_output_aliases=aliases or {},
            compiler_params=pltpu.CompilerParams(vmem_limit_bytes=24 * 1024 * 1024),
            cost_estimate=pl.CostEstimate(flops=int(flops * self.weight), bytes_accessed=int(size * self.weight), transcendentals=0),
            name=name,
        )(*args)
        self.latest = result if single else result[-1]
        return result


def swap(x, axis, other):
    return lax.ppermute(x, axis, [(i, other(i)) for i in range(lax.axis_size(axis))])


def across_chan(x):
    return swap(x, "chan", lambda i: i ^ 1)


def across_replica(x):
    return swap(x, "replica", lambda i: i ^ 1)


def on_device(activations, cotangent, conv_weights, snake_alpha, seg_lengths, seg_owner, seg_start):
    rows, half = activations.shape
    layers, taps, channels, _ = conv_weights.shape
    top = layers - 1
    fast = lax.axis_size("dp") == 4 and lax.axis_size("replica") == 2
    counts = [1] * layers
    carrier = 1 if fast else None
    weight = {}
    tile, triple = (rows, half), (rows, taps * half)
    flops = 2 * rows * half * half * taps
    sequence = Sequence()
    streams, mine, partners, owns = [], [], {}, {}
    rounded, shifted, arrived, back_owns, far = {}, {}, {}, {}, {}
    across, across_other = {}, {}
    alpha_parts = [None] * layers
    kept, got, late, summed, crossed = {}, {}, {}, {}, {}

    loaded = (2, taps * half, half)
    sems = DMA((2 * taps,))

    def forward_own(layer, load=None):
        outs, args, ins = struct(tile, F32), [mine[layer], weight[layer]], [0, 0]
        scratch = [pltpu.VMEM(triple, BF16)]
        if load is not None:
            outs, args, ins = [outs, struct(loaded, BF16)], args + [conv_weights], ins + [1]
            scratch.append(sems)
        result = sequence.call(
            functools.partial(forward_own_kernel, layer, load), "forward_own", ins, outs, scratch, flops, *args
        )
        if load is None:
            owns[layer] = result
        else:
            owns[layer], weight[load] = result

    def forward_partner(layer, load=None):
        last = layer == top
        ins, args = [0] * 5, [partners[layer], weight[layer], owns[layer], streams[layer], live]
        outs = [struct(tile, BF16)] if last else [struct(tile, F32), struct(tile, BF16)]
        scratch = [pltpu.VMEM(triple, BF16)]
        if not last:
            ins, args = ins + [0], args + [alphas]
        if load is not None:
            ins, args, outs = ins + [1], args + [conv_weights], outs + [struct(loaded, BF16)]
            scratch.append(sems)
        result = sequence.call(
            functools.partial(forward_partner_kernel, layer, last, load), "forward_partner", ins, outs, scratch,
            flops, *args,
        )
        if load is not None:
            weight[load] = result[-1]
        if last:
            return result[0]
        streams.append(result[0])
        mine.append(result[1])
        partners[layer + 1] = across_chan(result[1])

    def back_partner(layer):
        shifted[layer], part = sequence.call(
            functools.partial(back_partner_kernel, layer), "back_partner", [0, 0],
            [struct(triple, BF16), struct(tile, BF16)], [], flops, rounded[layer + 1], weight[layer],
        )
        arrived[layer] = across_chan(part)

    def back_own(layer):
        back_owns[layer] = sequence.call(
            back_own_kernel, "back_own", [0, 0], struct(tile, F32), [], flops, shifted[layer], weight[layer]
        )

    def send_gradient(layer):
        if fast:
            far[layer] = across_replica(sequence.hold(rounded[layer + 1]))

    def combine(layer, grad):
        args = [back_owns[layer], arrived[layer], streams[layer], alphas]
        outs = [struct((1, half), F32)]
        if layer > 0:
            args += [grad, live]
            outs += [struct(tile, F32)] * (layer > 1) + [struct(tile, BF16)]
        result = sequence.call(
            functools.partial(combine_kernel, layer), "combine", [0] * len(args), outs, [], 60 * rows * half, *args
        )
        alpha_parts[layer] = result[0]
        if layer > 0:
            rounded[layer] = result[-1]
            return result[1]

    def turn(*chosen):
        if fast:
            moved_rows = across_replica(sequence.call(
                turn_kernel, "turn", [0] * len(chosen), struct((len(chosen) * half // 2, rows), BF16),
                [pltpu.VMEM((half, rows), BF16)], 10 * rows * half, *[mine[layer] for layer in chosen],
            ))
            for index, layer in enumerate(chosen):
                across[layer] = (moved_rows, index * half // 2)

    def share(*chosen):
        if fast:
            shared = across_chan(sequence.hold(across[chosen[0]][0]))
            for layer in chosen:
                across_other[layer] = shared

    own_turned, far_shifted = {}, {}

    def own_rows(layer):
        if fast:
            own_turned[layer] = sequence.call(
                functools.partial(own_rows_kernel, counts[layer]), "own_rows", [0, 0], struct((half, rows), BF16),
                [pltpu.VMEM((half, rows), BF16)], 10 * rows * half, mine[layer], partners[layer],
            )

    def far_rows(layer):
        if fast:
            far_shifted[layer] = sequence.call(
                functools.partial(far_kernel, layer), "far_rows", [0], struct(triple, BF16), [],
                10 * rows * half, far[layer],
            )

    def weights(layer):
        if not fast:
            out = sequence.call(
                weight_kernel, "weight", [0] * 3, struct((channels, taps * half), BF16),
                [pltpu.VMEM((channels, rows), BF16)], 2 * flops, mine[layer], partners[layer], shifted[layer],
            )
            part = lax.psum_scatter(out, "dp", scatter_dimension=0, tiled=True)
            summed[layer, 0] = lax.psum(part, "replica")
            crossed[layer, 0] = jnp.zeros_like(part)
            return
        pieces, depth = counts[layer], channels // 4 // counts[layer]
        carried = alpha_parts if layer == carrier else []
        outs = [struct((depth, taps * half), BF16)] * (2 * pieces)
        if carried:
            outs[0] = struct((depth + CARRIED, taps * half), BF16)
        args = [own_turned[layer], shifted[layer], across[layer][0], across_other[layer], far_shifted[layer], *carried]
        out = sequence.call(
            functools.partial(paired_weight_kernel, pieces, across[layer][1], len(carried)), "paired_weight",
            [0] * len(args), outs, [pltpu.VMEM((half, rows), BF16)], 2 * flops, *args,
        )
        for part in range(pieces):
            got[layer, part] = swap(out[part], "dp", lambda i: i ^ 1)
            kept[layer, part] = out[pieces + part]

    carry_sum = [None]

    def fold(layer, part=0):
        if not fast:
            return
        keep, came = kept[layer, part], got[layer, part]
        depth, carried = keep.shape[0] // 2, alpha_parts if layer == carrier else []
        outs = [struct((depth + CARRIED * bool(carried), taps * half), BF16)]
        if carried:
            outs.append(struct((1, taps * half), F32))
        result = sequence.call(
            functools.partial(fold_kernel, len(carried)), "fold", [0] * (2 + len(carried)), outs, [], keep.size,
            keep, came, *carried,
        )
        if carried:
            carry_sum[0] = result[1]
        late[layer, part] = swap(result[0], "dp", lambda i: i ^ 3)

    def total(layer, part=0):
        if not fast:
            return
        keep, came, last = kept[layer, part], got[layer, part], late[layer, part]
        outs, args = [struct(last.shape, BF16)], [keep, came, last]
        if layer == carrier:
            outs.append(struct((1, taps * half), F32))
            args.append(carry_sum[0])
        result = sequence.call(
            functools.partial(total_kernel, layer == carrier), "total", [0] * len(args), outs, [], 2 * flops, *args
        )
        if layer == carrier:
            carry_sum[0] = result[1]
        summed[layer, part] = result[0]

    def cross(layer, part=0):
        if fast:
            crossed[layer, part] = across_replica(sequence.hold(summed[layer, part]))

    stream, snaked, grad, live, alphas, weight[0] = sequence.call(
        prep_kernel, "prep", [1] * 7,
        [struct(tile, F32), struct(tile, BF16), struct(tile, BF16), struct((rows, 128), F32),
         struct(snake_alpha.shape, F32), struct(loaded, BF16)],
        [pltpu.SMEM(seg_lengths.shape, jnp.int32)] * 3 + [pltpu.VMEM(tile, BF16)] * 2 + [DMA((6,)), sems],
        40 * rows * half,
        seg_lengths, seg_owner, seg_start, activations, cotangent, snake_alpha, conv_weights,
    )
    streams.append(stream)
    mine.append(snaked)
    partners[0] = across_chan(snaked)
    rounded[layers] = grad
    depth = channels // lax.axis_size("dp")

    def finish(chosen, before=None):
        pairs = [] if before is None else [before]
        carry = carrier in chosen
        if carry:
            pairs.append(carry_sum[0])
        for layer in chosen:
            for part in range(counts[layer]):
                pairs += [summed[layer, part], crossed[layer, part]]
        out = struct((layers, taps, depth, half), F32)
        return sequence.call(
            functools.partial(
                finish_kernel, fast, before is not None, carry, tuple((layer, counts[layer]) for layer in chosen)
            ),
            "finish", [2] * (before is not None) + [0] * (len(pairs) - (before is not None)),
            [out, struct((layers, half), F32)] if carry else [out],
            [pltpu.VMEM((len(chosen), taps, depth, half), F32), DMA((len(chosen),))],
            layers * taps * depth * half, *pairs, specs=[ANY_HBM] + [IN_VMEM] * carry,
            aliases={0: 0} if before is not None else None,
        )

    rounds = [("replica", 1 << bit) for bit in range(8) if lax.axis_size("replica") >> (bit + 1)]
    rounds += [("dp", 1 << bit) for bit in range(8) if lax.axis_size("dp") >> (bit + 1)]
    arrivals = []

    def alpha_round():
        if arrivals:
            value = sequence.call(
                add_kernel, "add", [0, 0], struct((layers, half), F32), [], layers * half, *arrivals.pop()
            )
        else:
            value = sequence.call(
                stack_kernel, "stack", [0] * layers, struct((layers, half), F32), [], layers * half, *alpha_parts
            )
        if not rounds:
            return value
        axis, apart = rounds.pop(0)
        arrivals.append((value, swap(value, axis, lambda place: place ^ apart)))

    send_gradient(2)
    forward_own(0, load=2)
    forward_partner(0, load=1)
    back_partner(2)
    forward_own(1)
    forward_partner(1)
    turn(2)
    back_own(2)
    grad = combine(2, grad)
    send_gradient(1)
    far_rows(2)
    own_rows(2)
    turn(1, 0)
    back_partner(1)
    share(2)
    back_own(1)
    combine(1, grad)
    back_partner(0)
    back_own(0)
    weights(2)
    sequence.weight = 10
    combine(0, None)
    own_rows(1)
    own_rows(0)
    forward_own(2)
    residual_out = forward_partner(2)
    far_rows(1)
    fold(2)
    share(1, 0)
    send_gradient(0)
    sequence.weight = 10
    total(2)
    weights(1)
    cross(2)
    sequence.weight = 0.01
    far_rows(0)
    weights(0)
    sequence.weight = 10
    fold(1)
    fold(0)
    total(1)
    cross(1)
    total(0)
    cross(0)
    if fast:
        weight_grads, alpha_grads = finish((2, 1))
        (weight_grads,) = finish((0,), weight_grads)
    else:
        alpha_grads = alpha_round()
        while alpha_grads is None:
            alpha_grads = alpha_round()
        (weight_grads,) = finish((2, 1, 0))
    return (residual_out, weight_grads, alpha_grads)


def solution(mesh):
    return jax.shard_map(
        on_device,
        mesh=mesh,
        in_specs=(
            P(("groups", "dp", "replica"), "chan"),
            P(("groups", "dp", "replica"), "chan"),
            P(None, None, None, "chan"),
            P(None, "chan"),
            P("groups"),
            P("groups"),
            P("groups"),
        ),
        out_specs=(
            P(("groups", "dp", "replica"), "chan"),
            P("groups", None, "dp", "chan"),
            P("groups", "chan"),
        ),
        check_vma=False,
    )
```

```python
import functools
import math

import jax
import jax.numpy as jnp
from jax import lax
from jax.experimental import pallas as pl
from jax.experimental.pallas import tpu as pltpu
from jax.sharding import PartitionSpec as P

dilations = (1, 3, 5)
F32, BF16 = jnp.float32, jnp.bfloat16
ANY_HBM = pl.BlockSpec(memory_space=pltpu.HBM)
IN_VMEM = pl.BlockSpec(memory_space=pltpu.VMEM)
DMA = pltpu.SemaphoreType.DMA
PI_PARTS = (3.140625, 9.67502593994140625e-4, 1.509957990978376432e-7)
SIN_TERMS = (-1.0 / 39916800, 1.0 / 362880, -1.0 / 5040, 1.0 / 120, -1.0 / 6)
COS_TERMS = (1.0 / 479001600, -1.0 / 3628800, 1.0 / 40320, -1.0 / 720, 1.0 / 24, -0.5)
RANGE = 8192.0
CHUNK = 64
CARRIED = 16


def horner(terms, x):
    total = jnp.full_like(x, terms[0])
    for term in terms[1:]:
        total = total * x + term
    return total


def reduced(angle):
    turns = jnp.round(angle * (1.0 / 3.14159265358979))
    for part in PI_PARTS:
        angle = angle - turns * part
    return angle


def sine(angle, exact_range):
    if not exact_range:
        return jnp.sin(angle)
    rest = reduced(angle)
    square = rest * rest
    return rest + rest * (square * horner(SIN_TERMS, square))


def sine_cosine(angle, exact_range):
    if not exact_range:
        return jnp.sin(angle), jnp.cos(angle)
    rest = reduced(angle)
    square = rest * rest
    return (
        rest + rest * (square * horner(SIN_TERMS, square)),
        1.0 + square * horner(COS_TERMS, square),
    )


def by_range(bound, body):
    @pl.when(bound < RANGE)
    def _():
        body(True)

    @pl.when(bound >= RANGE)
    def _():
        body(False)


def write_snake(stream_ref, alpha, out_ref):
    inverse = 1.0 / alpha
    bound = jnp.max(jnp.abs(stream_ref[...])) * jnp.max(alpha)

    def body(exact_range):
        @pl.loop(0, stream_ref.shape[0] // CHUNK)
        def _(step):
            rows = pl.ds(pl.multiple_of(step * CHUNK, CHUNK), CHUNK)
            stream = stream_ref[rows, :]
            wave = sine(alpha * stream, exact_range)
            out_ref[rows, :] = (stream + wave * wave * inverse).astype(BF16)

    by_range(bound, body)


def moved(values, offset):
    if offset == 0:
        return values
    rows = values.shape[0]
    place = lax.broadcasted_iota(jnp.int32, values.shape, 0)
    turned = pltpu.roll(values, (-offset) % rows, 0)
    inside = place < rows - offset if offset > 0 else place >= -offset
    return jnp.where(inside, turned, 0.0)


def write_shifts(values_ref, out_ref, dilation):
    width = values_ref.shape[1]
    values = values_ref[...].astype(F32)
    for tap in range(3):
        out_ref[:, tap * width : (tap + 1) * width] = moved(values, (tap - 1) * dilation).astype(BF16)


def chan_begin(side, half):
    chan = lax.axis_index("chan")
    return pl.multiple_of((chan if side == 0 else 1 - chan) * half, half)


def load_weights(layer, weight_hbm, weight_ref, sems):
    half = weight_hbm.shape[3]
    loads = []
    for side in range(2):
        for tap in range(3):
            source = weight_hbm.at[layer, tap, pl.ds(chan_begin(side, half), half), :]
            target = weight_ref.at[side, pl.ds(tap * half, half), :]
            loads.append(pltpu.make_async_copy(source, target, sems.at[len(loads)]))
    for copy in loads:
        copy.start()
    return loads


def prep_kernel(
    len_hbm, own_hbm, start_hbm, act_hbm, cot_hbm, alpha_hbm, weight_hbm,
    stream_ref, snake_ref, grad_ref, live_ref, alpha_ref, weight_ref,
    len_ref, own_ref, start_ref, act_ref, cot_ref, sems, weight_sems,
):
    pairs = (
        (len_hbm, len_ref), (own_hbm, own_ref), (start_hbm, start_ref),
        (alpha_hbm, alpha_ref), (act_hbm, act_ref), (cot_hbm, cot_ref),
    )
    copies = [pltpu.make_async_copy(a, b, sems.at[i]) for i, (a, b) in enumerate(pairs)]
    for copy in copies:
        copy.start()
    loads = load_weights(0, weight_hbm, weight_ref, weight_sems)
    replicas = lax.axis_size("replica")
    device = lax.axis_index("dp") * replicas + lax.axis_index("replica")
    rows, width = act_ref.shape
    place = lax.broadcasted_iota(jnp.int32, (rows, 128), 0)
    live_ref[...] = jnp.zeros((rows, 128), F32)
    for copy in copies[:3]:
        copy.wait()

    @pl.loop(0, len_ref.shape[0])
    def _(clip):
        @pl.when(own_ref[clip] == device)
        def _():
            first = start_ref[clip]
            inside = (place >= first) & (place < first + len_ref[clip])
            live_ref[...] = jnp.where(inside, 1.0, live_ref[...])

    live = jnp.tile(live_ref[...], (1, width // 128))
    for copy in copies[3:5]:
        copy.wait()
    stream_ref[...] = act_ref[...].astype(F32) * live
    write_snake(stream_ref, alpha_ref[0:1, :], snake_ref)
    copies[5].wait()
    grad_ref[...] = (cot_ref[...].astype(F32) * live).astype(BF16)
    for copy in loads:
        copy.wait()


def forward_own_kernel(layer, load, snake_ref, weight_ref, *rest):
    if load is None:
        out_ref, shifts_ref = rest
        loads = []
    else:
        weight_hbm, out_ref, loaded_ref, shifts_ref, sems = rest
        loads = load_weights(load, weight_hbm, loaded_ref, sems)
    write_shifts(snake_ref, shifts_ref, dilations[layer])
    out_ref[...] = jnp.dot(shifts_ref[...], weight_ref[0], preferred_element_type=F32)
    for copy in loads:
        copy.wait()


def forward_partner_kernel(layer, last, load, snake_ref, weight_ref, own_ref, old_ref, live_ref, *rest):
    rest = list(rest)
    alpha_ref = None if last else rest.pop(0)
    weight_hbm = None if load is None else rest.pop(0)
    result_ref = rest.pop(0)
    next_ref = None if last else rest.pop(0)
    loads = []
    if load is not None:
        loaded_ref, shifts_ref, sems = rest
        loads = load_weights(load, weight_hbm, loaded_ref, sems)
    else:
        (shifts_ref,) = rest
    write_shifts(snake_ref, shifts_ref, dilations[layer])
    part = jnp.dot(shifts_ref[...], weight_ref[1], preferred_element_type=F32)
    live = jnp.tile(live_ref[...], (1, old_ref.shape[1] // 128))
    new = (old_ref[...] + (own_ref[...] + part)) * live
    result_ref[...] = new.astype(result_ref.dtype)
    if not last:
        write_snake(result_ref, alpha_ref[layer + 1 : layer + 2, :], next_ref)
    for copy in loads:
        copy.wait()


def back_product(shifted_ref, weight_ref, side):
    half = weight_ref.shape[2]
    total = None
    for tap in range(3):
        span = slice(tap * half, (tap + 1) * half)
        part = lax.dot_general(
            shifted_ref[:, span], weight_ref[side, span, :], (((1,), (1,)), ((), ())),
            preferred_element_type=F32,
        )
        total = part if total is None else total + part
    return total


def back_partner_kernel(layer, grad_ref, weight_ref, shifted_ref, out_ref):
    write_shifts(grad_ref, shifted_ref, -dilations[layer])
    out_ref[...] = back_product(shifted_ref, weight_ref, 1).astype(BF16)


def back_own_kernel(shifted_ref, weight_ref, out_ref):
    out_ref[...] = back_product(shifted_ref, weight_ref, 0)


def combine_kernel(layer, own_ref, partner_ref, stream_ref, alphas_ref, *rest):
    if layer == 0:
        (alpha_grad_ref,) = rest
    elif len(rest) == 5:
        old_ref, live_ref, alpha_grad_ref, grad_ref, rounded_ref = rest
    else:
        old_ref, live_ref, alpha_grad_ref, rounded_ref = rest
        grad_ref = None
    alpha = alphas_ref[layer : layer + 1, :]
    inverse = 1.0 / alpha
    bound = jnp.max(jnp.abs(stream_ref[...])) * jnp.max(alpha)
    width = stream_ref.shape[1]

    def body(exact_range):
        def step_body(step, total):
            rows = pl.ds(pl.multiple_of(step * CHUNK, CHUNK), CHUNK)
            stream = stream_ref[rows, :]
            back = own_ref[rows, :] + partner_ref[rows, :].astype(F32)
            sin, cos = sine_cosine(alpha * stream, exact_range)
            double = 2.0 * sin * cos
            ratio = sin * inverse
            term = back * (stream * double * inverse - ratio * ratio)
            if layer > 0:
                live = jnp.tile(live_ref[rows, :], (1, width // 128))
                grad = (old_ref[rows, :].astype(F32) + back * (1.0 + double)) * live
                if grad_ref is not None:
                    grad_ref[rows, :] = grad
                rounded_ref[rows, :] = grad.astype(BF16)
            return total + jnp.sum(term.reshape(CHUNK // 8, 8, width), axis=0)

        total = lax.fori_loop(0, stream_ref.shape[0] // CHUNK, step_body, jnp.zeros((8, width), F32))
        alpha_grad_ref[...] = jnp.sum(total, axis=0, keepdims=True)

    by_range(bound, body)


def block_place(pieces, slice_index, part):
    apart = jnp.bitwise_xor(slice_index, lax.axis_index("dp"))
    order = (2 * pieces, 0, 1, 2 * pieces + 1)
    return 2 * part + jnp.where(
        apart == 0, order[0], jnp.where(apart == 1, order[1], jnp.where(apart == 2, order[2], order[3]))
    )


def weight_kernel(own_ref, partner_ref, shifted_ref, out_ref, turned_ref):
    half = own_ref.shape[1]
    chan = lax.axis_index("chan")
    for ref, side in ((own_ref, chan), (partner_ref, 1 - chan)):
        turned_ref[pl.ds(pl.multiple_of(side * half, half), half), :] = ref[...].T
    for tap in range(3):
        span = slice(tap * half, (tap + 1) * half)
        out_ref[:, span] = jnp.dot(turned_ref[...], shifted_ref[:, span], preferred_element_type=F32).astype(BF16)


def place_rows(pieces, rows_of, side, target_ref, columns):
    size = rows_of.shape[0] // (2 * pieces)
    for local in range(2):
        for part in range(pieces):
            begin = pl.multiple_of(block_place(pieces, side * 2 + local, part) * size, size)
            low = (local * pieces + part) * size
            target_ref[pl.ds(begin, size), columns] = rows_of[low : low + size, :]


def pick_parts(turned_ref, part, size):
    begin = pl.multiple_of(part * size, size)
    return [turned_ref[pl.ds(local * 2 * size + begin, size), :] for local in range(2)]


def turn_kernel(*refs):
    snakes, out_ref, turned_ref = refs[:-2], refs[-2], refs[-1]
    size = snakes[0].shape[1] // 4
    for index, ref in enumerate(snakes):
        turned_ref[...] = ref[...].T
        for local, piece in enumerate(pick_parts(turned_ref, 1 - lax.axis_index("replica"), size)):
            low = (2 * index + local) * size
            out_ref[low : low + size, :] = piece


def own_rows_kernel(pieces, own_ref, partner_ref, out_ref, half_ref):
    chan = lax.axis_index("chan")
    mine = lax.axis_index("replica")
    for ref, side in ((own_ref, chan), (partner_ref, 1 - chan)):
        half_ref[...] = ref[...].T
        both = jnp.concatenate(pick_parts(half_ref, mine, ref.shape[1] // 4), 0)
        place_rows(pieces, both, side, out_ref, slice(None))


def far_kernel(layer, grad_ref, out_ref):
    write_shifts(grad_ref, out_ref, -dilations[layer])


def write_carried(values, out_ref, low):
    first = values.astype(BF16).astype(F32)
    second = (values - first).astype(BF16).astype(F32)
    third = values - first - second
    shape = (CARRIED, values.shape[1])
    row = lax.broadcasted_iota(jnp.int32, shape, 0)
    block = jnp.where(row == 0, first, jnp.where(row == 1, second, jnp.where(row == 2, third, 0.0)))
    out_ref[low : low + CARRIED, :] = block.astype(BF16)


def read_carried(ref, low):
    block = ref[low : low + CARRIED, :].astype(F32)
    return (block[0:1, :] + block[1:2, :]) + block[2:3, :]


def paired_weight_kernel(pieces, low, carry, own_ref, shifted_ref, across_ref, across_other_ref, far_ref, *rest):
    if carry:
        write_carried(jnp.concatenate([ref[...] for ref in rest[:carry]], 1), rest[carry], own_ref.shape[0] // 2)
        rest = rest[carry:]
    outs, turned_ref = rest[:-1], rest[-1]
    half = own_ref.shape[0]
    chan = lax.axis_index("chan")
    for ref, side in ((across_ref, chan), (across_other_ref, 1 - chan)):
        place_rows(pieces, ref[low : low + half // 2, :], side, turned_ref, slice(None))
    for tap in range(3):
        span = slice(tap * half, (tap + 1) * half)
        product = jnp.dot(own_ref[...], shifted_ref[:, span], preferred_element_type=F32)
        product += jnp.dot(turned_ref[...], far_ref[:, span], preferred_element_type=F32)
        product = product.astype(BF16)
        size = product.shape[0] // len(outs)
        for place, ref in enumerate(outs):
            ref[0:size, span] = product[place * size : (place + 1) * size, :]


def finish_kernel(paired, held, carry, counts, *refs):
    total_ref, sems = refs[-2:]
    refs = list(refs[1:-2] if held else refs[:-2])
    if carry:
        alpha_ref = refs.pop()
        alpha_mine = refs.pop(0)
    out_ref = refs.pop()
    half = total_ref.shape[3]
    rows_of = total_ref.shape[2] // (2 if paired else 1)
    copies = []
    for index, (layer, pieces) in enumerate(counts):
        for part in range(pieces):
            mine_ref, other_ref = refs.pop(0), refs.pop(0)
            size = rows_of
            if carry and other_ref.shape[0] > size:
                alpha = alpha_mine[...] + read_carried(other_ref, size)
                for place in range(3):
                    alpha_ref[place : place + 1, :] = alpha[:, place * half : (place + 1) * half]
            for tap in range(3):
                span = slice(tap * half, (tap + 1) * half)
                mine, other = mine_ref[0:size, span].astype(F32), other_ref[0:size, span].astype(F32)
                if paired:
                    begin = lax.axis_index("replica") * (size * pieces)
                    for values, start in ((mine, begin), (other, size * pieces - begin)):
                        place = pl.multiple_of(start + part * size, size)
                        total_ref[index, tap, pl.ds(place, size), :] = values
                else:
                    total_ref[index, tap] = mine + other
        copies.append(pltpu.make_async_copy(total_ref.at[index], out_ref.at[layer], sems.at[index]))
        copies[-1].start()
    for copy in copies:
        copy.wait()


def fold_kernel(carry, keep, got, *rest):
    if carry:
        mine, rest = rest[:carry], rest[carry:]
        send, sum_ref = rest
    else:
        (send,) = rest
    rows = keep.shape[0] // 2
    send[0:rows, :] = (keep[rows:, :].astype(F32) + got[rows : 2 * rows, :].astype(F32)).astype(BF16)
    if carry:
        values = jnp.concatenate([ref[...] for ref in mine], 1) + read_carried(got, 2 * rows)
        sum_ref[...] = values
        write_carried(values, send, rows)


def total_kernel(carry, keep, got, late, *rest):
    if carry:
        mine, out_ref, sum_ref = rest
    else:
        (out_ref,) = rest
    rows = keep.shape[0] // 2
    total = keep[0:rows, :].astype(F32) + got[0:rows, :].astype(F32) + late[0:rows, :].astype(F32)
    out_ref[0:rows, :] = total.astype(BF16)
    if carry:
        values = mine[...] + read_carried(late, rows)
        sum_ref[...] = values
        write_carried(values, out_ref, rows)


def stack_kernel(*refs):
    for index, ref in enumerate(refs[:-1]):
        refs[-1][index : index + 1, :] = ref[...]


def add_kernel(left, right, out_ref):
    out_ref[...] = left[...] + right[...]


def struct(shape, dtype):
    return jax.ShapeDtypeStruct(shape, dtype)


def after(value, other):
    return value if other is None else lax.optimization_barrier((value, other))[0]


class Sequence:
    def __init__(self):
        self.latest = None
        self.weight = 10

    def hold(self, value):
        return after(value, self.latest)

    def call(self, kernel, name, ins, outs, scratch, flops, *args, specs=None, aliases=None):
        single = not isinstance(outs, list)
        size = sum(a.size * a.dtype.itemsize for a in args if a.size < 2000000)
        size += sum(math.prod(o.shape) * o.dtype.itemsize for o in ([outs] if single else outs))
        args = [pltpu.with_memory_space_constraint(a, pltpu.HBM) if i == 1 else a for i, a in zip(ins, args)]
        if self.latest is not None:
            held = ins.index(0)
            args[held] = self.hold(args[held])
        result = pl.pallas_call(
            kernel,
            in_specs=[ANY_HBM if i else IN_VMEM for i in ins],
            out_specs=specs or (IN_VMEM if single else [IN_VMEM] * len(outs)),
            out_shape=outs,
            scratch_shapes=scratch,
            input_output_aliases=aliases or {},
            compiler_params=pltpu.CompilerParams(vmem_limit_bytes=24 * 1024 * 1024),
            cost_estimate=pl.CostEstimate(flops=int(flops * self.weight), bytes_accessed=int(size * self.weight), transcendentals=0),
            name=name,
        )(*args)
        self.latest = result if single else result[-1]
        return result


def swap(x, axis, other):
    return lax.ppermute(x, axis, [(i, other(i)) for i in range(lax.axis_size(axis))])


def across_chan(x):
    return swap(x, "chan", lambda i: i ^ 1)


def across_replica(x):
    return swap(x, "replica", lambda i: i ^ 1)


def on_device(activations, cotangent, conv_weights, snake_alpha, seg_lengths, seg_owner, seg_start):
    rows, half = activations.shape
    layers, taps, channels, _ = conv_weights.shape
    top = layers - 1
    fast = lax.axis_size("dp") == 4 and lax.axis_size("replica") == 2
    counts = [1] * layers
    carrier = 1 if fast else None
    weight = {}
    tile, triple = (rows, half), (rows, taps * half)
    flops = 2 * rows * half * half * taps
    sequence = Sequence()
    streams, mine, partners, owns = [], [], {}, {}
    rounded, shifted, arrived, back_owns, far = {}, {}, {}, {}, {}
    across, across_other = {}, {}
    alpha_parts = [None] * layers
    kept, got, late, summed, crossed = {}, {}, {}, {}, {}

    loaded = (2, taps * half, half)
    sems = DMA((2 * taps,))

    def forward_own(layer, load=None):
        outs, args, ins = struct(tile, F32), [mine[layer], weight[layer]], [0, 0]
        scratch = [pltpu.VMEM(triple, BF16)]
        if load is not None:
            outs, args, ins = [outs, struct(loaded, BF16)], args + [conv_weights], ins + [1]
            scratch.append(sems)
        result = sequence.call(
            functools.partial(forward_own_kernel, layer, load), "forward_own", ins, outs, scratch, flops, *args
        )
        if load is None:
            owns[layer] = result
        else:
            owns[layer], weight[load] = result

    def forward_partner(layer, load=None):
        last = layer == top
        ins, args = [0] * 5, [partners[layer], weight[layer], owns[layer], streams[layer], live]
        outs = [struct(tile, BF16)] if last else [struct(tile, F32), struct(tile, BF16)]
        scratch = [pltpu.VMEM(triple, BF16)]
        if not last:
            ins, args = ins + [0], args + [alphas]
        if load is not None:
            ins, args, outs = ins + [1], args + [conv_weights], outs + [struct(loaded, BF16)]
            scratch.append(sems)
        result = sequence.call(
            functools.partial(forward_partner_kernel, layer, last, load), "forward_partner", ins, outs, scratch,
            flops, *args,
        )
        if load is not None:
            weight[load] = result[-1]
        if last:
            return result[0]
        streams.append(result[0])
        mine.append(result[1])
        partners[layer + 1] = across_chan(result[1])

    def back_partner(layer):
        shifted[layer], part = sequence.call(
            functools.partial(back_partner_kernel, layer), "back_partner", [0, 0],
            [struct(triple, BF16), struct(tile, BF16)], [], flops, rounded[layer + 1], weight[layer],
        )
        arrived[layer] = across_chan(part)

    def back_own(layer):
        back_owns[layer] = sequence.call(
            back_own_kernel, "back_own", [0, 0], struct(tile, F32), [], flops, shifted[layer], weight[layer]
        )

    def send_gradient(layer):
        if fast:
            far[layer] = across_replica(sequence.hold(rounded[layer + 1]))

    def combine(layer, grad):
        args = [back_owns[layer], arrived[layer], streams[layer], alphas]
        outs = [struct((1, half), F32)]
        if layer > 0:
            args += [grad, live]
            outs += [struct(tile, F32)] * (layer > 1) + [struct(tile, BF16)]
        result = sequence.call(
            functools.partial(combine_kernel, layer), "combine", [0] * len(args), outs, [], 60 * rows * half, *args
        )
        alpha_parts[layer] = result[0]
        if layer > 0:
            rounded[layer] = result[-1]
            return result[1]

    def turn(*chosen):
        if fast:
            moved_rows = across_replica(sequence.call(
                turn_kernel, "turn", [0] * len(chosen), struct((len(chosen) * half // 2, rows), BF16),
                [pltpu.VMEM((half, rows), BF16)], 10 * rows * half, *[mine[layer] for layer in chosen],
            ))
            for index, layer in enumerate(chosen):
                across[layer] = (moved_rows, index * half // 2)

    def share(*chosen):
        if fast:
            shared = across_chan(sequence.hold(across[chosen[0]][0]))
            for layer in chosen:
                across_other[layer] = shared

    own_turned, far_shifted = {}, {}

    def own_rows(layer):
        if fast:
            own_turned[layer] = sequence.call(
                functools.partial(own_rows_kernel, counts[layer]), "own_rows", [0, 0], struct((half, rows), BF16),
                [pltpu.VMEM((half, rows), BF16)], 10 * rows * half, mine[layer], partners[layer],
            )

    def far_rows(layer):
        if fast:
            far_shifted[layer] = sequence.call(
                functools.partial(far_kernel, layer), "far_rows", [0], struct(triple, BF16), [],
                10 * rows * half, far[layer],
            )

    def weights(layer):
        if not fast:
            out = sequence.call(
                weight_kernel, "weight", [0] * 3, struct((channels, taps * half), BF16),
                [pltpu.VMEM((channels, rows), BF16)], 2 * flops, mine[layer], partners[layer], shifted[layer],
            )
            part = lax.psum_scatter(out, "dp", scatter_dimension=0, tiled=True)
            summed[layer, 0] = lax.psum(part, "replica")
            crossed[layer, 0] = jnp.zeros_like(part)
            return
        pieces, depth = counts[layer], channels // 4 // counts[layer]
        carried = alpha_parts if layer == carrier else []
        outs = [struct((depth, taps * half), BF16)] * (2 * pieces)
        if carried:
            outs[0] = struct((depth + CARRIED, taps * half), BF16)
        args = [own_turned[layer], shifted[layer], across[layer][0], across_other[layer], far_shifted[layer], *carried]
        out = sequence.call(
            functools.partial(paired_weight_kernel, pieces, across[layer][1], len(carried)), "paired_weight",
            [0] * len(args), outs, [pltpu.VMEM((half, rows), BF16)], 2 * flops, *args,
        )
        for part in range(pieces):
            got[layer, part] = swap(out[part], "dp", lambda i: i ^ 1)
            kept[layer, part] = out[pieces + part]

    carry_sum = [None]

    def fold(layer, part=0):
        if not fast:
            return
        keep, came = kept[layer, part], got[layer, part]
        depth, carried = keep.shape[0] // 2, alpha_parts if layer == carrier else []
        outs = [struct((depth + CARRIED * bool(carried), taps * half), BF16)]
        if carried:
            outs.append(struct((1, taps * half), F32))
        result = sequence.call(
            functools.partial(fold_kernel, len(carried)), "fold", [0] * (2 + len(carried)), outs, [], keep.size,
            keep, came, *carried,
        )
        if carried:
            carry_sum[0] = result[1]
        late[layer, part] = swap(result[0], "dp", lambda i: i ^ 3)

    def total(layer, part=0):
        if not fast:
            return
        keep, came, last = kept[layer, part], got[layer, part], late[layer, part]
        outs, args = [struct(last.shape, BF16)], [keep, came, last]
        if layer == carrier:
            outs.append(struct((1, taps * half), F32))
            args.append(carry_sum[0])
        result = sequence.call(
            functools.partial(total_kernel, layer == carrier), "total", [0] * len(args), outs, [], 2 * flops, *args
        )
        if layer == carrier:
            carry_sum[0] = result[1]
        summed[layer, part] = result[0]

    def cross(layer, part=0):
        if fast:
            crossed[layer, part] = across_replica(sequence.hold(summed[layer, part]))

    stream, snaked, grad, live, alphas, weight[0] = sequence.call(
        prep_kernel, "prep", [1] * 7,
        [struct(tile, F32), struct(tile, BF16), struct(tile, BF16), struct((rows, 128), F32),
         struct(snake_alpha.shape, F32), struct(loaded, BF16)],
        [pltpu.SMEM(seg_lengths.shape, jnp.int32)] * 3 + [pltpu.VMEM(tile, BF16)] * 2 + [DMA((6,)), sems],
        40 * rows * half,
        seg_lengths, seg_owner, seg_start, activations, cotangent, snake_alpha, conv_weights,
    )
    streams.append(stream)
    mine.append(snaked)
    partners[0] = across_chan(snaked)
    rounded[layers] = grad
    depth = channels // lax.axis_size("dp")

    def finish(chosen, before=None):
        pairs = [] if before is None else [before]
        carry = carrier in chosen
        if carry:
            pairs.append(carry_sum[0])
        for layer in chosen:
            for part in range(counts[layer]):
                pairs += [summed[layer, part], crossed[layer, part]]
        out = struct((layers, taps, depth, half), F32)
        return sequence.call(
            functools.partial(
                finish_kernel, fast, before is not None, carry, tuple((layer, counts[layer]) for layer in chosen)
            ),
            "finish", [2] * (before is not None) + [0] * (len(pairs) - (before is not None)),
            [out, struct((layers, half), F32)] if carry else [out],
            [pltpu.VMEM((len(chosen), taps, depth, half), F32), DMA((len(chosen),))],
            layers * taps * depth * half, *pairs, specs=[ANY_HBM] + [IN_VMEM] * carry,
            aliases={0: 0} if before is not None else None,
        )

    rounds = [("replica", 1 << bit) for bit in range(8) if lax.axis_size("replica") >> (bit + 1)]
    rounds += [("dp", 1 << bit) for bit in range(8) if lax.axis_size("dp") >> (bit + 1)]
    arrivals = []

    def alpha_round():
        if arrivals:
            value = sequence.call(
                add_kernel, "add", [0, 0], struct((layers, half), F32), [], layers * half, *arrivals.pop()
            )
        else:
            value = sequence.call(
                stack_kernel, "stack", [0] * layers, struct((layers, half), F32), [], layers * half, *alpha_parts
            )
        if not rounds:
            return value
        axis, apart = rounds.pop(0)
        arrivals.append((value, swap(value, axis, lambda place: place ^ apart)))

    forward_own(0, load=2)
    send_gradient(2)
    forward_partner(0, load=1)
    back_partner(2)
    forward_own(1)
    forward_partner(1)
    turn(2)
    back_own(2)
    grad = combine(2, grad)
    send_gradient(1)
    far_rows(2)
    own_rows(2)
    turn(1)
    back_partner(1)
    share(2)
    back_own(1)
    combine(1, grad)
    back_partner(0)
    back_own(0)
    weights(2)
    sequence.weight = 10
    combine(0, None)
    own_rows(1)
    turn(0)
    far_rows(1)
    own_rows(0)
    share(1)
    forward_own(2)
    residual_out = forward_partner(2)
    sequence.weight = 10
    weights(1)
    send_gradient(0)
    share(0)
    fold(2)
    far_rows(0)
    sequence.weight = 0.01
    weights(0)
    total(2)
    cross(2)
    sequence.weight = 10
    fold(1)
    fold(0)
    total(1)
    cross(1)
    total(0)
    cross(0)
    if fast:
        weight_grads, alpha_grads = finish((2, 1))
        (weight_grads,) = finish((0,), weight_grads)
    else:
        alpha_grads = alpha_round()
        while alpha_grads is None:
            alpha_grads = alpha_round()
        (weight_grads,) = finish((2, 1, 0))
    return (residual_out, weight_grads, alpha_grads)


def solution(mesh):
    return jax.shard_map(
        on_device,
        mesh=mesh,
        in_specs=(
            P(("groups", "dp", "replica"), "chan"),
            P(("groups", "dp", "replica"), "chan"),
            P(None, None, None, "chan"),
            P(None, "chan"),
            P("groups"),
            P("groups"),
            P("groups"),
        ),
        out_specs=(
            P(("groups", "dp", "replica"), "chan"),
            P("groups", None, "dp", "chan"),
            P("groups", "chan"),
        ),
        check_vma=False,
    )
```

```python
import functools
import math

import jax
import jax.numpy as jnp
from jax import lax
from jax.experimental import pallas as pl
from jax.experimental.pallas import tpu as pltpu
from jax.sharding import PartitionSpec as P

dilations = (1, 3, 5)
F32, BF16 = jnp.float32, jnp.bfloat16
ANY_HBM = pl.BlockSpec(memory_space=pltpu.HBM)
IN_VMEM = pl.BlockSpec(memory_space=pltpu.VMEM)
DMA = pltpu.SemaphoreType.DMA
PI_PARTS = (3.140625, 9.67502593994140625e-4, 1.509957990978376432e-7)
SIN_TERMS = (-1.0 / 39916800, 1.0 / 362880, -1.0 / 5040, 1.0 / 120, -1.0 / 6)
COS_TERMS = (1.0 / 479001600, -1.0 / 3628800, 1.0 / 40320, -1.0 / 720, 1.0 / 24, -0.5)
RANGE = 8192.0
CHUNK = 64
CARRIED = 16


def horner(terms, x):
    total = jnp.full_like(x, terms[0])
    for term in terms[1:]:
        total = total * x + term
    return total


def reduced(angle):
    turns = jnp.round(angle * (1.0 / 3.14159265358979))
    for part in PI_PARTS:
        angle = angle - turns * part
    return angle


def sine(angle, exact_range):
    if not exact_range:
        return jnp.sin(angle)
    rest = reduced(angle)
    square = rest * rest
    return rest + rest * (square * horner(SIN_TERMS, square))


def sine_cosine(angle, exact_range):
    if not exact_range:
        return jnp.sin(angle), jnp.cos(angle)
    rest = reduced(angle)
    square = rest * rest
    return (
        rest + rest * (square * horner(SIN_TERMS, square)),
        1.0 + square * horner(COS_TERMS, square),
    )


def by_range(bound, body):
    @pl.when(bound < RANGE)
    def _():
        body(True)

    @pl.when(bound >= RANGE)
    def _():
        body(False)


def write_snake(stream_ref, alpha, out_ref):
    inverse = 1.0 / alpha
    bound = jnp.max(jnp.abs(stream_ref[...])) * jnp.max(alpha)

    def body(exact_range):
        @pl.loop(0, stream_ref.shape[0] // CHUNK)
        def _(step):
            rows = pl.ds(pl.multiple_of(step * CHUNK, CHUNK), CHUNK)
            stream = stream_ref[rows, :]
            wave = sine(alpha * stream, exact_range)
            out_ref[rows, :] = (stream + wave * wave * inverse).astype(BF16)

    by_range(bound, body)


def moved(values, offset):
    if offset == 0:
        return values
    rows = values.shape[0]
    place = lax.broadcasted_iota(jnp.int32, values.shape, 0)
    turned = pltpu.roll(values, (-offset) % rows, 0)
    inside = place < rows - offset if offset > 0 else place >= -offset
    return jnp.where(inside, turned, 0.0)


def write_shifts(values_ref, out_ref, dilation):
    width = values_ref.shape[1]
    values = values_ref[...].astype(F32)
    for tap in range(3):
        out_ref[:, tap * width : (tap + 1) * width] = moved(values, (tap - 1) * dilation).astype(BF16)


def chan_begin(side, half):
    chan = lax.axis_index("chan")
    return pl.multiple_of((chan if side == 0 else 1 - chan) * half, half)


def load_weights(layer, weight_hbm, weight_ref, sems):
    half = weight_hbm.shape[3]
    loads = []
    for side in range(2):
        for tap in range(3):
            source = weight_hbm.at[layer, tap, pl.ds(chan_begin(side, half), half), :]
            target = weight_ref.at[side, pl.ds(tap * half, half), :]
            loads.append(pltpu.make_async_copy(source, target, sems.at[len(loads)]))
    for copy in loads:
        copy.start()
    return loads


def prep_kernel(
    len_hbm, own_hbm, start_hbm, act_hbm, cot_hbm, alpha_hbm, weight_hbm,
    stream_ref, snake_ref, grad_ref, live_ref, alpha_ref, weight_ref,
    len_ref, own_ref, start_ref, act_ref, cot_ref, sems, weight_sems,
):
    pairs = (
        (len_hbm, len_ref), (own_hbm, own_ref), (start_hbm, start_ref),
        (alpha_hbm, alpha_ref), (act_hbm, act_ref), (cot_hbm, cot_ref),
    )
    copies = [pltpu.make_async_copy(a, b, sems.at[i]) for i, (a, b) in enumerate(pairs)]
    for copy in copies:
        copy.start()
    loads = load_weights(0, weight_hbm, weight_ref, weight_sems)
    replicas = lax.axis_size("replica")
    device = lax.axis_index("dp") * replicas + lax.axis_index("replica")
    rows, width = act_ref.shape
    place = lax.broadcasted_iota(jnp.int32, (rows, 128), 0)
    live_ref[...] = jnp.zeros((rows, 128), F32)
    for copy in copies[:3]:
        copy.wait()

    @pl.loop(0, len_ref.shape[0])
    def _(clip):
        @pl.when(own_ref[clip] == device)
        def _():
            first = start_ref[clip]
            inside = (place >= first) & (place < first + len_ref[clip])
            live_ref[...] = jnp.where(inside, 1.0, live_ref[...])

    live = jnp.tile(live_ref[...], (1, width // 128))
    for copy in copies[3:5]:
        copy.wait()
    stream_ref[...] = act_ref[...].astype(F32) * live
    write_snake(stream_ref, alpha_ref[0:1, :], snake_ref)
    copies[5].wait()
    grad_ref[...] = (cot_ref[...].astype(F32) * live).astype(BF16)
    for copy in loads:
        copy.wait()


def forward_own_kernel(layer, load, snake_ref, weight_ref, *rest):
    if load is None:
        out_ref, shifts_ref = rest
        loads = []
    else:
        weight_hbm, out_ref, loaded_ref, shifts_ref, sems = rest
        loads = load_weights(load, weight_hbm, loaded_ref, sems)
    write_shifts(snake_ref, shifts_ref, dilations[layer])
    out_ref[...] = jnp.dot(shifts_ref[...], weight_ref[0], preferred_element_type=F32)
    for copy in loads:
        copy.wait()


def forward_partner_kernel(layer, last, load, snake_ref, weight_ref, own_ref, old_ref, live_ref, *rest):
    rest = list(rest)
    alpha_ref = None if last else rest.pop(0)
    weight_hbm = None if load is None else rest.pop(0)
    result_ref = rest.pop(0)
    next_ref = None if last else rest.pop(0)
    loads = []
    if load is not None:
        loaded_ref, shifts_ref, sems = rest
        loads = load_weights(load, weight_hbm, loaded_ref, sems)
    else:
        (shifts_ref,) = rest
    write_shifts(snake_ref, shifts_ref, dilations[layer])
    part = jnp.dot(shifts_ref[...], weight_ref[1], preferred_element_type=F32)
    live = jnp.tile(live_ref[...], (1, old_ref.shape[1] // 128))
    new = (old_ref[...] + (own_ref[...] + part)) * live
    result_ref[...] = new.astype(result_ref.dtype)
    if not last:
        write_snake(result_ref, alpha_ref[layer + 1 : layer + 2, :], next_ref)
    for copy in loads:
        copy.wait()


def back_product(shifted_ref, weight_ref, side):
    half = weight_ref.shape[2]
    total = None
    for tap in range(3):
        span = slice(tap * half, (tap + 1) * half)
        part = lax.dot_general(
            shifted_ref[:, span], weight_ref[side, span, :], (((1,), (1,)), ((), ())),
            preferred_element_type=F32,
        )
        total = part if total is None else total + part
    return total


def back_partner_kernel(layer, grad_ref, weight_ref, shifted_ref, out_ref):
    write_shifts(grad_ref, shifted_ref, -dilations[layer])
    out_ref[...] = back_product(shifted_ref, weight_ref, 1).astype(BF16)


def back_own_kernel(shifted_ref, weight_ref, out_ref):
    out_ref[...] = back_product(shifted_ref, weight_ref, 0)


def combine_kernel(layer, own_ref, partner_ref, stream_ref, alphas_ref, *rest):
    if layer == 0:
        (alpha_grad_ref,) = rest
    elif len(rest) == 5:
        old_ref, live_ref, alpha_grad_ref, grad_ref, rounded_ref = rest
    else:
        old_ref, live_ref, alpha_grad_ref, rounded_ref = rest
        grad_ref = None
    alpha = alphas_ref[layer : layer + 1, :]
    inverse = 1.0 / alpha
    bound = jnp.max(jnp.abs(stream_ref[...])) * jnp.max(alpha)
    width = stream_ref.shape[1]

    def body(exact_range):
        def step_body(step, total):
            rows = pl.ds(pl.multiple_of(step * CHUNK, CHUNK), CHUNK)
            stream = stream_ref[rows, :]
            back = own_ref[rows, :] + partner_ref[rows, :].astype(F32)
            sin, cos = sine_cosine(alpha * stream, exact_range)
            double = 2.0 * sin * cos
            ratio = sin * inverse
            term = back * (stream * double * inverse - ratio * ratio)
            if layer > 0:
                live = jnp.tile(live_ref[rows, :], (1, width // 128))
                grad = (old_ref[rows, :].astype(F32) + back * (1.0 + double)) * live
                if grad_ref is not None:
                    grad_ref[rows, :] = grad
                rounded_ref[rows, :] = grad.astype(BF16)
            return total + jnp.sum(term.reshape(CHUNK // 8, 8, width), axis=0)

        total = lax.fori_loop(0, stream_ref.shape[0] // CHUNK, step_body, jnp.zeros((8, width), F32))
        alpha_grad_ref[...] = jnp.sum(total, axis=0, keepdims=True)

    by_range(bound, body)


def block_place(pieces, slice_index, part):
    apart = jnp.bitwise_xor(slice_index, lax.axis_index("dp"))
    order = (2 * pieces, 0, 2 * pieces + 1, 1)
    return 2 * part + jnp.where(
        apart == 0, order[0], jnp.where(apart == 1, order[1], jnp.where(apart == 2, order[2], order[3]))
    )


def weight_kernel(own_ref, partner_ref, shifted_ref, out_ref, turned_ref):
    half = own_ref.shape[1]
    chan = lax.axis_index("chan")
    for ref, side in ((own_ref, chan), (partner_ref, 1 - chan)):
        turned_ref[pl.ds(pl.multiple_of(side * half, half), half), :] = ref[...].T
    for tap in range(3):
        span = slice(tap * half, (tap + 1) * half)
        out_ref[:, span] = jnp.dot(turned_ref[...], shifted_ref[:, span], preferred_element_type=F32).astype(BF16)


def place_rows(pieces, rows_of, side, target_ref, columns):
    size = rows_of.shape[0] // (2 * pieces)
    for local in range(2):
        for part in range(pieces):
            begin = pl.multiple_of(block_place(pieces, side * 2 + local, part) * size, size)
            low = (local * pieces + part) * size
            target_ref[pl.ds(begin, size), columns] = rows_of[low : low + size, :]


def pick_parts(turned_ref, part, size):
    begin = pl.multiple_of(part * size, size)
    return [turned_ref[pl.ds(local * 2 * size + begin, size), :] for local in range(2)]


def turn_kernel(*refs):
    snakes, out_ref, turned_ref = refs[:-2], refs[-2], refs[-1]
    size = snakes[0].shape[1] // 4
    for index, ref in enumerate(snakes):
        turned_ref[...] = ref[...].T
        for local, piece in enumerate(pick_parts(turned_ref, 1 - lax.axis_index("replica"), size)):
            low = (2 * index + local) * size
            out_ref[low : low + size, :] = piece


def own_rows_kernel(pieces, own_ref, partner_ref, out_ref, half_ref):
    chan = lax.axis_index("chan")
    mine = lax.axis_index("replica")
    for ref, side in ((own_ref, chan), (partner_ref, 1 - chan)):
        half_ref[...] = ref[...].T
        both = jnp.concatenate(pick_parts(half_ref, mine, ref.shape[1] // 4), 0)
        place_rows(pieces, both, side, out_ref, slice(None))


def far_kernel(layer, grad_ref, out_ref):
    write_shifts(grad_ref, out_ref, -dilations[layer])


def write_carried(values, out_ref, low):
    first = values.astype(BF16).astype(F32)
    second = (values - first).astype(BF16).astype(F32)
    third = values - first - second
    shape = (CARRIED, values.shape[1])
    row = lax.broadcasted_iota(jnp.int32, shape, 0)
    block = jnp.where(row == 0, first, jnp.where(row == 1, second, jnp.where(row == 2, third, 0.0)))
    out_ref[low : low + CARRIED, :] = block.astype(BF16)


def read_carried(ref, low):
    block = ref[low : low + CARRIED, :].astype(F32)
    return (block[0:1, :] + block[1:2, :]) + block[2:3, :]


def paired_weight_kernel(pieces, low, carry, own_ref, shifted_ref, across_ref, across_other_ref, far_ref, *rest):
    if carry:
        write_carried(jnp.concatenate([ref[...] for ref in rest[:carry]], 1), rest[carry], own_ref.shape[0] // 2)
        rest = rest[carry:]
    outs, turned_ref = rest[:-1], rest[-1]
    half = own_ref.shape[0]
    chan = lax.axis_index("chan")
    for ref, side in ((across_ref, chan), (across_other_ref, 1 - chan)):
        place_rows(pieces, ref[low : low + half // 2, :], side, turned_ref, slice(None))
    for tap in range(3):
        span = slice(tap * half, (tap + 1) * half)
        product = jnp.dot(own_ref[...], shifted_ref[:, span], preferred_element_type=F32)
        product += jnp.dot(turned_ref[...], far_ref[:, span], preferred_element_type=F32)
        product = product.astype(BF16)
        size = product.shape[0] // len(outs)
        for place, ref in enumerate(outs):
            ref[0:size, span] = product[place * size : (place + 1) * size, :]


def finish_kernel(paired, held, carry, counts, *refs):
    total_ref, sems = refs[-2:]
    refs = list(refs[1:-2] if held else refs[:-2])
    if carry:
        alpha_ref = refs.pop()
        alpha_mine = refs.pop(0)
    out_ref = refs.pop()
    half = total_ref.shape[3]
    rows_of = total_ref.shape[2] // (2 if paired else 1)
    copies = []
    for index, (layer, pieces) in enumerate(counts):
        for part in range(pieces):
            mine_ref, other_ref = refs.pop(0), refs.pop(0)
            size = rows_of
            if carry and other_ref.shape[0] > size:
                alpha = alpha_mine[...] + read_carried(other_ref, size)
                for place in range(3):
                    alpha_ref[place : place + 1, :] = alpha[:, place * half : (place + 1) * half]
            for tap in range(3):
                span = slice(tap * half, (tap + 1) * half)
                mine, other = mine_ref[0:size, span].astype(F32), other_ref[0:size, span].astype(F32)
                if paired:
                    begin = lax.axis_index("replica") * (size * pieces)
                    for values, start in ((mine, begin), (other, size * pieces - begin)):
                        place = pl.multiple_of(start + part * size, size)
                        total_ref[index, tap, pl.ds(place, size), :] = values
                else:
                    total_ref[index, tap] = mine + other
        copies.append(pltpu.make_async_copy(total_ref.at[index], out_ref.at[layer], sems.at[index]))
        copies[-1].start()
    for copy in copies:
        copy.wait()


def fold_kernel(carry, keep, got, *rest):
    if carry:
        mine, rest = rest[:carry], rest[carry:]
        send, sum_ref = rest
    else:
        (send,) = rest
    rows = keep.shape[0] // 2
    send[0:rows, :] = (keep[rows:, :].astype(F32) + got[rows : 2 * rows, :].astype(F32)).astype(BF16)
    if carry:
        values = jnp.concatenate([ref[...] for ref in mine], 1) + read_carried(got, 2 * rows)
        sum_ref[...] = values
        write_carried(values, send, rows)


def total_kernel(carry, keep, got, late, *rest):
    if carry:
        mine, out_ref, sum_ref = rest
    else:
        (out_ref,) = rest
    rows = keep.shape[0] // 2
    total = keep[0:rows, :].astype(F32) + got[0:rows, :].astype(F32) + late[0:rows, :].astype(F32)
    out_ref[0:rows, :] = total.astype(BF16)
    if carry:
        values = mine[...] + read_carried(late, rows)
        sum_ref[...] = values
        write_carried(values, out_ref, rows)


def stack_kernel(*refs):
    for index, ref in enumerate(refs[:-1]):
        refs[-1][index : index + 1, :] = ref[...]


def add_kernel(left, right, out_ref):
    out_ref[...] = left[...] + right[...]


def struct(shape, dtype):
    return jax.ShapeDtypeStruct(shape, dtype)


def after(value, other):
    return value if other is None else lax.optimization_barrier((value, other))[0]


class Sequence:
    def __init__(self):
        self.latest = None
        self.weight = 10

    def hold(self, value):
        return after(value, self.latest)

    def call(self, kernel, name, ins, outs, scratch, flops, *args, specs=None, aliases=None):
        single = not isinstance(outs, list)
        size = sum(a.size * a.dtype.itemsize for a in args if a.size < 2000000)
        size += sum(math.prod(o.shape) * o.dtype.itemsize for o in ([outs] if single else outs))
        args = [pltpu.with_memory_space_constraint(a, pltpu.HBM) if i == 1 else a for i, a in zip(ins, args)]
        if self.latest is not None:
            held = ins.index(0)
            args[held] = self.hold(args[held])
        result = pl.pallas_call(
            kernel,
            in_specs=[ANY_HBM if i else IN_VMEM for i in ins],
            out_specs=specs or (IN_VMEM if single else [IN_VMEM] * len(outs)),
            out_shape=outs,
            scratch_shapes=scratch,
            input_output_aliases=aliases or {},
            compiler_params=pltpu.CompilerParams(vmem_limit_bytes=24 * 1024 * 1024),
            cost_estimate=pl.CostEstimate(flops=int(flops * self.weight), bytes_accessed=int(size * self.weight), transcendentals=0),
            name=name,
        )(*args)
        self.latest = result if single else result[-1]
        return result


def swap(x, axis, other):
    return lax.ppermute(x, axis, [(i, other(i)) for i in range(lax.axis_size(axis))])


def across_chan(x):
    return swap(x, "chan", lambda i: i ^ 1)


def across_replica(x):
    return swap(x, "replica", lambda i: i ^ 1)


def on_device(activations, cotangent, conv_weights, snake_alpha, seg_lengths, seg_owner, seg_start):
    rows, half = activations.shape
    layers, taps, channels, _ = conv_weights.shape
    top = layers - 1
    fast = lax.axis_size("dp") == 4 and lax.axis_size("replica") == 2
    counts = [1] * layers
    carrier = 1 if fast else None
    weight = {}
    tile, triple = (rows, half), (rows, taps * half)
    flops = 2 * rows * half * half * taps
    sequence = Sequence()
    streams, mine, partners, owns = [], [], {}, {}
    rounded, shifted, arrived, back_owns, far = {}, {}, {}, {}, {}
    across, across_other = {}, {}
    alpha_parts = [None] * layers
    kept, got, late, summed, crossed = {}, {}, {}, {}, {}

    loaded = (2, taps * half, half)
    sems = DMA((2 * taps,))

    def forward_own(layer, load=None):
        outs, args, ins = struct(tile, F32), [mine[layer], weight[layer]], [0, 0]
        scratch = [pltpu.VMEM(triple, BF16)]
        if load is not None:
            outs, args, ins = [outs, struct(loaded, BF16)], args + [conv_weights], ins + [1]
            scratch.append(sems)
        result = sequence.call(
            functools.partial(forward_own_kernel, layer, load), "forward_own", ins, outs, scratch, flops, *args
        )
        if load is None:
            owns[layer] = result
        else:
            owns[layer], weight[load] = result

    def forward_partner(layer, load=None):
        last = layer == top
        ins, args = [0] * 5, [partners[layer], weight[layer], owns[layer], streams[layer], live]
        outs = [struct(tile, BF16)] if last else [struct(tile, F32), struct(tile, BF16)]
        scratch = [pltpu.VMEM(triple, BF16)]
        if not last:
            ins, args = ins + [0], args + [alphas]
        if load is not None:
            ins, args, outs = ins + [1], args + [conv_weights], outs + [struct(loaded, BF16)]
            scratch.append(sems)
        result = sequence.call(
            functools.partial(forward_partner_kernel, layer, last, load), "forward_partner", ins, outs, scratch,
            flops, *args,
        )
        if load is not None:
            weight[load] = result[-1]
        if last:
            return result[0]
        streams.append(result[0])
        mine.append(result[1])
        partners[layer + 1] = across_chan(result[1])

    def back_partner(layer):
        shifted[layer], part = sequence.call(
            functools.partial(back_partner_kernel, layer), "back_partner", [0, 0],
            [struct(triple, BF16), struct(tile, BF16)], [], flops, rounded[layer + 1], weight[layer],
        )
        arrived[layer] = across_chan(part)

    def back_own(layer):
        back_owns[layer] = sequence.call(
            back_own_kernel, "back_own", [0, 0], struct(tile, F32), [], flops, shifted[layer], weight[layer]
        )

    def send_gradient(layer):
        if fast:
            far[layer] = across_replica(sequence.hold(rounded[layer + 1]))

    def combine(layer, grad):
        args = [back_owns[layer], arrived[layer], streams[layer], alphas]
        outs = [struct((1, half), F32)]
        if layer > 0:
            args += [grad, live]
            outs += [struct(tile, F32)] * (layer > 1) + [struct(tile, BF16)]
        result = sequence.call(
            functools.partial(combine_kernel, layer), "combine", [0] * len(args), outs, [], 60 * rows * half, *args
        )
        alpha_parts[layer] = result[0]
        if layer > 0:
            rounded[layer] = result[-1]
            return result[1]

    def turn(*chosen):
        if fast:
            moved_rows = across_replica(sequence.call(
                turn_kernel, "turn", [0] * len(chosen), struct((len(chosen) * half // 2, rows), BF16),
                [pltpu.VMEM((half, rows), BF16)], 10 * rows * half, *[mine[layer] for layer in chosen],
            ))
            for index, layer in enumerate(chosen):
                across[layer] = (moved_rows, index * half // 2)

    def share(*chosen):
        if fast:
            shared = across_chan(sequence.hold(across[chosen[0]][0]))
            for layer in chosen:
                across_other[layer] = shared

    own_turned, far_shifted = {}, {}

    def own_rows(layer):
        if fast:
            own_turned[layer] = sequence.call(
                functools.partial(own_rows_kernel, counts[layer]), "own_rows", [0, 0], struct((half, rows), BF16),
                [pltpu.VMEM((half, rows), BF16)], 10 * rows * half, mine[layer], partners[layer],
            )

    def far_rows(layer):
        if fast:
            far_shifted[layer] = sequence.call(
                functools.partial(far_kernel, layer), "far_rows", [0], struct(triple, BF16), [],
                10 * rows * half, far[layer],
            )

    def weights(layer):
        if not fast:
            out = sequence.call(
                weight_kernel, "weight", [0] * 3, struct((channels, taps * half), BF16),
                [pltpu.VMEM((channels, rows), BF16)], 2 * flops, mine[layer], partners[layer], shifted[layer],
            )
            part = lax.psum_scatter(out, "dp", scatter_dimension=0, tiled=True)
            summed[layer, 0] = lax.psum(part, "replica")
            crossed[layer, 0] = jnp.zeros_like(part)
            return
        pieces, depth = counts[layer], channels // 4 // counts[layer]
        carried = alpha_parts if layer == carrier else []
        outs = [struct((depth, taps * half), BF16)] * (2 * pieces)
        if carried:
            outs[0] = struct((depth + CARRIED, taps * half), BF16)
        args = [own_turned[layer], shifted[layer], across[layer][0], across_other[layer], far_shifted[layer], *carried]
        out = sequence.call(
            functools.partial(paired_weight_kernel, pieces, across[layer][1], len(carried)), "paired_weight",
            [0] * len(args), outs, [pltpu.VMEM((half, rows), BF16)], 2 * flops, *args,
        )
        for part in range(pieces):
            got[layer, part] = swap(out[part], "dp", lambda i: i ^ 1)
            kept[layer, part] = out[pieces + part]

    carry_sum = [None]

    def fold(layer, part=0):
        if not fast:
            return
        keep, came = kept[layer, part], got[layer, part]
        depth, carried = keep.shape[0] // 2, alpha_parts if layer == carrier else []
        outs = [struct((depth + CARRIED * bool(carried), taps * half), BF16)]
        if carried:
            outs.append(struct((1, taps * half), F32))
        result = sequence.call(
            functools.partial(fold_kernel, len(carried)), "fold", [0] * (2 + len(carried)), outs, [], keep.size,
            keep, came, *carried,
        )
        if carried:
            carry_sum[0] = result[1]
        late[layer, part] = swap(result[0], "dp", lambda i: i ^ 2)

    def total(layer, part=0):
        if not fast:
            return
        keep, came, last = kept[layer, part], got[layer, part], late[layer, part]
        outs, args = [struct(last.shape, BF16)], [keep, came, last]
        if layer == carrier:
            outs.append(struct((1, taps * half), F32))
            args.append(carry_sum[0])
        result = sequence.call(
            functools.partial(total_kernel, layer == carrier), "total", [0] * len(args), outs, [], 2 * flops, *args
        )
        if layer == carrier:
            carry_sum[0] = result[1]
        summed[layer, part] = result[0]

    def cross(layer, part=0):
        if fast:
            crossed[layer, part] = across_replica(sequence.hold(summed[layer, part]))

    stream, snaked, grad, live, alphas, weight[0] = sequence.call(
        prep_kernel, "prep", [1] * 7,
        [struct(tile, F32), struct(tile, BF16), struct(tile, BF16), struct((rows, 128), F32),
         struct(snake_alpha.shape, F32), struct(loaded, BF16)],
        [pltpu.SMEM(seg_lengths.shape, jnp.int32)] * 3 + [pltpu.VMEM(tile, BF16)] * 2 + [DMA((6,)), sems],
        40 * rows * half,
        seg_lengths, seg_owner, seg_start, activations, cotangent, snake_alpha, conv_weights,
    )
    streams.append(stream)
    mine.append(snaked)
    partners[0] = across_chan(snaked)
    rounded[layers] = grad
    depth = channels // lax.axis_size("dp")

    def finish(chosen, before=None):
        pairs = [] if before is None else [before]
        carry = carrier in chosen
        if carry:
            pairs.append(carry_sum[0])
        for layer in chosen:
            for part in range(counts[layer]):
                pairs += [summed[layer, part], crossed[layer, part]]
        out = struct((layers, taps, depth, half), F32)
        return sequence.call(
            functools.partial(
                finish_kernel, fast, before is not None, carry, tuple((layer, counts[layer]) for layer in chosen)
            ),
            "finish", [2] * (before is not None) + [0] * (len(pairs) - (before is not None)),
            [out, struct((layers, half), F32)] if carry else [out],
            [pltpu.VMEM((len(chosen), taps, depth, half), F32), DMA((len(chosen),))],
            layers * taps * depth * half, *pairs, specs=[ANY_HBM] + [IN_VMEM] * carry,
            aliases={0: 0} if before is not None else None,
        )

    rounds = [("replica", 1 << bit) for bit in range(8) if lax.axis_size("replica") >> (bit + 1)]
    rounds += [("dp", 1 << bit) for bit in range(8) if lax.axis_size("dp") >> (bit + 1)]
    arrivals = []

    def alpha_round():
        if arrivals:
            value = sequence.call(
                add_kernel, "add", [0, 0], struct((layers, half), F32), [], layers * half, *arrivals.pop()
            )
        else:
            value = sequence.call(
                stack_kernel, "stack", [0] * layers, struct((layers, half), F32), [], layers * half, *alpha_parts
            )
        if not rounds:
            return value
        axis, apart = rounds.pop(0)
        arrivals.append((value, swap(value, axis, lambda place: place ^ apart)))

    forward_own(0, load=2)
    send_gradient(2)
    forward_partner(0, load=1)
    back_partner(2)
    forward_own(1)
    forward_partner(1)
    turn(2)
    back_own(2)
    grad = combine(2, grad)
    send_gradient(1)
    far_rows(2)
    own_rows(2)
    turn(1, 0)
    back_partner(1)
    share(2)
    back_own(1)
    combine(1, grad)
    back_partner(0)
    back_own(0)
    weights(2)
    sequence.weight = 10
    combine(0, None)
    own_rows(1)
    own_rows(0)
    forward_own(2)
    far_rows(1)
    share(1, 0)
    send_gradient(0)
    sequence.weight = 0.01
    residual_out = forward_partner(2)
    fold(2)
    weights(1)
    sequence.weight = 0.01
    far_rows(0)
    weights(0)
    total(2)
    cross(2)
    sequence.weight = 10
    fold(1)
    fold(0)
    total(1)
    cross(1)
    total(0)
    cross(0)
    if fast:
        weight_grads, alpha_grads = finish((2, 1))
        (weight_grads,) = finish((0,), weight_grads)
    else:
        alpha_grads = alpha_round()
        while alpha_grads is None:
            alpha_grads = alpha_round()
        (weight_grads,) = finish((2, 1, 0))
    return (residual_out, weight_grads, alpha_grads)


def solution(mesh):
    return jax.shard_map(
        on_device,
        mesh=mesh,
        in_specs=(
            P(("groups", "dp", "replica"), "chan"),
            P(("groups", "dp", "replica"), "chan"),
            P(None, None, None, "chan"),
            P(None, "chan"),
            P("groups"),
            P("groups"),
            P("groups"),
        ),
        out_specs=(
            P(("groups", "dp", "replica"), "chan"),
            P("groups", None, "dp", "chan"),
            P("groups", "chan"),
        ),
        check_vma=False,
    )
```

```python
import functools
import math

import jax
import jax.numpy as jnp
from jax import lax
from jax.experimental import pallas as pl
from jax.experimental.pallas import tpu as pltpu
from jax.sharding import PartitionSpec as P

dilations = (1, 3, 5)
F32, BF16 = jnp.float32, jnp.bfloat16
ANY_HBM = pl.BlockSpec(memory_space=pltpu.HBM)
IN_VMEM = pl.BlockSpec(memory_space=pltpu.VMEM)
DMA = pltpu.SemaphoreType.DMA
PI_PARTS = (3.140625, 9.67502593994140625e-4, 1.509957990978376432e-7)
SIN_TERMS = (-1.0 / 39916800, 1.0 / 362880, -1.0 / 5040, 1.0 / 120, -1.0 / 6)
COS_TERMS = (1.0 / 479001600, -1.0 / 3628800, 1.0 / 40320, -1.0 / 720, 1.0 / 24, -0.5)
RANGE = 8192.0
CHUNK = 64
CARRIED = 16


def horner(terms, x):
    total = jnp.full_like(x, terms[0])
    for term in terms[1:]:
        total = total * x + term
    return total


def reduced(angle):
    turns = jnp.round(angle * (1.0 / 3.14159265358979))
    for part in PI_PARTS:
        angle = angle - turns * part
    return angle


def sine(angle, exact_range):
    if not exact_range:
        return jnp.sin(angle)
    rest = reduced(angle)
    square = rest * rest
    return rest + rest * (square * horner(SIN_TERMS, square))


def sine_cosine(angle, exact_range):
    if not exact_range:
        return jnp.sin(angle), jnp.cos(angle)
    rest = reduced(angle)
    square = rest * rest
    return (
        rest + rest * (square * horner(SIN_TERMS, square)),
        1.0 + square * horner(COS_TERMS, square),
    )


def by_range(bound, body):
    @pl.when(bound < RANGE)
    def _():
        body(True)

    @pl.when(bound >= RANGE)
    def _():
        body(False)


def write_snake(stream_ref, alpha, out_ref):
    inverse = 1.0 / alpha
    bound = jnp.max(jnp.abs(stream_ref[...])) * jnp.max(alpha)

    def body(exact_range):
        @pl.loop(0, stream_ref.shape[0] // CHUNK)
        def _(step):
            rows = pl.ds(pl.multiple_of(step * CHUNK, CHUNK), CHUNK)
            stream = stream_ref[rows, :]
            wave = sine(alpha * stream, exact_range)
            out_ref[rows, :] = (stream + wave * wave * inverse).astype(BF16)

    by_range(bound, body)


def moved(values, offset):
    if offset == 0:
        return values
    rows = values.shape[0]
    place = lax.broadcasted_iota(jnp.int32, values.shape, 0)
    turned = pltpu.roll(values, (-offset) % rows, 0)
    inside = place < rows - offset if offset > 0 else place >= -offset
    return jnp.where(inside, turned, 0.0)


def write_shifts(values_ref, out_ref, dilation):
    width = values_ref.shape[1]
    values = values_ref[...].astype(F32)
    for tap in range(3):
        out_ref[:, tap * width : (tap + 1) * width] = moved(values, (tap - 1) * dilation).astype(BF16)


def chan_begin(side, half):
    chan = lax.axis_index("chan")
    return pl.multiple_of((chan if side == 0 else 1 - chan) * half, half)


def load_weights(layer, weight_hbm, weight_ref, sems):
    half = weight_hbm.shape[3]
    loads = []
    for side in range(2):
        for tap in range(3):
            source = weight_hbm.at[layer, tap, pl.ds(chan_begin(side, half), half), :]
            target = weight_ref.at[side, pl.ds(tap * half, half), :]
            loads.append(pltpu.make_async_copy(source, target, sems.at[len(loads)]))
    for copy in loads:
        copy.start()
    return loads


def prep_kernel(
    len_hbm, own_hbm, start_hbm, act_hbm, cot_hbm, alpha_hbm, weight_hbm,
    stream_ref, snake_ref, grad_ref, live_ref, alpha_ref, weight_ref,
    len_ref, own_ref, start_ref, act_ref, cot_ref, sems, weight_sems,
):
    pairs = (
        (len_hbm, len_ref), (own_hbm, own_ref), (start_hbm, start_ref),
        (alpha_hbm, alpha_ref), (act_hbm, act_ref), (cot_hbm, cot_ref),
    )
    copies = [pltpu.make_async_copy(a, b, sems.at[i]) for i, (a, b) in enumerate(pairs)]
    for copy in copies:
        copy.start()
    loads = load_weights(0, weight_hbm, weight_ref, weight_sems)
    replicas = lax.axis_size("replica")
    device = lax.axis_index("dp") * replicas + lax.axis_index("replica")
    rows, width = act_ref.shape
    place = lax.broadcasted_iota(jnp.int32, (rows, 128), 0)
    live_ref[...] = jnp.zeros((rows, 128), F32)
    for copy in copies[:3]:
        copy.wait()

    @pl.loop(0, len_ref.shape[0])
    def _(clip):
        @pl.when(own_ref[clip] == device)
        def _():
            first = start_ref[clip]
            inside = (place >= first) & (place < first + len_ref[clip])
            live_ref[...] = jnp.where(inside, 1.0, live_ref[...])

    live = jnp.tile(live_ref[...], (1, width // 128))
    for copy in copies[3:5]:
        copy.wait()
    stream_ref[...] = act_ref[...].astype(F32) * live
    write_snake(stream_ref, alpha_ref[0:1, :], snake_ref)
    copies[5].wait()
    grad_ref[...] = (cot_ref[...].astype(F32) * live).astype(BF16)
    for copy in loads:
        copy.wait()


def forward_own_kernel(layer, load, snake_ref, weight_ref, *rest):
    if load is None:
        out_ref, shifts_ref = rest
        loads = []
    else:
        weight_hbm, out_ref, loaded_ref, shifts_ref, sems = rest
        loads = load_weights(load, weight_hbm, loaded_ref, sems)
    write_shifts(snake_ref, shifts_ref, dilations[layer])
    out_ref[...] = jnp.dot(shifts_ref[...], weight_ref[0], preferred_element_type=F32)
    for copy in loads:
        copy.wait()


def forward_partner_kernel(layer, last, load, snake_ref, weight_ref, own_ref, old_ref, live_ref, *rest):
    rest = list(rest)
    alpha_ref = None if last else rest.pop(0)
    weight_hbm = None if load is None else rest.pop(0)
    result_ref = rest.pop(0)
    next_ref = None if last else rest.pop(0)
    loads = []
    if load is not None:
        loaded_ref, shifts_ref, sems = rest
        loads = load_weights(load, weight_hbm, loaded_ref, sems)
    else:
        (shifts_ref,) = rest
    write_shifts(snake_ref, shifts_ref, dilations[layer])
    part = jnp.dot(shifts_ref[...], weight_ref[1], preferred_element_type=F32)
    live = jnp.tile(live_ref[...], (1, old_ref.shape[1] // 128))
    new = (old_ref[...] + (own_ref[...] + part)) * live
    result_ref[...] = new.astype(result_ref.dtype)
    if not last:
        write_snake(result_ref, alpha_ref[layer + 1 : layer + 2, :], next_ref)
    for copy in loads:
        copy.wait()


def back_product(shifted_ref, weight_ref, side):
    half = weight_ref.shape[2]
    total = None
    for tap in range(3):
        span = slice(tap * half, (tap + 1) * half)
        part = lax.dot_general(
            shifted_ref[:, span], weight_ref[side, span, :], (((1,), (1,)), ((), ())),
            preferred_element_type=F32,
        )
        total = part if total is None else total + part
    return total


def back_partner_kernel(layer, grad_ref, weight_ref, shifted_ref, out_ref):
    write_shifts(grad_ref, shifted_ref, -dilations[layer])
    out_ref[...] = back_product(shifted_ref, weight_ref, 1).astype(BF16)


def back_own_kernel(shifted_ref, weight_ref, out_ref):
    out_ref[...] = back_product(shifted_ref, weight_ref, 0)


def combine_kernel(layer, own_ref, partner_ref, stream_ref, alphas_ref, *rest):
    if layer == 0:
        (alpha_grad_ref,) = rest
    elif len(rest) == 5:
        old_ref, live_ref, alpha_grad_ref, grad_ref, rounded_ref = rest
    else:
        old_ref, live_ref, alpha_grad_ref, rounded_ref = rest
        grad_ref = None
    alpha = alphas_ref[layer : layer + 1, :]
    inverse = 1.0 / alpha
    bound = jnp.max(jnp.abs(stream_ref[...])) * jnp.max(alpha)
    width = stream_ref.shape[1]

    def body(exact_range):
        def step_body(step, total):
            rows = pl.ds(pl.multiple_of(step * CHUNK, CHUNK), CHUNK)
            stream = stream_ref[rows, :]
            back = own_ref[rows, :] + partner_ref[rows, :].astype(F32)
            sin, cos = sine_cosine(alpha * stream, exact_range)
            double = 2.0 * sin * cos
            ratio = sin * inverse
            term = back * (stream * double * inverse - ratio * ratio)
            if layer > 0:
                live = jnp.tile(live_ref[rows, :], (1, width // 128))
                grad = (old_ref[rows, :].astype(F32) + back * (1.0 + double)) * live
                if grad_ref is not None:
                    grad_ref[rows, :] = grad
                rounded_ref[rows, :] = grad.astype(BF16)
            return total + jnp.sum(term.reshape(CHUNK // 8, 8, width), axis=0)

        total = lax.fori_loop(0, stream_ref.shape[0] // CHUNK, step_body, jnp.zeros((8, width), F32))
        alpha_grad_ref[...] = jnp.sum(total, axis=0, keepdims=True)

    by_range(bound, body)


def block_place(pieces, slice_index, part):
    apart = jnp.bitwise_xor(slice_index, lax.axis_index("dp"))
    order = (2 * pieces, 0, 2 * pieces + 1, 1)
    return 2 * part + jnp.where(
        apart == 0, order[0], jnp.where(apart == 1, order[1], jnp.where(apart == 2, order[2], order[3]))
    )


def weight_kernel(own_ref, partner_ref, shifted_ref, out_ref, turned_ref):
    half = own_ref.shape[1]
    chan = lax.axis_index("chan")
    for ref, side in ((own_ref, chan), (partner_ref, 1 - chan)):
        turned_ref[pl.ds(pl.multiple_of(side * half, half), half), :] = ref[...].T
    for tap in range(3):
        span = slice(tap * half, (tap + 1) * half)
        out_ref[:, span] = jnp.dot(turned_ref[...], shifted_ref[:, span], preferred_element_type=F32).astype(BF16)


def place_rows(pieces, rows_of, side, target_ref, columns):
    size = rows_of.shape[0] // (2 * pieces)
    for local in range(2):
        for part in range(pieces):
            begin = pl.multiple_of(block_place(pieces, side * 2 + local, part) * size, size)
            low = (local * pieces + part) * size
            target_ref[pl.ds(begin, size), columns] = rows_of[low : low + size, :]


def pick_parts(turned_ref, part, size):
    begin = pl.multiple_of(part * size, size)
    return [turned_ref[pl.ds(local * 2 * size + begin, size), :] for local in range(2)]


def turn_kernel(*refs):
    snakes, out_ref, turned_ref = refs[:-2], refs[-2], refs[-1]
    size = snakes[0].shape[1] // 4
    for index, ref in enumerate(snakes):
        turned_ref[...] = ref[...].T
        for local, piece in enumerate(pick_parts(turned_ref, 1 - lax.axis_index("replica"), size)):
            low = (2 * index + local) * size
            out_ref[low : low + size, :] = piece


def own_rows_kernel(pieces, own_ref, partner_ref, out_ref, half_ref):
    chan = lax.axis_index("chan")
    mine = lax.axis_index("replica")
    for ref, side in ((own_ref, chan), (partner_ref, 1 - chan)):
        half_ref[...] = ref[...].T
        both = jnp.concatenate(pick_parts(half_ref, mine, ref.shape[1] // 4), 0)
        place_rows(pieces, both, side, out_ref, slice(None))


def far_kernel(layer, grad_ref, out_ref):
    write_shifts(grad_ref, out_ref, -dilations[layer])


def write_carried(values, out_ref, low):
    first = values.astype(BF16).astype(F32)
    second = (values - first).astype(BF16).astype(F32)
    third = values - first - second
    shape = (CARRIED, values.shape[1])
    row = lax.broadcasted_iota(jnp.int32, shape, 0)
    block = jnp.where(row == 0, first, jnp.where(row == 1, second, jnp.where(row == 2, third, 0.0)))
    out_ref[low : low + CARRIED, :] = block.astype(BF16)


def read_carried(ref, low):
    block = ref[low : low + CARRIED, :].astype(F32)
    return (block[0:1, :] + block[1:2, :]) + block[2:3, :]


def paired_weight_kernel(pieces, low, carry, own_ref, shifted_ref, across_ref, across_other_ref, far_ref, *rest):
    if carry:
        write_carried(jnp.concatenate([ref[...] for ref in rest[:carry]], 1), rest[carry], own_ref.shape[0] // 2)
        rest = rest[carry:]
    outs, turned_ref = rest[:-1], rest[-1]
    half = own_ref.shape[0]
    chan = lax.axis_index("chan")
    for ref, side in ((across_ref, chan), (across_other_ref, 1 - chan)):
        place_rows(pieces, ref[low : low + half // 2, :], side, turned_ref, slice(None))
    for tap in range(3):
        span = slice(tap * half, (tap + 1) * half)
        product = jnp.dot(own_ref[...], shifted_ref[:, span], preferred_element_type=F32)
        product += jnp.dot(turned_ref[...], far_ref[:, span], preferred_element_type=F32)
        product = product.astype(BF16)
        size = product.shape[0] // len(outs)
        for place, ref in enumerate(outs):
            ref[0:size, span] = product[place * size : (place + 1) * size, :]


def finish_kernel(paired, held, carry, counts, *refs):
    total_ref, sems = refs[-2:]
    refs = list(refs[1:-2] if held else refs[:-2])
    if carry:
        alpha_ref = refs.pop()
        alpha_mine = refs.pop(0)
    out_ref = refs.pop()
    half = total_ref.shape[3]
    rows_of = total_ref.shape[2] // (2 if paired else 1)
    copies = []
    for index, (layer, pieces) in enumerate(counts):
        for part in range(pieces):
            mine_ref, other_ref = refs.pop(0), refs.pop(0)
            size = rows_of
            if carry and other_ref.shape[0] > size:
                alpha = alpha_mine[...] + read_carried(other_ref, size)
                for place in range(3):
                    alpha_ref[place : place + 1, :] = alpha[:, place * half : (place + 1) * half]
            for tap in range(3):
                span = slice(tap * half, (tap + 1) * half)
                mine, other = mine_ref[0:size, span].astype(F32), other_ref[0:size, span].astype(F32)
                if paired:
                    begin = lax.axis_index("replica") * (size * pieces)
                    for values, start in ((mine, begin), (other, size * pieces - begin)):
                        place = pl.multiple_of(start + part * size, size)
                        total_ref[index, tap, pl.ds(place, size), :] = values
                else:
                    total_ref[index, tap] = mine + other
        copies.append(pltpu.make_async_copy(total_ref.at[index], out_ref.at[layer], sems.at[index]))
        copies[-1].start()
    for copy in copies:
        copy.wait()


def fold_kernel(carry, keep, got, *rest):
    if carry:
        mine, rest = rest[:carry], rest[carry:]
        send, sum_ref = rest
    else:
        (send,) = rest
    rows = keep.shape[0] // 2
    send[0:rows, :] = (keep[rows:, :].astype(F32) + got[rows : 2 * rows, :].astype(F32)).astype(BF16)
    if carry:
        values = jnp.concatenate([ref[...] for ref in mine], 1) + read_carried(got, 2 * rows)
        sum_ref[...] = values
        write_carried(values, send, rows)


def total_kernel(carry, keep, got, late, *rest):
    if carry:
        mine, out_ref, sum_ref = rest
    else:
        (out_ref,) = rest
    rows = keep.shape[0] // 2
    total = keep[0:rows, :].astype(F32) + got[0:rows, :].astype(F32) + late[0:rows, :].astype(F32)
    out_ref[0:rows, :] = total.astype(BF16)
    if carry:
        values = mine[...] + read_carried(late, rows)
        sum_ref[...] = values
        write_carried(values, out_ref, rows)


def stack_kernel(*refs):
    for index, ref in enumerate(refs[:-1]):
        refs[-1][index : index + 1, :] = ref[...]


def add_kernel(left, right, out_ref):
    out_ref[...] = left[...] + right[...]


def struct(shape, dtype):
    return jax.ShapeDtypeStruct(shape, dtype)


def after(value, other):
    return value if other is None else lax.optimization_barrier((value, other))[0]


class Sequence:
    def __init__(self):
        self.latest = None
        self.weight = 10

    def hold(self, value):
        return after(value, self.latest)

    def call(self, kernel, name, ins, outs, scratch, flops, *args, specs=None, aliases=None):
        single = not isinstance(outs, list)
        size = sum(a.size * a.dtype.itemsize for a in args if a.size < 2000000)
        size += sum(math.prod(o.shape) * o.dtype.itemsize for o in ([outs] if single else outs))
        args = [pltpu.with_memory_space_constraint(a, pltpu.HBM) if i == 1 else a for i, a in zip(ins, args)]
        if self.latest is not None:
            held = ins.index(0)
            args[held] = self.hold(args[held])
        result = pl.pallas_call(
            kernel,
            in_specs=[ANY_HBM if i else IN_VMEM for i in ins],
            out_specs=specs or (IN_VMEM if single else [IN_VMEM] * len(outs)),
            out_shape=outs,
            scratch_shapes=scratch,
            input_output_aliases=aliases or {},
            compiler_params=pltpu.CompilerParams(vmem_limit_bytes=24 * 1024 * 1024),
            cost_estimate=pl.CostEstimate(flops=int(flops * self.weight), bytes_accessed=int(size * self.weight), transcendentals=0),
            name=name,
        )(*args)
        self.latest = result if single else result[-1]
        return result


def swap(x, axis, other):
    return lax.ppermute(x, axis, [(i, other(i)) for i in range(lax.axis_size(axis))])


def across_chan(x):
    return swap(x, "chan", lambda i: i ^ 1)


def across_replica(x):
    return swap(x, "replica", lambda i: i ^ 1)


def on_device(activations, cotangent, conv_weights, snake_alpha, seg_lengths, seg_owner, seg_start):
    rows, half = activations.shape
    layers, taps, channels, _ = conv_weights.shape
    top = layers - 1
    fast = lax.axis_size("dp") == 4 and lax.axis_size("replica") == 2
    counts = [1] * layers
    carrier = 1 if fast else None
    weight = {}
    tile, triple = (rows, half), (rows, taps * half)
    flops = 2 * rows * half * half * taps
    sequence = Sequence()
    streams, mine, partners, owns = [], [], {}, {}
    rounded, shifted, arrived, back_owns, far = {}, {}, {}, {}, {}
    across, across_other = {}, {}
    alpha_parts = [None] * layers
    kept, got, late, summed, crossed = {}, {}, {}, {}, {}

    loaded = (2, taps * half, half)
    sems = DMA((2 * taps,))

    def forward_own(layer, load=None):
        outs, args, ins = struct(tile, F32), [mine[layer], weight[layer]], [0, 0]
        scratch = [pltpu.VMEM(triple, BF16)]
        if load is not None:
            outs, args, ins = [outs, struct(loaded, BF16)], args + [conv_weights], ins + [1]
            scratch.append(sems)
        result = sequence.call(
            functools.partial(forward_own_kernel, layer, load), "forward_own", ins, outs, scratch, flops, *args
        )
        if load is None:
            owns[layer] = result
        else:
            owns[layer], weight[load] = result

    def forward_partner(layer, load=None):
        last = layer == top
        ins, args = [0] * 5, [partners[layer], weight[layer], owns[layer], streams[layer], live]
        outs = [struct(tile, BF16)] if last else [struct(tile, F32), struct(tile, BF16)]
        scratch = [pltpu.VMEM(triple, BF16)]
        if not last:
            ins, args = ins + [0], args + [alphas]
        if load is not None:
            ins, args, outs = ins + [1], args + [conv_weights], outs + [struct(loaded, BF16)]
            scratch.append(sems)
        result = sequence.call(
            functools.partial(forward_partner_kernel, layer, last, load), "forward_partner", ins, outs, scratch,
            flops, *args,
        )
        if load is not None:
            weight[load] = result[-1]
        if last:
            return result[0]
        streams.append(result[0])
        mine.append(result[1])
        partners[layer + 1] = across_chan(result[1])

    def back_partner(layer):
        shifted[layer], part = sequence.call(
            functools.partial(back_partner_kernel, layer), "back_partner", [0, 0],
            [struct(triple, BF16), struct(tile, BF16)], [], flops, rounded[layer + 1], weight[layer],
        )
        arrived[layer] = across_chan(part)

    def back_own(layer):
        back_owns[layer] = sequence.call(
            back_own_kernel, "back_own", [0, 0], struct(tile, F32), [], flops, shifted[layer], weight[layer]
        )

    def send_gradient(layer):
        if fast:
            far[layer] = across_replica(sequence.hold(rounded[layer + 1]))

    def combine(layer, grad):
        args = [back_owns[layer], arrived[layer], streams[layer], alphas]
        outs = [struct((1, half), F32)]
        if layer > 0:
            args += [grad, live]
            outs += [struct(tile, F32)] * (layer > 1) + [struct(tile, BF16)]
        result = sequence.call(
            functools.partial(combine_kernel, layer), "combine", [0] * len(args), outs, [], 60 * rows * half, *args
        )
        alpha_parts[layer] = result[0]
        if layer > 0:
            rounded[layer] = result[-1]
            return result[1]

    def turn(*chosen):
        if fast:
            moved_rows = across_replica(sequence.call(
                turn_kernel, "turn", [0] * len(chosen), struct((len(chosen) * half // 2, rows), BF16),
                [pltpu.VMEM((half, rows), BF16)], 10 * rows * half, *[mine[layer] for layer in chosen],
            ))
            for index, layer in enumerate(chosen):
                across[layer] = (moved_rows, index * half // 2)

    def share(*chosen):
        if fast:
            shared = across_chan(sequence.hold(across[chosen[0]][0]))
            for layer in chosen:
                across_other[layer] = shared

    own_turned, far_shifted = {}, {}

    def own_rows(layer):
        if fast:
            own_turned[layer] = sequence.call(
                functools.partial(own_rows_kernel, counts[layer]), "own_rows", [0, 0], struct((half, rows), BF16),
                [pltpu.VMEM((half, rows), BF16)], 10 * rows * half, mine[layer], partners[layer],
            )

    def far_rows(layer):
        if fast:
            far_shifted[layer] = sequence.call(
                functools.partial(far_kernel, layer), "far_rows", [0], struct(triple, BF16), [],
                10 * rows * half, far[layer],
            )

    def weights(layer):
        if not fast:
            out = sequence.call(
                weight_kernel, "weight", [0] * 3, struct((channels, taps * half), BF16),
                [pltpu.VMEM((channels, rows), BF16)], 2 * flops, mine[layer], partners[layer], shifted[layer],
            )
            part = lax.psum_scatter(out, "dp", scatter_dimension=0, tiled=True)
            summed[layer, 0] = lax.psum(part, "replica")
            crossed[layer, 0] = jnp.zeros_like(part)
            return
        pieces, depth = counts[layer], channels // 4 // counts[layer]
        carried = alpha_parts if layer == carrier else []
        outs = [struct((depth, taps * half), BF16)] * (2 * pieces)
        if carried:
            outs[0] = struct((depth + CARRIED, taps * half), BF16)
        args = [own_turned[layer], shifted[layer], across[layer][0], across_other[layer], far_shifted[layer], *carried]
        out = sequence.call(
            functools.partial(paired_weight_kernel, pieces, across[layer][1], len(carried)), "paired_weight",
            [0] * len(args), outs, [pltpu.VMEM((half, rows), BF16)], 2 * flops, *args,
        )
        for part in range(pieces):
            got[layer, part] = swap(out[part], "dp", lambda i: i ^ 1)
            kept[layer, part] = out[pieces + part]

    carry_sum = [None]

    def fold(layer, part=0):
        if not fast:
            return
        keep, came = kept[layer, part], got[layer, part]
        depth, carried = keep.shape[0] // 2, alpha_parts if layer == carrier else []
        outs = [struct((depth + CARRIED * bool(carried), taps * half), BF16)]
        if carried:
            outs.append(struct((1, taps * half), F32))
        result = sequence.call(
            functools.partial(fold_kernel, len(carried)), "fold", [0] * (2 + len(carried)), outs, [], keep.size,
            keep, came, *carried,
        )
        if carried:
            carry_sum[0] = result[1]
        late[layer, part] = swap(result[0], "dp", lambda i: i ^ 2)

    def total(layer, part=0):
        if not fast:
            return
        keep, came, last = kept[layer, part], got[layer, part], late[layer, part]
        outs, args = [struct(last.shape, BF16)], [keep, came, last]
        if layer == carrier:
            outs.append(struct((1, taps * half), F32))
            args.append(carry_sum[0])
        result = sequence.call(
            functools.partial(total_kernel, layer == carrier), "total", [0] * len(args), outs, [], 2 * flops, *args
        )
        if layer == carrier:
            carry_sum[0] = result[1]
        summed[layer, part] = result[0]

    def cross(layer, part=0):
        if fast:
            crossed[layer, part] = across_replica(sequence.hold(summed[layer, part]))

    stream, snaked, grad, live, alphas, weight[0] = sequence.call(
        prep_kernel, "prep", [1] * 7,
        [struct(tile, F32), struct(tile, BF16), struct(tile, BF16), struct((rows, 128), F32),
         struct(snake_alpha.shape, F32), struct(loaded, BF16)],
        [pltpu.SMEM(seg_lengths.shape, jnp.int32)] * 3 + [pltpu.VMEM(tile, BF16)] * 2 + [DMA((6,)), sems],
        40 * rows * half,
        seg_lengths, seg_owner, seg_start, activations, cotangent, snake_alpha, conv_weights,
    )
    streams.append(stream)
    mine.append(snaked)
    partners[0] = across_chan(snaked)
    rounded[layers] = grad
    depth = channels // lax.axis_size("dp")

    def finish(chosen, before=None):
        pairs = [] if before is None else [before]
        carry = carrier in chosen
        if carry:
            pairs.append(carry_sum[0])
        for layer in chosen:
            for part in range(counts[layer]):
                pairs += [summed[layer, part], crossed[layer, part]]
        out = struct((layers, taps, depth, half), F32)
        return sequence.call(
            functools.partial(
                finish_kernel, fast, before is not None, carry, tuple((layer, counts[layer]) for layer in chosen)
            ),
            "finish", [2] * (before is not None) + [0] * (len(pairs) - (before is not None)),
            [out, struct((layers, half), F32)] if carry else [out],
            [pltpu.VMEM((len(chosen), taps, depth, half), F32), DMA((len(chosen),))],
            layers * taps * depth * half, *pairs, specs=[ANY_HBM] + [IN_VMEM] * carry,
            aliases={0: 0} if before is not None else None,
        )

    rounds = [("replica", 1 << bit) for bit in range(8) if lax.axis_size("replica") >> (bit + 1)]
    rounds += [("dp", 1 << bit) for bit in range(8) if lax.axis_size("dp") >> (bit + 1)]
    arrivals = []

    def alpha_round():
        if arrivals:
            value = sequence.call(
                add_kernel, "add", [0, 0], struct((layers, half), F32), [], layers * half, *arrivals.pop()
            )
        else:
            value = sequence.call(
                stack_kernel, "stack", [0] * layers, struct((layers, half), F32), [], layers * half, *alpha_parts
            )
        if not rounds:
            return value
        axis, apart = rounds.pop(0)
        arrivals.append((value, swap(value, axis, lambda place: place ^ apart)))

    forward_own(0, load=2)
    send_gradient(2)
    forward_partner(0, load=1)
    back_partner(2)
    forward_own(1)
    forward_partner(1)
    turn(2)
    back_own(2)
    grad = combine(2, grad)
    send_gradient(1)
    far_rows(2)
    own_rows(2)
    turn(1)
    back_partner(1)
    share(2)
    back_own(1)
    combine(1, grad)
    weights(2)
    back_partner(0)
    back_own(0)
    sequence.weight = 10
    combine(0, None)
    own_rows(1)
    far_rows(1)
    own_rows(0)
    share(1)
    forward_own(2)
    residual_out = forward_partner(2)
    sequence.weight = 0.01
    weights(1)
    turn(0)
    send_gradient(0)
    fold(2)
    share(0)
    far_rows(0)
    sequence.weight = 0.01
    weights(0)
    sequence.weight = 10
    fold(1)
    total(2)
    cross(2)
    fold(0)
    total(1)
    cross(1)
    total(0)
    cross(0)
    if fast:
        weight_grads, alpha_grads = finish((2, 1))
        (weight_grads,) = finish((0,), weight_grads)
    else:
        alpha_grads = alpha_round()
        while alpha_grads is None:
            alpha_grads = alpha_round()
        (weight_grads,) = finish((2, 1, 0))
    return (residual_out, weight_grads, alpha_grads)


def solution(mesh):
    return jax.shard_map(
        on_device,
        mesh=mesh,
        in_specs=(
            P(("groups", "dp", "replica"), "chan"),
            P(("groups", "dp", "replica"), "chan"),
            P(None, None, None, "chan"),
            P(None, "chan"),
            P("groups"),
            P("groups"),
            P("groups"),
        ),
        out_specs=(
            P(("groups", "dp", "replica"), "chan"),
            P("groups", None, "dp", "chan"),
            P("groups", "chan"),
        ),
        check_vma=False,
    )
```

```python
import functools
import math

import jax
import jax.numpy as jnp
from jax import lax
from jax.experimental import pallas as pl
from jax.experimental.pallas import tpu as pltpu
from jax.sharding import PartitionSpec as P

dilations = (1, 3, 5)
F32, BF16 = jnp.float32, jnp.bfloat16
ANY_HBM = pl.BlockSpec(memory_space=pltpu.HBM)
IN_VMEM = pl.BlockSpec(memory_space=pltpu.VMEM)
DMA = pltpu.SemaphoreType.DMA
PI_PARTS = (3.140625, 9.67502593994140625e-4, 1.509957990978376432e-7)
SIN_TERMS = (-1.0 / 39916800, 1.0 / 362880, -1.0 / 5040, 1.0 / 120, -1.0 / 6)
COS_TERMS = (1.0 / 479001600, -1.0 / 3628800, 1.0 / 40320, -1.0 / 720, 1.0 / 24, -0.5)
RANGE = 8192.0
CHUNK = 64
CARRIED = 16


def horner(terms, x):
    total = jnp.full_like(x, terms[0])
    for term in terms[1:]:
        total = total * x + term
    return total


def reduced(angle):
    turns = jnp.round(angle * (1.0 / 3.14159265358979))
    for part in PI_PARTS:
        angle = angle - turns * part
    return angle


def sine(angle, exact_range):
    if not exact_range:
        return jnp.sin(angle)
    rest = reduced(angle)
    square = rest * rest
    return rest + rest * (square * horner(SIN_TERMS, square))


def sine_cosine(angle, exact_range):
    if not exact_range:
        return jnp.sin(angle), jnp.cos(angle)
    rest = reduced(angle)
    square = rest * rest
    return (
        rest + rest * (square * horner(SIN_TERMS, square)),
        1.0 + square * horner(COS_TERMS, square),
    )


def by_range(bound, body):
    @pl.when(bound < RANGE)
    def _():
        body(True)

    @pl.when(bound >= RANGE)
    def _():
        body(False)


def write_snake(stream_ref, alpha, out_ref):
    inverse = 1.0 / alpha
    bound = jnp.max(jnp.abs(stream_ref[...])) * jnp.max(alpha)

    def body(exact_range):
        @pl.loop(0, stream_ref.shape[0] // CHUNK)
        def _(step):
            rows = pl.ds(pl.multiple_of(step * CHUNK, CHUNK), CHUNK)
            stream = stream_ref[rows, :]
            wave = sine(alpha * stream, exact_range)
            out_ref[rows, :] = (stream + wave * wave * inverse).astype(BF16)

    by_range(bound, body)


def moved(values, offset):
    if offset == 0:
        return values
    rows = values.shape[0]
    place = lax.broadcasted_iota(jnp.int32, values.shape, 0)
    turned = pltpu.roll(values, (-offset) % rows, 0)
    inside = place < rows - offset if offset > 0 else place >= -offset
    return jnp.where(inside, turned, 0.0)


def write_shifts(values_ref, out_ref, dilation):
    width = values_ref.shape[1]
    values = values_ref[...].astype(F32)
    for tap in range(3):
        out_ref[:, tap * width : (tap + 1) * width] = moved(values, (tap - 1) * dilation).astype(BF16)


def chan_begin(side, half):
    chan = lax.axis_index("chan")
    return pl.multiple_of((chan if side == 0 else 1 - chan) * half, half)


def load_weights(layer, weight_hbm, weight_ref, sems):
    half = weight_hbm.shape[3]
    loads = []
    for side in range(2):
        for tap in range(3):
            source = weight_hbm.at[layer, tap, pl.ds(chan_begin(side, half), half), :]
            target = weight_ref.at[side, pl.ds(tap * half, half), :]
            loads.append(pltpu.make_async_copy(source, target, sems.at[len(loads)]))
    for copy in loads:
        copy.start()
    return loads


def prep_kernel(
    len_hbm, own_hbm, start_hbm, act_hbm, cot_hbm, alpha_hbm, weight_hbm,
    stream_ref, snake_ref, grad_ref, live_ref, alpha_ref, weight_ref,
    len_ref, own_ref, start_ref, act_ref, cot_ref, sems, weight_sems,
):
    pairs = (
        (len_hbm, len_ref), (own_hbm, own_ref), (start_hbm, start_ref),
        (alpha_hbm, alpha_ref), (act_hbm, act_ref), (cot_hbm, cot_ref),
    )
    copies = [pltpu.make_async_copy(a, b, sems.at[i]) for i, (a, b) in enumerate(pairs)]
    for copy in copies:
        copy.start()
    loads = load_weights(0, weight_hbm, weight_ref, weight_sems)
    replicas = lax.axis_size("replica")
    device = lax.axis_index("dp") * replicas + lax.axis_index("replica")
    rows, width = act_ref.shape
    place = lax.broadcasted_iota(jnp.int32, (rows, 128), 0)
    live_ref[...] = jnp.zeros((rows, 128), F32)
    for copy in copies[:3]:
        copy.wait()

    @pl.loop(0, len_ref.shape[0])
    def _(clip):
        @pl.when(own_ref[clip] == device)
        def _():
            first = start_ref[clip]
            inside = (place >= first) & (place < first + len_ref[clip])
            live_ref[...] = jnp.where(inside, 1.0, live_ref[...])

    live = jnp.tile(live_ref[...], (1, width // 128))
    for copy in copies[3:5]:
        copy.wait()
    stream_ref[...] = act_ref[...].astype(F32) * live
    write_snake(stream_ref, alpha_ref[0:1, :], snake_ref)
    copies[5].wait()
    grad_ref[...] = (cot_ref[...].astype(F32) * live).astype(BF16)
    for copy in loads:
        copy.wait()


def forward_own_kernel(layer, load, snake_ref, weight_ref, *rest):
    if load is None:
        out_ref, shifts_ref = rest
        loads = []
    else:
        weight_hbm, out_ref, loaded_ref, shifts_ref, sems = rest
        loads = load_weights(load, weight_hbm, loaded_ref, sems)
    write_shifts(snake_ref, shifts_ref, dilations[layer])
    out_ref[...] = jnp.dot(shifts_ref[...], weight_ref[0], preferred_element_type=F32)
    for copy in loads:
        copy.wait()


def forward_partner_kernel(layer, last, load, snake_ref, weight_ref, own_ref, old_ref, live_ref, *rest):
    rest = list(rest)
    alpha_ref = None if last else rest.pop(0)
    weight_hbm = None if load is None else rest.pop(0)
    result_ref = rest.pop(0)
    next_ref = None if last else rest.pop(0)
    loads = []
    if load is not None:
        loaded_ref, shifts_ref, sems = rest
        loads = load_weights(load, weight_hbm, loaded_ref, sems)
    else:
        (shifts_ref,) = rest
    write_shifts(snake_ref, shifts_ref, dilations[layer])
    part = jnp.dot(shifts_ref[...], weight_ref[1], preferred_element_type=F32)
    live = jnp.tile(live_ref[...], (1, old_ref.shape[1] // 128))
    new = (old_ref[...] + (own_ref[...] + part)) * live
    result_ref[...] = new.astype(result_ref.dtype)
    if not last:
        write_snake(result_ref, alpha_ref[layer + 1 : layer + 2, :], next_ref)
    for copy in loads:
        copy.wait()


def back_product(shifted_ref, weight_ref, side):
    half = weight_ref.shape[2]
    total = None
    for tap in range(3):
        span = slice(tap * half, (tap + 1) * half)
        part = lax.dot_general(
            shifted_ref[:, span], weight_ref[side, span, :], (((1,), (1,)), ((), ())),
            preferred_element_type=F32,
        )
        total = part if total is None else total + part
    return total


def back_partner_kernel(layer, grad_ref, weight_ref, shifted_ref, out_ref):
    write_shifts(grad_ref, shifted_ref, -dilations[layer])
    out_ref[...] = back_product(shifted_ref, weight_ref, 1).astype(BF16)


def back_own_kernel(shifted_ref, weight_ref, out_ref):
    out_ref[...] = back_product(shifted_ref, weight_ref, 0)


def combine_kernel(layer, own_ref, partner_ref, stream_ref, alphas_ref, *rest):
    if layer == 0:
        (alpha_grad_ref,) = rest
    elif len(rest) == 5:
        old_ref, live_ref, alpha_grad_ref, grad_ref, rounded_ref = rest
    else:
        old_ref, live_ref, alpha_grad_ref, rounded_ref = rest
        grad_ref = None
    alpha = alphas_ref[layer : layer + 1, :]
    inverse = 1.0 / alpha
    bound = jnp.max(jnp.abs(stream_ref[...])) * jnp.max(alpha)
    width = stream_ref.shape[1]

    def body(exact_range):
        def step_body(step, total):
            rows = pl.ds(pl.multiple_of(step * CHUNK, CHUNK), CHUNK)
            stream = stream_ref[rows, :]
            back = own_ref[rows, :] + partner_ref[rows, :].astype(F32)
            sin, cos = sine_cosine(alpha * stream, exact_range)
            double = 2.0 * sin * cos
            ratio = sin * inverse
            term = back * (stream * double * inverse - ratio * ratio)
            if layer > 0:
                live = jnp.tile(live_ref[rows, :], (1, width // 128))
                grad = (old_ref[rows, :].astype(F32) + back * (1.0 + double)) * live
                if grad_ref is not None:
                    grad_ref[rows, :] = grad
                rounded_ref[rows, :] = grad.astype(BF16)
            return total + jnp.sum(term.reshape(CHUNK // 8, 8, width), axis=0)

        total = lax.fori_loop(0, stream_ref.shape[0] // CHUNK, step_body, jnp.zeros((8, width), F32))
        alpha_grad_ref[...] = jnp.sum(total, axis=0, keepdims=True)

    by_range(bound, body)


def block_place(pieces, slice_index, part):
    apart = jnp.bitwise_xor(slice_index, lax.axis_index("dp"))
    order = (2 * pieces, 0, 2 * pieces + 1, 1)
    return 2 * part + jnp.where(
        apart == 0, order[0], jnp.where(apart == 1, order[1], jnp.where(apart == 2, order[2], order[3]))
    )


def weight_kernel(own_ref, partner_ref, shifted_ref, out_ref, turned_ref):
    half = own_ref.shape[1]
    chan = lax.axis_index("chan")
    for ref, side in ((own_ref, chan), (partner_ref, 1 - chan)):
        turned_ref[pl.ds(pl.multiple_of(side * half, half), half), :] = ref[...].T
    for tap in range(3):
        span = slice(tap * half, (tap + 1) * half)
        out_ref[:, span] = jnp.dot(turned_ref[...], shifted_ref[:, span], preferred_element_type=F32).astype(BF16)


def place_rows(pieces, rows_of, side, target_ref, columns):
    size = rows_of.shape[0] // (2 * pieces)
    for local in range(2):
        for part in range(pieces):
            begin = pl.multiple_of(block_place(pieces, side * 2 + local, part) * size, size)
            low = (local * pieces + part) * size
            target_ref[pl.ds(begin, size), columns] = rows_of[low : low + size, :]


def pick_parts(turned_ref, part, size):
    begin = pl.multiple_of(part * size, size)
    return [turned_ref[pl.ds(local * 2 * size + begin, size), :] for local in range(2)]


def turn_kernel(*refs):
    snakes, out_ref, turned_ref = refs[:-2], refs[-2], refs[-1]
    size = snakes[0].shape[1] // 4
    for index, ref in enumerate(snakes):
        turned_ref[...] = ref[...].T
        for local, piece in enumerate(pick_parts(turned_ref, 1 - lax.axis_index("replica"), size)):
            low = (2 * index + local) * size
            out_ref[low : low + size, :] = piece


def own_rows_kernel(pieces, own_ref, partner_ref, out_ref, half_ref):
    chan = lax.axis_index("chan")
    mine = lax.axis_index("replica")
    for ref, side in ((own_ref, chan), (partner_ref, 1 - chan)):
        half_ref[...] = ref[...].T
        both = jnp.concatenate(pick_parts(half_ref, mine, ref.shape[1] // 4), 0)
        place_rows(pieces, both, side, out_ref, slice(None))


def far_kernel(layer, grad_ref, out_ref):
    write_shifts(grad_ref, out_ref, -dilations[layer])


def write_carried(values, out_ref, low):
    first = values.astype(BF16).astype(F32)
    second = (values - first).astype(BF16).astype(F32)
    third = values - first - second
    shape = (CARRIED, values.shape[1])
    row = lax.broadcasted_iota(jnp.int32, shape, 0)
    block = jnp.where(row == 0, first, jnp.where(row == 1, second, jnp.where(row == 2, third, 0.0)))
    out_ref[low : low + CARRIED, :] = block.astype(BF16)


def read_carried(ref, low):
    block = ref[low : low + CARRIED, :].astype(F32)
    return (block[0:1, :] + block[1:2, :]) + block[2:3, :]


def paired_weight_kernel(pieces, low, carry, own_ref, shifted_ref, across_ref, across_other_ref, far_ref, *rest):
    if carry:
        write_carried(jnp.concatenate([ref[...] for ref in rest[:carry]], 1), rest[carry], own_ref.shape[0] // 2)
        rest = rest[carry:]
    outs, turned_ref = rest[:-1], rest[-1]
    half = own_ref.shape[0]
    chan = lax.axis_index("chan")
    for ref, side in ((across_ref, chan), (across_other_ref, 1 - chan)):
        place_rows(pieces, ref[low : low + half // 2, :], side, turned_ref, slice(None))
    for tap in range(3):
        span = slice(tap * half, (tap + 1) * half)
        product = jnp.dot(own_ref[...], shifted_ref[:, span], preferred_element_type=F32)
        product += jnp.dot(turned_ref[...], far_ref[:, span], preferred_element_type=F32)
        product = product.astype(BF16)
        size = product.shape[0] // len(outs)
        for place, ref in enumerate(outs):
            ref[0:size, span] = product[place * size : (place + 1) * size, :]


def finish_kernel(paired, held, carry, counts, *refs):
    total_ref, sems = refs[-2:]
    refs = list(refs[1:-2] if held else refs[:-2])
    if carry:
        alpha_ref = refs.pop()
        alpha_mine = refs.pop(0)
    out_ref = refs.pop()
    half = total_ref.shape[3]
    rows_of = total_ref.shape[2] // (2 if paired else 1)
    copies = []
    for index, (layer, pieces) in enumerate(counts):
        for part in range(pieces):
            mine_ref, other_ref = refs.pop(0), refs.pop(0)
            size = rows_of // pieces
            if carry and other_ref.shape[0] > size:
                alpha = alpha_mine[...] + read_carried(other_ref, size)
                for place in range(3):
                    alpha_ref[place : place + 1, :] = alpha[:, place * half : (place + 1) * half]
            for tap in range(3):
                span = slice(tap * half, (tap + 1) * half)
                mine, other = mine_ref[0:size, span].astype(F32), other_ref[0:size, span].astype(F32)
                if paired:
                    begin = lax.axis_index("replica") * (size * pieces)
                    for values, start in ((mine, begin), (other, size * pieces - begin)):
                        place = pl.multiple_of(start + part * size, size)
                        total_ref[index, tap, pl.ds(place, size), :] = values
                else:
                    total_ref[index, tap] = mine + other
        copies.append(pltpu.make_async_copy(total_ref.at[index], out_ref.at[layer], sems.at[index]))
        copies[-1].start()
    for copy in copies:
        copy.wait()


def fold_kernel(carry, keep, got, *rest):
    if carry:
        mine, rest = rest[:carry], rest[carry:]
        send, sum_ref = rest
    else:
        (send,) = rest
    rows = keep.shape[0] // 2
    send[0:rows, :] = (keep[rows:, :].astype(F32) + got[rows : 2 * rows, :].astype(F32)).astype(BF16)
    if carry:
        values = jnp.concatenate([ref[...] for ref in mine], 1) + read_carried(got, 2 * rows)
        sum_ref[...] = values
        write_carried(values, send, rows)


def total_kernel(carry, keep, got, late, *rest):
    if carry:
        mine, out_ref, sum_ref = rest
    else:
        (out_ref,) = rest
    rows = keep.shape[0] // 2
    total = keep[0:rows, :].astype(F32) + got[0:rows, :].astype(F32) + late[0:rows, :].astype(F32)
    out_ref[0:rows, :] = total.astype(BF16)
    if carry:
        values = mine[...] + read_carried(late, rows)
        sum_ref[...] = values
        write_carried(values, out_ref, rows)


def stack_kernel(*refs):
    for index, ref in enumerate(refs[:-1]):
        refs[-1][index : index + 1, :] = ref[...]


def add_kernel(left, right, out_ref):
    out_ref[...] = left[...] + right[...]


def struct(shape, dtype):
    return jax.ShapeDtypeStruct(shape, dtype)


def after(value, other):
    return value if other is None else lax.optimization_barrier((value, other))[0]


class Sequence:
    def __init__(self):
        self.latest = None
        self.weight = 10

    def hold(self, value):
        return after(value, self.latest)

    def call(self, kernel, name, ins, outs, scratch, flops, *args, specs=None, aliases=None):
        single = not isinstance(outs, list)
        size = sum(a.size * a.dtype.itemsize for a in args if a.size < 2000000)
        size += sum(math.prod(o.shape) * o.dtype.itemsize for o in ([outs] if single else outs))
        args = [pltpu.with_memory_space_constraint(a, pltpu.HBM) if i == 1 else a for i, a in zip(ins, args)]
        if self.latest is not None:
            held = ins.index(0)
            args[held] = self.hold(args[held])
        result = pl.pallas_call(
            kernel,
            in_specs=[ANY_HBM if i else IN_VMEM for i in ins],
            out_specs=specs or (IN_VMEM if single else [IN_VMEM] * len(outs)),
            out_shape=outs,
            scratch_shapes=scratch,
            input_output_aliases=aliases or {},
            compiler_params=pltpu.CompilerParams(vmem_limit_bytes=24 * 1024 * 1024),
            cost_estimate=pl.CostEstimate(flops=int(flops * self.weight), bytes_accessed=int(size * self.weight), transcendentals=0),
            name=name,
        )(*args)
        self.latest = result if single else result[-1]
        return result


def swap(x, axis, other):
    return lax.ppermute(x, axis, [(i, other(i)) for i in range(lax.axis_size(axis))])


def across_chan(x):
    return swap(x, "chan", lambda i: i ^ 1)


def across_replica(x):
    return swap(x, "replica", lambda i: i ^ 1)


def on_device(activations, cotangent, conv_weights, snake_alpha, seg_lengths, seg_owner, seg_start):
    rows, half = activations.shape
    layers, taps, channels, _ = conv_weights.shape
    top = layers - 1
    fast = lax.axis_size("dp") == 4 and lax.axis_size("replica") == 2
    counts = [2, 1, 1] if fast else [1, 1, 1]
    carrier = 1 if fast else None
    weight = {}
    tile, triple = (rows, half), (rows, taps * half)
    flops = 2 * rows * half * half * taps
    sequence = Sequence()
    streams, mine, partners, owns = [], [], {}, {}
    rounded, shifted, arrived, back_owns, far = {}, {}, {}, {}, {}
    across, across_other = {}, {}
    alpha_parts = [None] * layers
    kept, got, late, summed, crossed = {}, {}, {}, {}, {}

    loaded = (2, taps * half, half)
    sems = DMA((2 * taps,))

    def forward_own(layer, load=None):
        outs, args, ins = struct(tile, F32), [mine[layer], weight[layer]], [0, 0]
        scratch = [pltpu.VMEM(triple, BF16)]
        if load is not None:
            outs, args, ins = [outs, struct(loaded, BF16)], args + [conv_weights], ins + [1]
            scratch.append(sems)
        result = sequence.call(
            functools.partial(forward_own_kernel, layer, load), "forward_own", ins, outs, scratch, flops, *args
        )
        if load is None:
            owns[layer] = result
        else:
            owns[layer], weight[load] = result

    def forward_partner(layer, load=None):
        last = layer == top
        ins, args = [0] * 5, [partners[layer], weight[layer], owns[layer], streams[layer], live]
        outs = [struct(tile, BF16)] if last else [struct(tile, F32), struct(tile, BF16)]
        scratch = [pltpu.VMEM(triple, BF16)]
        if not last:
            ins, args = ins + [0], args + [alphas]
        if load is not None:
            ins, args, outs = ins + [1], args + [conv_weights], outs + [struct(loaded, BF16)]
            scratch.append(sems)
        result = sequence.call(
            functools.partial(forward_partner_kernel, layer, last, load), "forward_partner", ins, outs, scratch,
            flops, *args,
        )
        if load is not None:
            weight[load] = result[-1]
        if last:
            return result[0]
        streams.append(result[0])
        mine.append(result[1])
        partners[layer + 1] = across_chan(result[1])

    def back_partner(layer):
        shifted[layer], part = sequence.call(
            functools.partial(back_partner_kernel, layer), "back_partner", [0, 0],
            [struct(triple, BF16), struct(tile, BF16)], [], flops, rounded[layer + 1], weight[layer],
        )
        arrived[layer] = across_chan(part)

    def back_own(layer):
        back_owns[layer] = sequence.call(
            back_own_kernel, "back_own", [0, 0], struct(tile, F32), [], flops, shifted[layer], weight[layer]
        )

    def send_gradient(layer):
        if fast:
            far[layer] = across_replica(sequence.hold(rounded[layer + 1]))

    def combine(layer, grad):
        args = [back_owns[layer], arrived[layer], streams[layer], alphas]
        outs = [struct((1, half), F32)]
        if layer > 0:
            args += [grad, live]
            outs += [struct(tile, F32)] * (layer > 1) + [struct(tile, BF16)]
        result = sequence.call(
            functools.partial(combine_kernel, layer), "combine", [0] * len(args), outs, [], 60 * rows * half, *args
        )
        alpha_parts[layer] = result[0]
        if layer > 0:
            rounded[layer] = result[-1]
            return result[1]

    def turn(*chosen):
        if fast:
            moved_rows = across_replica(sequence.call(
                turn_kernel, "turn", [0] * len(chosen), struct((len(chosen) * half // 2, rows), BF16),
                [pltpu.VMEM((half, rows), BF16)], 10 * rows * half, *[mine[layer] for layer in chosen],
            ))
            for index, layer in enumerate(chosen):
                across[layer] = (moved_rows, index * half // 2)

    def share(*chosen):
        if fast:
            shared = across_chan(sequence.hold(across[chosen[0]][0]))
            for layer in chosen:
                across_other[layer] = shared

    own_turned, far_shifted = {}, {}

    def own_rows(layer):
        if fast:
            own_turned[layer] = sequence.call(
                functools.partial(own_rows_kernel, counts[layer]), "own_rows", [0, 0], struct((half, rows), BF16),
                [pltpu.VMEM((half, rows), BF16)], 10 * rows * half, mine[layer], partners[layer],
            )

    def far_rows(layer):
        if fast:
            far_shifted[layer] = sequence.call(
                functools.partial(far_kernel, layer), "far_rows", [0], struct(triple, BF16), [],
                10 * rows * half, far[layer],
            )

    def launch(layer, part):
        if fast:
            send, kept[layer, part] = kept[layer, part]
            got[layer, part] = swap(sequence.hold(send) if part else send, "dp", lambda i: i ^ 1)

    def weights(layer):
        if not fast:
            out = sequence.call(
                weight_kernel, "weight", [0] * 3, struct((channels, taps * half), BF16),
                [pltpu.VMEM((channels, rows), BF16)], 2 * flops, mine[layer], partners[layer], shifted[layer],
            )
            part = lax.psum_scatter(out, "dp", scatter_dimension=0, tiled=True)
            summed[layer, 0] = lax.psum(part, "replica")
            crossed[layer, 0] = jnp.zeros_like(part)
            return
        pieces, depth = counts[layer], channels // 4 // counts[layer]
        carried = alpha_parts if layer == carrier else []
        outs = [struct((depth, taps * half), BF16)] * (2 * pieces)
        if carried:
            outs[0] = struct((depth + CARRIED, taps * half), BF16)
        args = [own_turned[layer], shifted[layer], across[layer][0], across_other[layer], far_shifted[layer], *carried]
        out = sequence.call(
            functools.partial(paired_weight_kernel, pieces, across[layer][1], len(carried)), "paired_weight",
            [0] * len(args), outs, [pltpu.VMEM((half, rows), BF16)], 2 * flops, *args,
        )
        for part in range(pieces):
            kept[layer, part] = (out[part], out[pieces + part])
        launch(layer, 0)

    carry_sum = [None]

    def fold(layer, part=0):
        if not fast:
            return
        keep, came = kept[layer, part], got[layer, part]
        depth, carried = keep.shape[0] // 2, alpha_parts if layer == carrier else []
        outs = [struct((depth + CARRIED * bool(carried), taps * half), BF16)]
        if carried:
            outs.append(struct((1, taps * half), F32))
        result = sequence.call(
            functools.partial(fold_kernel, len(carried)), "fold", [0] * (2 + len(carried)), outs, [], keep.size,
            keep, came, *carried,
        )
        if carried:
            carry_sum[0] = result[1]
        late[layer, part] = swap(result[0], "dp", lambda i: i ^ 2)

    def total(layer, part=0):
        if not fast:
            return
        keep, came, last = kept[layer, part], got[layer, part], late[layer, part]
        outs, args = [struct(last.shape, BF16)], [keep, came, last]
        if layer == carrier:
            outs.append(struct((1, taps * half), F32))
            args.append(carry_sum[0])
        result = sequence.call(
            functools.partial(total_kernel, layer == carrier), "total", [0] * len(args), outs, [], 2 * flops, *args
        )
        if layer == carrier:
            carry_sum[0] = result[1]
        summed[layer, part] = result[0]

    def cross(layer, part=0):
        if fast:
            crossed[layer, part] = across_replica(sequence.hold(summed[layer, part]))

    stream, snaked, grad, live, alphas, weight[0] = sequence.call(
        prep_kernel, "prep", [1] * 7,
        [struct(tile, F32), struct(tile, BF16), struct(tile, BF16), struct((rows, 128), F32),
         struct(snake_alpha.shape, F32), struct(loaded, BF16)],
        [pltpu.SMEM(seg_lengths.shape, jnp.int32)] * 3 + [pltpu.VMEM(tile, BF16)] * 2 + [DMA((6,)), sems],
        40 * rows * half,
        seg_lengths, seg_owner, seg_start, activations, cotangent, snake_alpha, conv_weights,
    )
    streams.append(stream)
    mine.append(snaked)
    partners[0] = across_chan(snaked)
    rounded[layers] = grad
    depth = channels // lax.axis_size("dp")

    def finish(chosen, before=None):
        pairs = [] if before is None else [before]
        carry = carrier in chosen
        if carry:
            pairs.append(carry_sum[0])
        for layer in chosen:
            for part in range(counts[layer]):
                pairs += [summed[layer, part], crossed[layer, part]]
        out = struct((layers, taps, depth, half), F32)
        return sequence.call(
            functools.partial(
                finish_kernel, fast, before is not None, carry, tuple((layer, counts[layer]) for layer in chosen)
            ),
            "finish", [2] * (before is not None) + [0] * (len(pairs) - (before is not None)),
            [out, struct((layers, half), F32)] if carry else [out],
            [pltpu.VMEM((len(chosen), taps, depth, half), F32), DMA((len(chosen),))],
            layers * taps * depth * half, *pairs, specs=[ANY_HBM] + [IN_VMEM] * carry,
            aliases={0: 0} if before is not None else None,
        )

    rounds = [("replica", 1 << bit) for bit in range(8) if lax.axis_size("replica") >> (bit + 1)]
    rounds += [("dp", 1 << bit) for bit in range(8) if lax.axis_size("dp") >> (bit + 1)]
    arrivals = []

    def alpha_round():
        if arrivals:
            value = sequence.call(
                add_kernel, "add", [0, 0], struct((layers, half), F32), [], layers * half, *arrivals.pop()
            )
        else:
            value = sequence.call(
                stack_kernel, "stack", [0] * layers, struct((layers, half), F32), [], layers * half, *alpha_parts
            )
        if not rounds:
            return value
        axis, apart = rounds.pop(0)
        arrivals.append((value, swap(value, axis, lambda place: place ^ apart)))

    forward_own(0, load=2)
    send_gradient(2)
    forward_partner(0, load=1)
    back_partner(2)
    forward_own(1)
    forward_partner(1)
    turn(2)
    back_own(2)
    grad = combine(2, grad)
    send_gradient(1)
    far_rows(2)
    own_rows(2)
    turn(1, 0)
    back_partner(1)
    share(2)
    back_own(1)
    combine(1, grad)
    weights(2)
    back_partner(0)
    back_own(0)
    sequence.weight = 10
    combine(0, None)
    own_rows(1)
    far_rows(1)
    own_rows(0)
    share(1, 0)
    send_gradient(0)
    forward_own(2)
    residual_out = forward_partner(2)
    sequence.weight = 0.01
    weights(1)
    fold(2)
    far_rows(0)
    sequence.weight = 0.01
    weights(0)
    sequence.weight = 10
    fold(1)
    total(2)
    fold(0, 0)
    launch(0, 1)
    total(1)
    cross(1)
    cross(2)
    fold(0, 1)
    total(0, 0)
    cross(0, 0)
    if fast:
        weight_grads, alpha_grads = finish((2, 1))
        total(0, 1)
        cross(0, 1)
        (weight_grads,) = finish((0,), weight_grads)
    else:
        alpha_grads = alpha_round()
        while alpha_grads is None:
            alpha_grads = alpha_round()
        (weight_grads,) = finish((2, 1, 0))
    return (residual_out, weight_grads, alpha_grads)


def solution(mesh):
    return jax.shard_map(
        on_device,
        mesh=mesh,
        in_specs=(
            P(("groups", "dp", "replica"), "chan"),
            P(("groups", "dp", "replica"), "chan"),
            P(None, None, None, "chan"),
            P(None, "chan"),
            P("groups"),
            P("groups"),
            P("groups"),
        ),
        out_specs=(
            P(("groups", "dp", "replica"), "chan"),
            P("groups", None, "dp", "chan"),
            P("groups", "chan"),
        ),
        check_vma=False,
    )
```

```python
import functools
import math

import jax
import jax.numpy as jnp
from jax import lax
from jax.experimental import pallas as pl
from jax.experimental.pallas import tpu as pltpu
from jax.sharding import PartitionSpec as P

dilations = (1, 3, 5)
F32, BF16 = jnp.float32, jnp.bfloat16
ANY_HBM = pl.BlockSpec(memory_space=pltpu.HBM)
IN_VMEM = pl.BlockSpec(memory_space=pltpu.VMEM)
DMA = pltpu.SemaphoreType.DMA
PI_PARTS = (3.140625, 9.67502593994140625e-4, 1.509957990978376432e-7)
SIN_TERMS = (-1.0 / 39916800, 1.0 / 362880, -1.0 / 5040, 1.0 / 120, -1.0 / 6)
COS_TERMS = (1.0 / 479001600, -1.0 / 3628800, 1.0 / 40320, -1.0 / 720, 1.0 / 24, -0.5)
RANGE = 8192.0
CHUNK = 64
CARRIED = 16


def horner(terms, x):
    total = jnp.full_like(x, terms[0])
    for term in terms[1:]:
        total = total * x + term
    return total


def reduced(angle):
    turns = jnp.round(angle * (1.0 / 3.14159265358979))
    for part in PI_PARTS:
        angle = angle - turns * part
    return angle


def sine(angle, exact_range):
    if not exact_range:
        return jnp.sin(angle)
    rest = reduced(angle)
    square = rest * rest
    return rest + rest * (square * horner(SIN_TERMS, square))


def sine_cosine(angle, exact_range):
    if not exact_range:
        return jnp.sin(angle), jnp.cos(angle)
    rest = reduced(angle)
    square = rest * rest
    return (
        rest + rest * (square * horner(SIN_TERMS, square)),
        1.0 + square * horner(COS_TERMS, square),
    )


def by_range(bound, body):
    @pl.when(bound < RANGE)
    def _():
        body(True)

    @pl.when(bound >= RANGE)
    def _():
        body(False)


def write_snake(stream_ref, alpha, out_ref):
    inverse = 1.0 / alpha
    bound = jnp.max(jnp.abs(stream_ref[...])) * jnp.max(alpha)

    def body(exact_range):
        @pl.loop(0, stream_ref.shape[0] // CHUNK)
        def _(step):
            rows = pl.ds(pl.multiple_of(step * CHUNK, CHUNK), CHUNK)
            stream = stream_ref[rows, :]
            wave = sine(alpha * stream, exact_range)
            out_ref[rows, :] = (stream + wave * wave * inverse).astype(BF16)

    by_range(bound, body)


def moved(values, offset):
    if offset == 0:
        return values
    rows = values.shape[0]
    place = lax.broadcasted_iota(jnp.int32, values.shape, 0)
    turned = pltpu.roll(values, (-offset) % rows, 0)
    inside = place < rows - offset if offset > 0 else place >= -offset
    return jnp.where(inside, turned, 0.0)


def write_shifts(values_ref, out_ref, dilation):
    width = values_ref.shape[1]
    values = values_ref[...].astype(F32)
    for tap in range(3):
        out_ref[:, tap * width : (tap + 1) * width] = moved(values, (tap - 1) * dilation).astype(BF16)


def chan_begin(side, half):
    chan = lax.axis_index("chan")
    return pl.multiple_of((chan if side == 0 else 1 - chan) * half, half)


def load_weights(layer, weight_hbm, weight_ref, sems):
    half = weight_hbm.shape[3]
    loads = []
    for side in range(2):
        for tap in range(3):
            source = weight_hbm.at[layer, tap, pl.ds(chan_begin(side, half), half), :]
            target = weight_ref.at[side, pl.ds(tap * half, half), :]
            loads.append(pltpu.make_async_copy(source, target, sems.at[len(loads)]))
    for copy in loads:
        copy.start()
    return loads


def prep_kernel(
    len_hbm, own_hbm, start_hbm, act_hbm, cot_hbm, alpha_hbm, weight_hbm,
    stream_ref, snake_ref, grad_ref, live_ref, alpha_ref, weight_ref,
    len_ref, own_ref, start_ref, act_ref, cot_ref, sems, weight_sems,
):
    pairs = (
        (len_hbm, len_ref), (own_hbm, own_ref), (start_hbm, start_ref),
        (alpha_hbm, alpha_ref), (act_hbm, act_ref), (cot_hbm, cot_ref),
    )
    copies = [pltpu.make_async_copy(a, b, sems.at[i]) for i, (a, b) in enumerate(pairs)]
    for copy in copies:
        copy.start()
    loads = load_weights(0, weight_hbm, weight_ref, weight_sems)
    replicas = lax.axis_size("replica")
    device = lax.axis_index("dp") * replicas + lax.axis_index("replica")
    rows, width = act_ref.shape
    place = lax.broadcasted_iota(jnp.int32, (rows, 128), 0)
    live_ref[...] = jnp.zeros((rows, 128), F32)
    for copy in copies[:3]:
        copy.wait()

    @pl.loop(0, len_ref.shape[0])
    def _(clip):
        @pl.when(own_ref[clip] == device)
        def _():
            first = start_ref[clip]
            inside = (place >= first) & (place < first + len_ref[clip])
            live_ref[...] = jnp.where(inside, 1.0, live_ref[...])

    live = jnp.tile(live_ref[...], (1, width // 128))
    for copy in copies[3:5]:
        copy.wait()
    stream_ref[...] = act_ref[...].astype(F32) * live
    write_snake(stream_ref, alpha_ref[0:1, :], snake_ref)
    copies[5].wait()
    grad_ref[...] = (cot_ref[...].astype(F32) * live).astype(BF16)
    for copy in loads:
        copy.wait()


def forward_own_kernel(layer, load, snake_ref, weight_ref, *rest):
    if load is None:
        out_ref, shifts_ref = rest
        loads = []
    else:
        weight_hbm, out_ref, loaded_ref, shifts_ref, sems = rest
        loads = load_weights(load, weight_hbm, loaded_ref, sems)
    write_shifts(snake_ref, shifts_ref, dilations[layer])
    out_ref[...] = jnp.dot(shifts_ref[...], weight_ref[0], preferred_element_type=F32)
    for copy in loads:
        copy.wait()


def forward_partner_kernel(layer, last, load, snake_ref, weight_ref, own_ref, old_ref, live_ref, *rest):
    rest = list(rest)
    alpha_ref = None if last else rest.pop(0)
    weight_hbm = None if load is None else rest.pop(0)
    result_ref = rest.pop(0)
    next_ref = None if last else rest.pop(0)
    loads = []
    if load is not None:
        loaded_ref, shifts_ref, sems = rest
        loads = load_weights(load, weight_hbm, loaded_ref, sems)
    else:
        (shifts_ref,) = rest
    write_shifts(snake_ref, shifts_ref, dilations[layer])
    part = jnp.dot(shifts_ref[...], weight_ref[1], preferred_element_type=F32)
    live = jnp.tile(live_ref[...], (1, old_ref.shape[1] // 128))
    new = (old_ref[...] + (own_ref[...] + part)) * live
    result_ref[...] = new.astype(result_ref.dtype)
    if not last:
        write_snake(result_ref, alpha_ref[layer + 1 : layer + 2, :], next_ref)
    for copy in loads:
        copy.wait()


def back_product(shifted_ref, weight_ref, side):
    half = weight_ref.shape[2]
    total = None
    for tap in range(3):
        span = slice(tap * half, (tap + 1) * half)
        part = lax.dot_general(
            shifted_ref[:, span], weight_ref[side, span, :], (((1,), (1,)), ((), ())),
            preferred_element_type=F32,
        )
        total = part if total is None else total + part
    return total


def back_partner_kernel(layer, grad_ref, weight_ref, shifted_ref, out_ref):
    write_shifts(grad_ref, shifted_ref, -dilations[layer])
    out_ref[...] = back_product(shifted_ref, weight_ref, 1).astype(BF16)


def back_own_kernel(shifted_ref, weight_ref, out_ref):
    out_ref[...] = back_product(shifted_ref, weight_ref, 0)


def combine_kernel(layer, own_ref, partner_ref, stream_ref, alphas_ref, *rest):
    if layer == 0:
        (alpha_grad_ref,) = rest
    elif len(rest) == 5:
        old_ref, live_ref, alpha_grad_ref, grad_ref, rounded_ref = rest
    else:
        old_ref, live_ref, alpha_grad_ref, rounded_ref = rest
        grad_ref = None
    alpha = alphas_ref[layer : layer + 1, :]
    inverse = 1.0 / alpha
    bound = jnp.max(jnp.abs(stream_ref[...])) * jnp.max(alpha)
    width = stream_ref.shape[1]

    def body(exact_range):
        def step_body(step, total):
            rows = pl.ds(pl.multiple_of(step * CHUNK, CHUNK), CHUNK)
            stream = stream_ref[rows, :]
            back = own_ref[rows, :] + partner_ref[rows, :].astype(F32)
            sin, cos = sine_cosine(alpha * stream, exact_range)
            double = 2.0 * sin * cos
            ratio = sin * inverse
            term = back * (stream * double * inverse - ratio * ratio)
            if layer > 0:
                live = jnp.tile(live_ref[rows, :], (1, width // 128))
                grad = (old_ref[rows, :].astype(F32) + back * (1.0 + double)) * live
                if grad_ref is not None:
                    grad_ref[rows, :] = grad
                rounded_ref[rows, :] = grad.astype(BF16)
            return total + jnp.sum(term.reshape(CHUNK // 8, 8, width), axis=0)

        total = lax.fori_loop(0, stream_ref.shape[0] // CHUNK, step_body, jnp.zeros((8, width), F32))
        alpha_grad_ref[...] = jnp.sum(total, axis=0, keepdims=True)

    by_range(bound, body)


def block_place(pieces, slice_index, part):
    apart = jnp.bitwise_xor(slice_index, lax.axis_index("dp"))
    order = (2 * pieces, 0, 2 * pieces + 1, 1)
    return 2 * part + jnp.where(
        apart == 0, order[0], jnp.where(apart == 1, order[1], jnp.where(apart == 2, order[2], order[3]))
    )


def weight_kernel(own_ref, partner_ref, shifted_ref, out_ref, turned_ref):
    half = own_ref.shape[1]
    chan = lax.axis_index("chan")
    for ref, side in ((own_ref, chan), (partner_ref, 1 - chan)):
        turned_ref[pl.ds(pl.multiple_of(side * half, half), half), :] = ref[...].T
    for tap in range(3):
        span = slice(tap * half, (tap + 1) * half)
        out_ref[:, span] = jnp.dot(turned_ref[...], shifted_ref[:, span], preferred_element_type=F32).astype(BF16)


def place_rows(pieces, rows_of, side, target_ref, columns):
    size = rows_of.shape[0] // (2 * pieces)
    for local in range(2):
        for part in range(pieces):
            begin = pl.multiple_of(block_place(pieces, side * 2 + local, part) * size, size)
            low = (local * pieces + part) * size
            target_ref[pl.ds(begin, size), columns] = rows_of[low : low + size, :]


def pick_parts(turned_ref, part, size):
    begin = pl.multiple_of(part * size, size)
    return [turned_ref[pl.ds(local * 2 * size + begin, size), :] for local in range(2)]


def turn_whole_kernel(own_ref, partner_ref, out_ref, turned_ref):
    size = own_ref.shape[1] // 4
    chan = lax.axis_index("chan")
    for ref, side in ((own_ref, chan), (partner_ref, 1 - chan)):
        turned_ref[...] = ref[...].T
        for local, piece in enumerate(pick_parts(turned_ref, 1 - lax.axis_index("replica"), size)):
            out_ref[pl.ds(pl.multiple_of((2 * side + local) * size, size), size), :] = piece


def turn_kernel(*refs):
    snakes, out_ref, turned_ref = refs[:-2], refs[-2], refs[-1]
    size = snakes[0].shape[1] // 4
    for index, ref in enumerate(snakes):
        turned_ref[...] = ref[...].T
        for local, piece in enumerate(pick_parts(turned_ref, 1 - lax.axis_index("replica"), size)):
            low = (2 * index + local) * size
            out_ref[low : low + size, :] = piece


def own_rows_kernel(pieces, own_ref, partner_ref, out_ref, half_ref):
    chan = lax.axis_index("chan")
    mine = lax.axis_index("replica")
    for ref, side in ((own_ref, chan), (partner_ref, 1 - chan)):
        half_ref[...] = ref[...].T
        both = jnp.concatenate(pick_parts(half_ref, mine, ref.shape[1] // 4), 0)
        place_rows(pieces, both, side, out_ref, slice(None))


def far_kernel(layer, grad_ref, out_ref):
    write_shifts(grad_ref, out_ref, -dilations[layer])


def write_carried(values, out_ref, low):
    first = values.astype(BF16).astype(F32)
    second = (values - first).astype(BF16).astype(F32)
    third = values - first - second
    shape = (CARRIED, values.shape[1])
    row = lax.broadcasted_iota(jnp.int32, shape, 0)
    block = jnp.where(row == 0, first, jnp.where(row == 1, second, jnp.where(row == 2, third, 0.0)))
    out_ref[low : low + CARRIED, :] = block.astype(BF16)


def read_carried(ref, low):
    block = ref[low : low + CARRIED, :].astype(F32)
    return (block[0:1, :] + block[1:2, :]) + block[2:3, :]


def paired_weight_kernel(pieces, low, carry, own_ref, shifted_ref, across_ref, across_other_ref, far_ref, *rest):
    if carry:
        write_carried(jnp.concatenate([ref[...] for ref in rest[:carry]], 1), rest[carry], own_ref.shape[0] // 2)
        rest = rest[carry:]
    outs, turned_ref = rest[:-1], rest[-1]
    half = own_ref.shape[0]
    chan = lax.axis_index("chan")
    whole = across_ref.shape[0] == half
    sources = ((across_ref, 0, 0), (across_ref, 1, half // 2)) if whole else (
        (across_ref, chan, 0), (across_other_ref, 1 - chan, 0))
    for ref, side, low in sources:
        place_rows(pieces, ref[low : low + half // 2, :], side, turned_ref, slice(None))
    for tap in range(3):
        span = slice(tap * half, (tap + 1) * half)
        product = jnp.dot(own_ref[...], shifted_ref[:, span], preferred_element_type=F32)
        product += jnp.dot(turned_ref[...], far_ref[:, span], preferred_element_type=F32)
        product = product.astype(BF16)
        size = product.shape[0] // len(outs)
        for place, ref in enumerate(outs):
            ref[0:size, span] = product[place * size : (place + 1) * size, :]


def finish_kernel(paired, held, carry, counts, *refs):
    total_ref, sems = refs[-2:]
    refs = list(refs[1:-2] if held else refs[:-2])
    if carry:
        alpha_ref = refs.pop()
        alpha_mine = refs.pop(0)
    out_ref = refs.pop()
    half = total_ref.shape[3]
    rows_of = total_ref.shape[2] // (2 if paired else 1)
    copies = []
    for index, (layer, pieces) in enumerate(counts):
        for part in range(pieces):
            mine_ref, other_ref = refs.pop(0), refs.pop(0)
            size = rows_of
            if carry and other_ref.shape[0] > size:
                alpha = alpha_mine[...] + read_carried(other_ref, size)
                for place in range(3):
                    alpha_ref[place : place + 1, :] = alpha[:, place * half : (place + 1) * half]
            for tap in range(3):
                span = slice(tap * half, (tap + 1) * half)
                mine, other = mine_ref[0:size, span].astype(F32), other_ref[0:size, span].astype(F32)
                if paired:
                    begin = lax.axis_index("replica") * (size * pieces)
                    for values, start in ((mine, begin), (other, size * pieces - begin)):
                        place = pl.multiple_of(start + part * size, size)
                        total_ref[index, tap, pl.ds(place, size), :] = values
                else:
                    total_ref[index, tap] = mine + other
        copies.append(pltpu.make_async_copy(total_ref.at[index], out_ref.at[layer], sems.at[index]))
        copies[-1].start()
    for copy in copies:
        copy.wait()


def fold_kernel(carry, keep, got, *rest):
    if carry:
        mine, rest = rest[:carry], rest[carry:]
        send, sum_ref = rest
    else:
        (send,) = rest
    rows = keep.shape[0] // 2
    send[0:rows, :] = (keep[rows:, :].astype(F32) + got[rows : 2 * rows, :].astype(F32)).astype(BF16)
    if carry:
        values = jnp.concatenate([ref[...] for ref in mine], 1) + read_carried(got, 2 * rows)
        sum_ref[...] = values
        write_carried(values, send, rows)


def total_kernel(carry, keep, got, late, *rest):
    if carry:
        mine, out_ref, sum_ref = rest
    else:
        (out_ref,) = rest
    rows = keep.shape[0] // 2
    total = keep[0:rows, :].astype(F32) + got[0:rows, :].astype(F32) + late[0:rows, :].astype(F32)
    out_ref[0:rows, :] = total.astype(BF16)
    if carry:
        values = mine[...] + read_carried(late, rows)
        sum_ref[...] = values
        write_carried(values, out_ref, rows)


def stack_kernel(*refs):
    for index, ref in enumerate(refs[:-1]):
        refs[-1][index : index + 1, :] = ref[...]


def add_kernel(left, right, out_ref):
    out_ref[...] = left[...] + right[...]


def struct(shape, dtype):
    return jax.ShapeDtypeStruct(shape, dtype)


def after(value, other):
    return value if other is None else lax.optimization_barrier((value, other))[0]


class Sequence:
    def __init__(self):
        self.latest = None
        self.weight = 10

    def hold(self, value):
        return after(value, self.latest)

    def call(self, kernel, name, ins, outs, scratch, flops, *args, specs=None, aliases=None):
        single = not isinstance(outs, list)
        size = sum(a.size * a.dtype.itemsize for a in args if a.size < 2000000)
        size += sum(math.prod(o.shape) * o.dtype.itemsize for o in ([outs] if single else outs))
        args = [pltpu.with_memory_space_constraint(a, pltpu.HBM) if i == 1 else a for i, a in zip(ins, args)]
        if self.latest is not None:
            held = ins.index(0)
            args[held] = self.hold(args[held])
        result = pl.pallas_call(
            kernel,
            in_specs=[ANY_HBM if i else IN_VMEM for i in ins],
            out_specs=specs or (IN_VMEM if single else [IN_VMEM] * len(outs)),
            out_shape=outs,
            scratch_shapes=scratch,
            input_output_aliases=aliases or {},
            compiler_params=pltpu.CompilerParams(vmem_limit_bytes=24 * 1024 * 1024),
            cost_estimate=pl.CostEstimate(flops=int(flops * self.weight), bytes_accessed=int(size * self.weight), transcendentals=0),
            name=name,
        )(*args)
        self.latest = result if single else result[-1]
        return result


def swap(x, axis, other):
    return lax.ppermute(x, axis, [(i, other(i)) for i in range(lax.axis_size(axis))])


def across_chan(x):
    return swap(x, "chan", lambda i: i ^ 1)


def across_replica(x):
    return swap(x, "replica", lambda i: i ^ 1)


def on_device(activations, cotangent, conv_weights, snake_alpha, seg_lengths, seg_owner, seg_start):
    rows, half = activations.shape
    layers, taps, channels, _ = conv_weights.shape
    top = layers - 1
    fast = lax.axis_size("dp") == 4 and lax.axis_size("replica") == 2
    counts = [1] * layers
    carrier = 1 if fast else None
    weight = {}
    tile, triple = (rows, half), (rows, taps * half)
    flops = 2 * rows * half * half * taps
    sequence = Sequence()
    streams, mine, partners, owns = [], [], {}, {}
    rounded, shifted, arrived, back_owns, far = {}, {}, {}, {}, {}
    across, across_other = {}, {}
    alpha_parts = [None] * layers
    kept, got, late, summed, crossed = {}, {}, {}, {}, {}

    loaded = (2, taps * half, half)
    sems = DMA((2 * taps,))

    def forward_own(layer, load=None):
        outs, args, ins = struct(tile, F32), [mine[layer], weight[layer]], [0, 0]
        scratch = [pltpu.VMEM(triple, BF16)]
        if load is not None:
            outs, args, ins = [outs, struct(loaded, BF16)], args + [conv_weights], ins + [1]
            scratch.append(sems)
        result = sequence.call(
            functools.partial(forward_own_kernel, layer, load), "forward_own", ins, outs, scratch, flops, *args
        )
        if load is None:
            owns[layer] = result
        else:
            owns[layer], weight[load] = result

    def forward_partner(layer, load=None):
        last = layer == top
        ins, args = [0] * 5, [partners[layer], weight[layer], owns[layer], streams[layer], live]
        outs = [struct(tile, BF16)] if last else [struct(tile, F32), struct(tile, BF16)]
        scratch = [pltpu.VMEM(triple, BF16)]
        if not last:
            ins, args = ins + [0], args + [alphas]
        if load is not None:
            ins, args, outs = ins + [1], args + [conv_weights], outs + [struct(loaded, BF16)]
            scratch.append(sems)
        result = sequence.call(
            functools.partial(forward_partner_kernel, layer, last, load), "forward_partner", ins, outs, scratch,
            flops, *args,
        )
        if load is not None:
            weight[load] = result[-1]
        if last:
            return result[0]
        streams.append(result[0])
        mine.append(result[1])
        partners[layer + 1] = across_chan(result[1])

    def back_partner(layer):
        shifted[layer], part = sequence.call(
            functools.partial(back_partner_kernel, layer), "back_partner", [0, 0],
            [struct(triple, BF16), struct(tile, BF16)], [], flops, rounded[layer + 1], weight[layer],
        )
        arrived[layer] = across_chan(part)

    def back_own(layer):
        back_owns[layer] = sequence.call(
            back_own_kernel, "back_own", [0, 0], struct(tile, F32), [], flops, shifted[layer], weight[layer]
        )

    def send_gradient(layer):
        if fast:
            far[layer] = across_replica(sequence.hold(rounded[layer + 1]))

    def combine(layer, grad):
        args = [back_owns[layer], arrived[layer], streams[layer], alphas]
        outs = [struct((1, half), F32)]
        if layer > 0:
            args += [grad, live]
            outs += [struct(tile, F32)] * (layer > 1) + [struct(tile, BF16)]
        result = sequence.call(
            functools.partial(combine_kernel, layer), "combine", [0] * len(args), outs, [], 60 * rows * half, *args
        )
        alpha_parts[layer] = result[0]
        if layer > 0:
            rounded[layer] = result[-1]
            return result[1]

    def turn(*chosen):
        if fast:
            moved_rows = across_replica(sequence.call(
                turn_kernel, "turn", [0] * len(chosen), struct((len(chosen) * half // 2, rows), BF16),
                [pltpu.VMEM((half, rows), BF16)], 10 * rows * half, *[mine[layer] for layer in chosen],
            ))
            for index, layer in enumerate(chosen):
                across[layer] = (moved_rows, index * half // 2)

    def turn_whole(layer):
        if fast:
            across_other[layer] = across_replica(sequence.call(
                turn_whole_kernel, "turn_whole", [0, 0], struct((half, rows), BF16),
                [pltpu.VMEM((half, rows), BF16)], 10 * rows * half, mine[layer], partners[layer],
            ))
            across[layer] = (across_other[layer], 0)

    def share(*chosen):
        if fast:
            shared = across_chan(sequence.hold(across[chosen[0]][0]))
            for layer in chosen:
                across_other[layer] = shared

    own_turned, far_shifted = {}, {}

    def own_rows(layer):
        if fast:
            own_turned[layer] = sequence.call(
                functools.partial(own_rows_kernel, counts[layer]), "own_rows", [0, 0], struct((half, rows), BF16),
                [pltpu.VMEM((half, rows), BF16)], 10 * rows * half, mine[layer], partners[layer],
            )

    def far_rows(layer):
        if fast:
            far_shifted[layer] = sequence.call(
                functools.partial(far_kernel, layer), "far_rows", [0], struct(triple, BF16), [],
                10 * rows * half, far[layer],
            )

    def weights(layer):
        if not fast:
            out = sequence.call(
                weight_kernel, "weight", [0] * 3, struct((channels, taps * half), BF16),
                [pltpu.VMEM((channels, rows), BF16)], 2 * flops, mine[layer], partners[layer], shifted[layer],
            )
            part = lax.psum_scatter(out, "dp", scatter_dimension=0, tiled=True)
            summed[layer, 0] = lax.psum(part, "replica")
            crossed[layer, 0] = jnp.zeros_like(part)
            return
        pieces, depth = counts[layer], channels // 4 // counts[layer]
        carried = alpha_parts if layer == carrier else []
        outs = [struct((depth, taps * half), BF16)] * (2 * pieces)
        if carried:
            outs[0] = struct((depth + CARRIED, taps * half), BF16)
        args = [own_turned[layer], shifted[layer], across[layer][0], across_other[layer], far_shifted[layer], *carried]
        out = sequence.call(
            functools.partial(paired_weight_kernel, pieces, across[layer][1], len(carried)), "paired_weight",
            [0] * len(args), outs, [pltpu.VMEM((half, rows), BF16)], 2 * flops, *args,
        )
        for part in range(pieces):
            got[layer, part] = swap(out[part], "dp", lambda i: i ^ 1)
            kept[layer, part] = out[pieces + part]

    carry_sum = [None]

    def fold(layer, part=0):
        if not fast:
            return
        keep, came = kept[layer, part], got[layer, part]
        depth, carried = keep.shape[0] // 2, alpha_parts if layer == carrier else []
        outs = [struct((depth + CARRIED * bool(carried), taps * half), BF16)]
        if carried:
            outs.append(struct((1, taps * half), F32))
        result = sequence.call(
            functools.partial(fold_kernel, len(carried)), "fold", [0] * (2 + len(carried)), outs, [], keep.size,
            keep, came, *carried,
        )
        if carried:
            carry_sum[0] = result[1]
        late[layer, part] = swap(result[0], "dp", lambda i: i ^ 2)

    def total(layer, part=0):
        if not fast:
            return
        keep, came, last = kept[layer, part], got[layer, part], late[layer, part]
        outs, args = [struct(last.shape, BF16)], [keep, came, last]
        if layer == carrier:
            outs.append(struct((1, taps * half), F32))
            args.append(carry_sum[0])
        result = sequence.call(
            functools.partial(total_kernel, layer == carrier), "total", [0] * len(args), outs, [], 2 * flops, *args
        )
        if layer == carrier:
            carry_sum[0] = result[1]
        summed[layer, part] = result[0]

    def cross(layer, part=0):
        if fast:
            crossed[layer, part] = across_replica(sequence.hold(summed[layer, part]))

    stream, snaked, grad, live, alphas, weight[0] = sequence.call(
        prep_kernel, "prep", [1] * 7,
        [struct(tile, F32), struct(tile, BF16), struct(tile, BF16), struct((rows, 128), F32),
         struct(snake_alpha.shape, F32), struct(loaded, BF16)],
        [pltpu.SMEM(seg_lengths.shape, jnp.int32)] * 3 + [pltpu.VMEM(tile, BF16)] * 2 + [DMA((6,)), sems],
        40 * rows * half,
        seg_lengths, seg_owner, seg_start, activations, cotangent, snake_alpha, conv_weights,
    )
    streams.append(stream)
    mine.append(snaked)
    partners[0] = across_chan(snaked)
    rounded[layers] = grad
    depth = channels // lax.axis_size("dp")

    def finish(chosen, before=None):
        pairs = [] if before is None else [before]
        carry = carrier in chosen
        if carry:
            pairs.append(carry_sum[0])
        for layer in chosen:
            for part in range(counts[layer]):
                pairs += [summed[layer, part], crossed[layer, part]]
        out = struct((layers, taps, depth, half), F32)
        return sequence.call(
            functools.partial(
                finish_kernel, fast, before is not None, carry, tuple((layer, counts[layer]) for layer in chosen)
            ),
            "finish", [2] * (before is not None) + [0] * (len(pairs) - (before is not None)),
            [out, struct((layers, half), F32)] if carry else [out],
            [pltpu.VMEM((len(chosen), taps, depth, half), F32), DMA((len(chosen),))],
            layers * taps * depth * half, *pairs, specs=[ANY_HBM] + [IN_VMEM] * carry,
            aliases={0: 0} if before is not None else None,
        )

    rounds = [("replica", 1 << bit) for bit in range(8) if lax.axis_size("replica") >> (bit + 1)]
    rounds += [("dp", 1 << bit) for bit in range(8) if lax.axis_size("dp") >> (bit + 1)]
    arrivals = []

    def alpha_round():
        if arrivals:
            value = sequence.call(
                add_kernel, "add", [0, 0], struct((layers, half), F32), [], layers * half, *arrivals.pop()
            )
        else:
            value = sequence.call(
                stack_kernel, "stack", [0] * layers, struct((layers, half), F32), [], layers * half, *alpha_parts
            )
        if not rounds:
            return value
        axis, apart = rounds.pop(0)
        arrivals.append((value, swap(value, axis, lambda place: place ^ apart)))

    forward_own(0, load=2)
    send_gradient(2)
    forward_partner(0, load=1)
    back_partner(2)
    forward_own(1)
    forward_partner(1)
    turn(2)
    back_own(2)
    grad = combine(2, grad)
    send_gradient(1)
    far_rows(2)
    own_rows(2)
    turn(1)
    back_partner(1)
    share(2)
    back_own(1)
    combine(1, grad)
    weights(2)
    back_partner(0)
    back_own(0)
    sequence.weight = 10
    combine(0, None)
    own_rows(1)
    far_rows(1)
    own_rows(0)
    share(1)
    turn_whole(0)
    send_gradient(0)
    forward_own(2)
    residual_out = forward_partner(2)
    sequence.weight = 0.01
    weights(1)
    fold(2)
    far_rows(0)
    sequence.weight = 0.01
    weights(0)
    sequence.weight = 3
    fold(1)
    total(2)
    cross(2)
    fold(0)
    total(1)
    cross(1)
    total(0)
    cross(0)
    if fast:
        weight_grads, alpha_grads = finish((2, 1))
        (weight_grads,) = finish((0,), weight_grads)
    else:
        alpha_grads = alpha_round()
        while alpha_grads is None:
            alpha_grads = alpha_round()
        (weight_grads,) = finish((2, 1, 0))
    return (residual_out, weight_grads, alpha_grads)


def solution(mesh):
    return jax.shard_map(
        on_device,
        mesh=mesh,
        in_specs=(
            P(("groups", "dp", "replica"), "chan"),
            P(("groups", "dp", "replica"), "chan"),
            P(None, None, None, "chan"),
            P(None, "chan"),
            P("groups"),
            P("groups"),
            P("groups"),
        ),
        out_specs=(
            P(("groups", "dp", "replica"), "chan"),
            P("groups", None, "dp", "chan"),
            P("groups", "chan"),
        ),
        check_vma=False,
    )
```

```python
import functools
import math

import jax
import jax.numpy as jnp
from jax import lax
from jax.experimental import pallas as pl
from jax.experimental.pallas import tpu as pltpu
from jax.sharding import PartitionSpec as P

dilations = (1, 3, 5)
F32, BF16 = jnp.float32, jnp.bfloat16
ANY_HBM = pl.BlockSpec(memory_space=pltpu.HBM)
IN_VMEM = pl.BlockSpec(memory_space=pltpu.VMEM)
DMA = pltpu.SemaphoreType.DMA
PI_PARTS = (3.140625, 9.67502593994140625e-4, 1.509957990978376432e-7)
SIN_TERMS = (-1.0 / 39916800, 1.0 / 362880, -1.0 / 5040, 1.0 / 120, -1.0 / 6)
COS_TERMS = (1.0 / 479001600, -1.0 / 3628800, 1.0 / 40320, -1.0 / 720, 1.0 / 24, -0.5)
RANGE = 8192.0
CHUNK = 64
CARRIED = 16


def horner(terms, x):
    total = jnp.full_like(x, terms[0])
    for term in terms[1:]:
        total = total * x + term
    return total


def reduced(angle):
    turns = jnp.round(angle * (1.0 / 3.14159265358979))
    for part in PI_PARTS:
        angle = angle - turns * part
    return angle


def sine(angle, exact_range):
    if not exact_range:
        return jnp.sin(angle)
    rest = reduced(angle)
    square = rest * rest
    return rest + rest * (square * horner(SIN_TERMS, square))


def sine_cosine(angle, exact_range):
    if not exact_range:
        return jnp.sin(angle), jnp.cos(angle)
    rest = reduced(angle)
    square = rest * rest
    return (
        rest + rest * (square * horner(SIN_TERMS, square)),
        1.0 + square * horner(COS_TERMS, square),
    )


def by_range(bound, body):
    @pl.when(bound < RANGE)
    def _():
        body(True)

    @pl.when(bound >= RANGE)
    def _():
        body(False)


def write_snake(stream_ref, alpha, out_ref):
    inverse = 1.0 / alpha
    bound = jnp.max(jnp.abs(stream_ref[...])) * jnp.max(alpha)

    def body(exact_range):
        @pl.loop(0, stream_ref.shape[0] // CHUNK)
        def _(step):
            rows = pl.ds(pl.multiple_of(step * CHUNK, CHUNK), CHUNK)
            stream = stream_ref[rows, :]
            wave = sine(alpha * stream, exact_range)
            out_ref[rows, :] = (stream + wave * wave * inverse).astype(BF16)

    by_range(bound, body)


def moved(values, offset):
    if offset == 0:
        return values
    rows = values.shape[0]
    place = lax.broadcasted_iota(jnp.int32, values.shape, 0)
    turned = pltpu.roll(values, (-offset) % rows, 0)
    inside = place < rows - offset if offset > 0 else place >= -offset
    return jnp.where(inside, turned, 0.0)


def write_shifts(values_ref, out_ref, dilation):
    width = values_ref.shape[1]
    values = values_ref[...].astype(F32)
    for tap in range(3):
        out_ref[:, tap * width : (tap + 1) * width] = moved(values, (tap - 1) * dilation).astype(BF16)


def chan_begin(side, half):
    chan = lax.axis_index("chan")
    return pl.multiple_of((chan if side == 0 else 1 - chan) * half, half)


def load_weights(layer, weight_hbm, weight_ref, sems):
    half = weight_hbm.shape[3]
    loads = []
    for side in range(2):
        for tap in range(3):
            source = weight_hbm.at[layer, tap, pl.ds(chan_begin(side, half), half), :]
            target = weight_ref.at[side, pl.ds(tap * half, half), :]
            loads.append(pltpu.make_async_copy(source, target, sems.at[len(loads)]))
    for copy in loads:
        copy.start()
    return loads


def prep_kernel(
    len_hbm, own_hbm, start_hbm, act_hbm, cot_hbm, alpha_hbm, weight_hbm,
    stream_ref, snake_ref, grad_ref, live_ref, alpha_ref, weight_ref,
    len_ref, own_ref, start_ref, act_ref, cot_ref, sems, weight_sems,
):
    pairs = (
        (len_hbm, len_ref), (own_hbm, own_ref), (start_hbm, start_ref),
        (alpha_hbm, alpha_ref), (act_hbm, act_ref), (cot_hbm, cot_ref),
    )
    copies = [pltpu.make_async_copy(a, b, sems.at[i]) for i, (a, b) in enumerate(pairs)]
    for copy in copies:
        copy.start()
    loads = load_weights(0, weight_hbm, weight_ref, weight_sems)
    replicas = lax.axis_size("replica")
    device = lax.axis_index("dp") * replicas + lax.axis_index("replica")
    rows, width = act_ref.shape
    place = lax.broadcasted_iota(jnp.int32, (rows, 128), 0)
    live_ref[...] = jnp.zeros((rows, 128), F32)
    for copy in copies[:3]:
        copy.wait()

    @pl.loop(0, len_ref.shape[0])
    def _(clip):
        @pl.when(own_ref[clip] == device)
        def _():
            first = start_ref[clip]
            inside = (place >= first) & (place < first + len_ref[clip])
            live_ref[...] = jnp.where(inside, 1.0, live_ref[...])

    live = jnp.tile(live_ref[...], (1, width // 128))
    for copy in copies[3:5]:
        copy.wait()
    stream_ref[...] = act_ref[...].astype(F32) * live
    write_snake(stream_ref, alpha_ref[0:1, :], snake_ref)
    copies[5].wait()
    grad_ref[...] = (cot_ref[...].astype(F32) * live).astype(BF16)
    for copy in loads:
        copy.wait()


def forward_own_kernel(layer, load, snake_ref, weight_ref, *rest):
    if load is None:
        out_ref, shifts_ref = rest
        loads = []
    else:
        weight_hbm, out_ref, loaded_ref, shifts_ref, sems = rest
        loads = load_weights(load, weight_hbm, loaded_ref, sems)
    write_shifts(snake_ref, shifts_ref, dilations[layer])
    out_ref[...] = jnp.dot(shifts_ref[...], weight_ref[0], preferred_element_type=F32)
    for copy in loads:
        copy.wait()


def forward_partner_kernel(layer, last, load, snake_ref, weight_ref, own_ref, old_ref, live_ref, *rest):
    rest = list(rest)
    alpha_ref = None if last else rest.pop(0)
    weight_hbm = None if load is None else rest.pop(0)
    result_ref = rest.pop(0)
    next_ref = None if last else rest.pop(0)
    loads = []
    if load is not None:
        loaded_ref, shifts_ref, sems = rest
        loads = load_weights(load, weight_hbm, loaded_ref, sems)
    else:
        (shifts_ref,) = rest
    write_shifts(snake_ref, shifts_ref, dilations[layer])
    part = jnp.dot(shifts_ref[...], weight_ref[1], preferred_element_type=F32)
    live = jnp.tile(live_ref[...], (1, old_ref.shape[1] // 128))
    new = (old_ref[...] + (own_ref[...] + part)) * live
    result_ref[...] = new.astype(result_ref.dtype)
    if not last:
        write_snake(result_ref, alpha_ref[layer + 1 : layer + 2, :], next_ref)
    for copy in loads:
        copy.wait()


def back_product(shifted_ref, weight_ref, side):
    half = weight_ref.shape[2]
    total = None
    for tap in range(3):
        span = slice(tap * half, (tap + 1) * half)
        part = lax.dot_general(
            shifted_ref[:, span], weight_ref[side, span, :], (((1,), (1,)), ((), ())),
            preferred_element_type=F32,
        )
        total = part if total is None else total + part
    return total


def back_partner_kernel(layer, grad_ref, weight_ref, shifted_ref, out_ref):
    write_shifts(grad_ref, shifted_ref, -dilations[layer])
    out_ref[...] = back_product(shifted_ref, weight_ref, 1).astype(BF16)


def back_own_kernel(shifted_ref, weight_ref, out_ref):
    out_ref[...] = back_product(shifted_ref, weight_ref, 0)


def combine_kernel(layer, own_ref, partner_ref, stream_ref, alphas_ref, *rest):
    if layer == 0:
        (alpha_grad_ref,) = rest
    elif len(rest) == 5:
        old_ref, live_ref, alpha_grad_ref, grad_ref, rounded_ref = rest
    else:
        old_ref, live_ref, alpha_grad_ref, rounded_ref = rest
        grad_ref = None
    alpha = alphas_ref[layer : layer + 1, :]
    inverse = 1.0 / alpha
    bound = jnp.max(jnp.abs(stream_ref[...])) * jnp.max(alpha)
    width = stream_ref.shape[1]

    def body(exact_range):
        def step_body(step, total):
            rows = pl.ds(pl.multiple_of(step * CHUNK, CHUNK), CHUNK)
            stream = stream_ref[rows, :]
            back = own_ref[rows, :] + partner_ref[rows, :].astype(F32)
            sin, cos = sine_cosine(alpha * stream, exact_range)
            double = 2.0 * sin * cos
            ratio = sin * inverse
            term = back * (stream * double * inverse - ratio * ratio)
            if layer > 0:
                live = jnp.tile(live_ref[rows, :], (1, width // 128))
                grad = (old_ref[rows, :].astype(F32) + back * (1.0 + double)) * live
                if grad_ref is not None:
                    grad_ref[rows, :] = grad
                rounded_ref[rows, :] = grad.astype(BF16)
            return total + jnp.sum(term.reshape(CHUNK // 8, 8, width), axis=0)

        total = lax.fori_loop(0, stream_ref.shape[0] // CHUNK, step_body, jnp.zeros((8, width), F32))
        alpha_grad_ref[...] = jnp.sum(total, axis=0, keepdims=True)

    by_range(bound, body)


def block_place(pieces, slice_index, part):
    apart = jnp.bitwise_xor(slice_index, lax.axis_index("dp"))
    order = (2 * pieces, 0, 2 * pieces + 1, 1)
    return 2 * part + jnp.where(
        apart == 0, order[0], jnp.where(apart == 1, order[1], jnp.where(apart == 2, order[2], order[3]))
    )


def weight_kernel(own_ref, partner_ref, shifted_ref, out_ref, turned_ref):
    half = own_ref.shape[1]
    chan = lax.axis_index("chan")
    for ref, side in ((own_ref, chan), (partner_ref, 1 - chan)):
        turned_ref[pl.ds(pl.multiple_of(side * half, half), half), :] = ref[...].T
    for tap in range(3):
        span = slice(tap * half, (tap + 1) * half)
        out_ref[:, span] = jnp.dot(turned_ref[...], shifted_ref[:, span], preferred_element_type=F32).astype(BF16)


def place_rows(pieces, rows_of, side, target_ref, columns):
    size = rows_of.shape[0] // (2 * pieces)
    for local in range(2):
        for part in range(pieces):
            begin = pl.multiple_of(block_place(pieces, side * 2 + local, part) * size, size)
            low = (local * pieces + part) * size
            target_ref[pl.ds(begin, size), columns] = rows_of[low : low + size, :]


def pick_parts(turned_ref, part, size):
    begin = pl.multiple_of(part * size, size)
    return [turned_ref[pl.ds(local * 2 * size + begin, size), :] for local in range(2)]


def turn_whole_kernel(own_ref, partner_ref, out_ref, turned_ref):
    size = own_ref.shape[1] // 4
    chan = lax.axis_index("chan")
    for ref, side in ((own_ref, chan), (partner_ref, 1 - chan)):
        turned_ref[...] = ref[...].T
        for local, piece in enumerate(pick_parts(turned_ref, 1 - lax.axis_index("replica"), size)):
            out_ref[pl.ds(pl.multiple_of((2 * side + local) * size, size), size), :] = piece


def turn_kernel(*refs):
    snakes, out_ref, turned_ref = refs[:-2], refs[-2], refs[-1]
    size = snakes[0].shape[1] // 4
    for index, ref in enumerate(snakes):
        turned_ref[...] = ref[...].T
        for local, piece in enumerate(pick_parts(turned_ref, 1 - lax.axis_index("replica"), size)):
            low = (2 * index + local) * size
            out_ref[low : low + size, :] = piece


def own_rows_kernel(pieces, own_ref, partner_ref, out_ref, half_ref):
    chan = lax.axis_index("chan")
    mine = lax.axis_index("replica")
    for ref, side in ((own_ref, chan), (partner_ref, 1 - chan)):
        half_ref[...] = ref[...].T
        both = jnp.concatenate(pick_parts(half_ref, mine, ref.shape[1] // 4), 0)
        place_rows(pieces, both, side, out_ref, slice(None))


def far_kernel(layer, grad_ref, out_ref):
    write_shifts(grad_ref, out_ref, -dilations[layer])


def write_carried(values, out_ref, low):
    first = values.astype(BF16).astype(F32)
    second = (values - first).astype(BF16).astype(F32)
    third = values - first - second
    shape = (CARRIED, values.shape[1])
    row = lax.broadcasted_iota(jnp.int32, shape, 0)
    block = jnp.where(row == 0, first, jnp.where(row == 1, second, jnp.where(row == 2, third, 0.0)))
    out_ref[low : low + CARRIED, :] = block.astype(BF16)


def read_carried(ref, low):
    block = ref[low : low + CARRIED, :].astype(F32)
    return (block[0:1, :] + block[1:2, :]) + block[2:3, :]


def paired_weight_kernel(pieces, low, carry, own_ref, shifted_ref, across_ref, across_other_ref, far_ref, *rest):
    if carry:
        write_carried(jnp.concatenate([ref[...] for ref in rest[:carry]], 1), rest[carry], own_ref.shape[0] // 2)
        rest = rest[carry:]
    outs, turned_ref = rest[:-1], rest[-1]
    half = own_ref.shape[0]
    chan = lax.axis_index("chan")
    whole = across_ref.shape[0] == half
    sources = ((across_ref, 0, 0), (across_ref, 1, half // 2)) if whole else (
        (across_ref, chan, 0), (across_other_ref, 1 - chan, 0))
    for ref, side, low in sources:
        place_rows(pieces, ref[low : low + half // 2, :], side, turned_ref, slice(None))
    for tap in range(3):
        span = slice(tap * half, (tap + 1) * half)
        product = jnp.dot(own_ref[...], shifted_ref[:, span], preferred_element_type=F32)
        product += jnp.dot(turned_ref[...], far_ref[:, span], preferred_element_type=F32)
        product = product.astype(BF16)
        size = product.shape[0] // len(outs)
        for place, ref in enumerate(outs):
            ref[0:size, span] = product[place * size : (place + 1) * size, :]


def finish_kernel(paired, held, carry, counts, *refs):
    total_ref, sems = refs[-2:]
    refs = list(refs[1:-2] if held else refs[:-2])
    if carry:
        alpha_ref = refs.pop()
        alpha_mine = refs.pop(0)
    out_ref = refs.pop()
    half = total_ref.shape[3]
    rows_of = total_ref.shape[2] // (2 if paired else 1)
    copies = []
    for index, (layer, pieces) in enumerate(counts):
        for part in range(pieces):
            mine_ref, other_ref = refs.pop(0), refs.pop(0)
            size = rows_of
            if carry and other_ref.shape[0] > size:
                alpha = alpha_mine[...] + read_carried(other_ref, size)
                for place in range(3):
                    alpha_ref[place : place + 1, :] = alpha[:, place * half : (place + 1) * half]
            for tap in range(3):
                span = slice(tap * half, (tap + 1) * half)
                mine, other = mine_ref[0:size, span].astype(F32), other_ref[0:size, span].astype(F32)
                if paired:
                    begin = lax.axis_index("replica") * (size * pieces)
                    for values, start in ((mine, begin), (other, size * pieces - begin)):
                        place = pl.multiple_of(start + part * size, size)
                        total_ref[index, tap, pl.ds(place, size), :] = values
                else:
                    total_ref[index, tap] = mine + other
        copies.append(pltpu.make_async_copy(total_ref.at[index], out_ref.at[layer], sems.at[index]))
        copies[-1].start()
    for copy in copies:
        copy.wait()


def fold_kernel(carry, keep, got, *rest):
    if carry:
        mine, rest = rest[:carry], rest[carry:]
        send, sum_ref = rest
    else:
        (send,) = rest
    rows = keep.shape[0] // 2
    send[0:rows, :] = (keep[rows:, :].astype(F32) + got[rows : 2 * rows, :].astype(F32)).astype(BF16)
    if carry:
        values = jnp.concatenate([ref[...] for ref in mine], 1) + read_carried(got, 2 * rows)
        sum_ref[...] = values
        write_carried(values, send, rows)


def total_kernel(carry, keep, got, late, *rest):
    if carry:
        mine, out_ref, sum_ref = rest
    else:
        (out_ref,) = rest
    rows = keep.shape[0] // 2
    total = keep[0:rows, :].astype(F32) + got[0:rows, :].astype(F32) + late[0:rows, :].astype(F32)
    out_ref[0:rows, :] = total.astype(BF16)
    if carry:
        values = mine[...] + read_carried(late, rows)
        sum_ref[...] = values
        write_carried(values, out_ref, rows)


def stack_kernel(*refs):
    for index, ref in enumerate(refs[:-1]):
        refs[-1][index : index + 1, :] = ref[...]


def add_kernel(left, right, out_ref):
    out_ref[...] = left[...] + right[...]


def struct(shape, dtype):
    return jax.ShapeDtypeStruct(shape, dtype)


def after(value, other):
    return value if other is None else lax.optimization_barrier((value, other))[0]


class Sequence:
    def __init__(self):
        self.latest = None
        self.weight = 10

    def hold(self, value):
        return after(value, self.latest)

    def call(self, kernel, name, ins, outs, scratch, flops, *args, specs=None, aliases=None):
        single = not isinstance(outs, list)
        size = sum(a.size * a.dtype.itemsize for a in args if a.size < 2000000)
        size += sum(math.prod(o.shape) * o.dtype.itemsize for o in ([outs] if single else outs))
        args = [pltpu.with_memory_space_constraint(a, pltpu.HBM) if i == 1 else a for i, a in zip(ins, args)]
        if self.latest is not None:
            held = ins.index(0)
            args[held] = self.hold(args[held])
        result = pl.pallas_call(
            kernel,
            in_specs=[ANY_HBM if i else IN_VMEM for i in ins],
            out_specs=specs or (IN_VMEM if single else [IN_VMEM] * len(outs)),
            out_shape=outs,
            scratch_shapes=scratch,
            input_output_aliases=aliases or {},
            compiler_params=pltpu.CompilerParams(vmem_limit_bytes=24 * 1024 * 1024),
            cost_estimate=pl.CostEstimate(flops=int(flops * self.weight), bytes_accessed=int(size * self.weight), transcendentals=0),
            name=name,
        )(*args)
        self.latest = result if single else result[-1]
        return result


def swap(x, axis, other):
    return lax.ppermute(x, axis, [(i, other(i)) for i in range(lax.axis_size(axis))])


def across_chan(x):
    return swap(x, "chan", lambda i: i ^ 1)


def across_replica(x):
    return swap(x, "replica", lambda i: i ^ 1)


def on_device(activations, cotangent, conv_weights, snake_alpha, seg_lengths, seg_owner, seg_start):
    rows, half = activations.shape
    layers, taps, channels, _ = conv_weights.shape
    top = layers - 1
    fast = lax.axis_size("dp") == 4 and lax.axis_size("replica") == 2
    counts = [1] * layers
    carrier = 1 if fast else None
    weight = {}
    tile, triple = (rows, half), (rows, taps * half)
    flops = 2 * rows * half * half * taps
    sequence = Sequence()
    streams, mine, partners, owns = [], [], {}, {}
    rounded, shifted, arrived, back_owns, far = {}, {}, {}, {}, {}
    across, across_other = {}, {}
    alpha_parts = [None] * layers
    kept, got, late, summed, crossed = {}, {}, {}, {}, {}

    loaded = (2, taps * half, half)
    sems = DMA((2 * taps,))

    def forward_own(layer, load=None):
        outs, args, ins = struct(tile, F32), [mine[layer], weight[layer]], [0, 0]
        scratch = [pltpu.VMEM(triple, BF16)]
        if load is not None:
            outs, args, ins = [outs, struct(loaded, BF16)], args + [conv_weights], ins + [1]
            scratch.append(sems)
        result = sequence.call(
            functools.partial(forward_own_kernel, layer, load), "forward_own", ins, outs, scratch, flops, *args
        )
        if load is None:
            owns[layer] = result
        else:
            owns[layer], weight[load] = result

    def forward_partner(layer, load=None):
        last = layer == top
        ins, args = [0] * 5, [partners[layer], weight[layer], owns[layer], streams[layer], live]
        outs = [struct(tile, BF16)] if last else [struct(tile, F32), struct(tile, BF16)]
        scratch = [pltpu.VMEM(triple, BF16)]
        if not last:
            ins, args = ins + [0], args + [alphas]
        if load is not None:
            ins, args, outs = ins + [1], args + [conv_weights], outs + [struct(loaded, BF16)]
            scratch.append(sems)
        result = sequence.call(
            functools.partial(forward_partner_kernel, layer, last, load), "forward_partner", ins, outs, scratch,
            flops, *args,
        )
        if load is not None:
            weight[load] = result[-1]
        if last:
            return result[0]
        streams.append(result[0])
        mine.append(result[1])
        partners[layer + 1] = across_chan(result[1])

    def back_partner(layer):
        shifted[layer], part = sequence.call(
            functools.partial(back_partner_kernel, layer), "back_partner", [0, 0],
            [struct(triple, BF16), struct(tile, BF16)], [], flops, rounded[layer + 1], weight[layer],
        )
        arrived[layer] = across_chan(part)

    def back_own(layer):
        back_owns[layer] = sequence.call(
            back_own_kernel, "back_own", [0, 0], struct(tile, F32), [], flops, shifted[layer], weight[layer]
        )

    def send_gradient(layer):
        if fast:
            far[layer] = across_replica(sequence.hold(rounded[layer + 1]))

    def combine(layer, grad):
        args = [back_owns[layer], arrived[layer], streams[layer], alphas]
        outs = [struct((1, half), F32)]
        if layer > 0:
            args += [grad, live]
            outs += [struct(tile, F32)] * (layer > 1) + [struct(tile, BF16)]
        result = sequence.call(
            functools.partial(combine_kernel, layer), "combine", [0] * len(args), outs, [], 60 * rows * half, *args
        )
        alpha_parts[layer] = result[0]
        if layer > 0:
            rounded[layer] = result[-1]
            return result[1]

    def turn(*chosen):
        if fast:
            moved_rows = across_replica(sequence.call(
                turn_kernel, "turn", [0] * len(chosen), struct((len(chosen) * half // 2, rows), BF16),
                [pltpu.VMEM((half, rows), BF16)], 10 * rows * half, *[mine[layer] for layer in chosen],
            ))
            for index, layer in enumerate(chosen):
                across[layer] = (moved_rows, index * half // 2)

    def turn_whole(layer):
        if fast:
            across_other[layer] = across_replica(sequence.call(
                turn_whole_kernel, "turn_whole", [0, 0], struct((half, rows), BF16),
                [pltpu.VMEM((half, rows), BF16)], 10 * rows * half, mine[layer], partners[layer],
            ))
            across[layer] = (across_other[layer], 0)

    def share(*chosen):
        if fast:
            shared = across_chan(sequence.hold(across[chosen[0]][0]))
            for layer in chosen:
                across_other[layer] = shared

    own_turned, far_shifted = {}, {}

    def own_rows(layer):
        if fast:
            own_turned[layer] = sequence.call(
                functools.partial(own_rows_kernel, counts[layer]), "own_rows", [0, 0], struct((half, rows), BF16),
                [pltpu.VMEM((half, rows), BF16)], 10 * rows * half, mine[layer], partners[layer],
            )

    def far_rows(layer):
        if fast:
            far_shifted[layer] = sequence.call(
                functools.partial(far_kernel, layer), "far_rows", [0], struct(triple, BF16), [],
                10 * rows * half, far[layer],
            )

    def weights(layer):
        if not fast:
            out = sequence.call(
                weight_kernel, "weight", [0] * 3, struct((channels, taps * half), BF16),
                [pltpu.VMEM((channels, rows), BF16)], 2 * flops, mine[layer], partners[layer], shifted[layer],
            )
            part = lax.psum_scatter(out, "dp", scatter_dimension=0, tiled=True)
            summed[layer, 0] = lax.psum(part, "replica")
            crossed[layer, 0] = jnp.zeros_like(part)
            return
        pieces, depth = counts[layer], channels // 4 // counts[layer]
        carried = alpha_parts if layer == carrier else []
        outs = [struct((depth, taps * half), BF16)] * (2 * pieces)
        if carried:
            outs[0] = struct((depth + CARRIED, taps * half), BF16)
        args = [own_turned[layer], shifted[layer], across[layer][0], across_other[layer], far_shifted[layer], *carried]
        out = sequence.call(
            functools.partial(paired_weight_kernel, pieces, across[layer][1], len(carried)), "paired_weight",
            [0] * len(args), outs, [pltpu.VMEM((half, rows), BF16)], 2 * flops, *args,
        )
        for part in range(pieces):
            got[layer, part] = swap(out[part], "dp", lambda i: i ^ 1)
            kept[layer, part] = out[pieces + part]

    carry_sum = [None]

    def fold(layer, part=0):
        if not fast:
            return
        keep, came = kept[layer, part], got[layer, part]
        depth, carried = keep.shape[0] // 2, alpha_parts if layer == carrier else []
        outs = [struct((depth + CARRIED * bool(carried), taps * half), BF16)]
        if carried:
            outs.append(struct((1, taps * half), F32))
        result = sequence.call(
            functools.partial(fold_kernel, len(carried)), "fold", [0] * (2 + len(carried)), outs, [], keep.size,
            keep, came, *carried,
        )
        if carried:
            carry_sum[0] = result[1]
        late[layer, part] = swap(result[0], "dp", lambda i: i ^ 2)

    def total(layer, part=0):
        if not fast:
            return
        keep, came, last = kept[layer, part], got[layer, part], late[layer, part]
        outs, args = [struct(last.shape, BF16)], [keep, came, last]
        if layer == carrier:
            outs.append(struct((1, taps * half), F32))
            args.append(carry_sum[0])
        result = sequence.call(
            functools.partial(total_kernel, layer == carrier), "total", [0] * len(args), outs, [], 2 * flops, *args
        )
        if layer == carrier:
            carry_sum[0] = result[1]
        summed[layer, part] = result[0]

    def cross(layer, part=0):
        if fast:
            crossed[layer, part] = across_replica(sequence.hold(summed[layer, part]))

    stream, snaked, grad, live, alphas, weight[0] = sequence.call(
        prep_kernel, "prep", [1] * 7,
        [struct(tile, F32), struct(tile, BF16), struct(tile, BF16), struct((rows, 128), F32),
         struct(snake_alpha.shape, F32), struct(loaded, BF16)],
        [pltpu.SMEM(seg_lengths.shape, jnp.int32)] * 3 + [pltpu.VMEM(tile, BF16)] * 2 + [DMA((6,)), sems],
        40 * rows * half,
        seg_lengths, seg_owner, seg_start, activations, cotangent, snake_alpha, conv_weights,
    )
    streams.append(stream)
    mine.append(snaked)
    partners[0] = across_chan(snaked)
    rounded[layers] = grad
    depth = channels // lax.axis_size("dp")

    def finish(chosen, before=None):
        pairs = [] if before is None else [before]
        carry = carrier in chosen
        if carry:
            pairs.append(carry_sum[0])
        for layer in chosen:
            for part in range(counts[layer]):
                pairs += [summed[layer, part], crossed[layer, part]]
        out = struct((layers, taps, depth, half), F32)
        return sequence.call(
            functools.partial(
                finish_kernel, fast, before is not None, carry, tuple((layer, counts[layer]) for layer in chosen)
            ),
            "finish", [2] * (before is not None) + [0] * (len(pairs) - (before is not None)),
            [out, struct((layers, half), F32)] if carry else [out],
            [pltpu.VMEM((len(chosen), taps, depth, half), F32), DMA((len(chosen),))],
            layers * taps * depth * half, *pairs, specs=[ANY_HBM] + [IN_VMEM] * carry,
            aliases={0: 0} if before is not None else None,
        )

    rounds = [("replica", 1 << bit) for bit in range(8) if lax.axis_size("replica") >> (bit + 1)]
    rounds += [("dp", 1 << bit) for bit in range(8) if lax.axis_size("dp") >> (bit + 1)]
    arrivals = []

    def alpha_round():
        if arrivals:
            value = sequence.call(
                add_kernel, "add", [0, 0], struct((layers, half), F32), [], layers * half, *arrivals.pop()
            )
        else:
            value = sequence.call(
                stack_kernel, "stack", [0] * layers, struct((layers, half), F32), [], layers * half, *alpha_parts
            )
        if not rounds:
            return value
        axis, apart = rounds.pop(0)
        arrivals.append((value, swap(value, axis, lambda place: place ^ apart)))

    send_gradient(2)
    forward_own(0, load=2)
    forward_partner(0, load=1)
    back_partner(2)
    forward_own(1)
    forward_partner(1)
    turn(2)
    back_own(2)
    grad = combine(2, grad)
    send_gradient(1)
    far_rows(2)
    own_rows(2)
    turn(1)
    back_partner(1)
    share(2)
    back_own(1)
    combine(1, grad)
    weights(2)
    back_partner(0)
    back_own(0)
    sequence.weight = 10
    combine(0, None)
    own_rows(1)
    far_rows(1)
    own_rows(0)
    share(1)
    turn_whole(0)
    send_gradient(0)
    forward_own(2)
    residual_out = forward_partner(2)
    sequence.weight = 0.01
    weights(1)
    fold(2)
    far_rows(0)
    sequence.weight = 0.01
    weights(0)
    sequence.weight = 3
    fold(1)
    total(2)
    cross(2)
    fold(0)
    total(1)
    cross(1)
    total(0)
    cross(0)
    if fast:
        weight_grads, alpha_grads = finish((2, 1))
        (weight_grads,) = finish((0,), weight_grads)
    else:
        alpha_grads = alpha_round()
        while alpha_grads is None:
            alpha_grads = alpha_round()
        (weight_grads,) = finish((2, 1, 0))
    return (residual_out, weight_grads, alpha_grads)


def solution(mesh):
    return jax.shard_map(
        on_device,
        mesh=mesh,
        in_specs=(
            P(("groups", "dp", "replica"), "chan"),
            P(("groups", "dp", "replica"), "chan"),
            P(None, None, None, "chan"),
            P(None, "chan"),
            P("groups"),
            P("groups"),
            P("groups"),
        ),
        out_specs=(
            P(("groups", "dp", "replica"), "chan"),
            P("groups", None, "dp", "chan"),
            P("groups", "chan"),
        ),
        check_vma=False,
    )
```

```python
import functools
import math

import jax
import jax.numpy as jnp
from jax import lax
from jax.experimental import pallas as pl
from jax.experimental.pallas import tpu as pltpu
from jax.sharding import PartitionSpec as P

dilations = (1, 3, 5)
F32, BF16 = jnp.float32, jnp.bfloat16
ANY_HBM = pl.BlockSpec(memory_space=pltpu.HBM)
IN_VMEM = pl.BlockSpec(memory_space=pltpu.VMEM)
DMA = pltpu.SemaphoreType.DMA
PI_PARTS = (3.140625, 9.67502593994140625e-4, 1.509957990978376432e-7)
SIN_TERMS = (-1.0 / 39916800, 1.0 / 362880, -1.0 / 5040, 1.0 / 120, -1.0 / 6)
COS_TERMS = (1.0 / 479001600, -1.0 / 3628800, 1.0 / 40320, -1.0 / 720, 1.0 / 24, -0.5)
RANGE = 8192.0
CHUNK = 64
CARRIED = 16


def horner(terms, x):
    total = jnp.full_like(x, terms[0])
    for term in terms[1:]:
        total = total * x + term
    return total


def reduced(angle):
    turns = jnp.round(angle * (1.0 / 3.14159265358979))
    for part in PI_PARTS:
        angle = angle - turns * part
    return angle


def sine(angle, exact_range):
    if not exact_range:
        return jnp.sin(angle)
    rest = reduced(angle)
    square = rest * rest
    return rest + rest * (square * horner(SIN_TERMS, square))


def sine_cosine(angle, exact_range):
    if not exact_range:
        return jnp.sin(angle), jnp.cos(angle)
    rest = reduced(angle)
    square = rest * rest
    return (
        rest + rest * (square * horner(SIN_TERMS, square)),
        1.0 + square * horner(COS_TERMS, square),
    )


def by_range(bound, body):
    @pl.when(bound < RANGE)
    def _():
        body(True)

    @pl.when(bound >= RANGE)
    def _():
        body(False)


def write_snake(stream_ref, alpha, out_ref):
    inverse = 1.0 / alpha
    bound = jnp.max(jnp.abs(stream_ref[...])) * jnp.max(alpha)

    def body(exact_range):
        @pl.loop(0, stream_ref.shape[0] // CHUNK)
        def _(step):
            rows = pl.ds(pl.multiple_of(step * CHUNK, CHUNK), CHUNK)
            stream = stream_ref[rows, :]
            wave = sine(alpha * stream, exact_range)
            out_ref[rows, :] = (stream + wave * wave * inverse).astype(BF16)

    by_range(bound, body)


def moved(values, offset):
    if offset == 0:
        return values
    rows = values.shape[0]
    place = lax.broadcasted_iota(jnp.int32, values.shape, 0)
    turned = pltpu.roll(values, (-offset) % rows, 0)
    inside = place < rows - offset if offset > 0 else place >= -offset
    return jnp.where(inside, turned, 0.0)


def write_shifts(values_ref, out_ref, dilation):
    width = values_ref.shape[1]
    values = values_ref[...].astype(F32)
    for tap in range(3):
        out_ref[:, tap * width : (tap + 1) * width] = moved(values, (tap - 1) * dilation).astype(BF16)


def chan_begin(side, half):
    chan = lax.axis_index("chan")
    return pl.multiple_of((chan if side == 0 else 1 - chan) * half, half)


def load_weights(layer, weight_hbm, weight_ref, sems):
    half = weight_hbm.shape[3]
    loads = []
    for side in range(2):
        for tap in range(3):
            source = weight_hbm.at[layer, tap, pl.ds(chan_begin(side, half), half), :]
            target = weight_ref.at[side, pl.ds(tap * half, half), :]
            loads.append(pltpu.make_async_copy(source, target, sems.at[len(loads)]))
    for copy in loads:
        copy.start()
    return loads


def prep_kernel(
    len_hbm, own_hbm, start_hbm, act_hbm, cot_hbm, alpha_hbm, weight_hbm,
    stream_ref, snake_ref, grad_ref, live_ref, alpha_ref, weight_ref,
    len_ref, own_ref, start_ref, act_ref, cot_ref, sems, weight_sems,
):
    pairs = (
        (len_hbm, len_ref), (own_hbm, own_ref), (start_hbm, start_ref),
        (alpha_hbm, alpha_ref), (act_hbm, act_ref), (cot_hbm, cot_ref),
    )
    copies = [pltpu.make_async_copy(a, b, sems.at[i]) for i, (a, b) in enumerate(pairs)]
    for copy in copies:
        copy.start()
    loads = load_weights(0, weight_hbm, weight_ref, weight_sems)
    replicas = lax.axis_size("replica")
    device = lax.axis_index("dp") * replicas + lax.axis_index("replica")
    rows, width = act_ref.shape
    place = lax.broadcasted_iota(jnp.int32, (rows, 128), 0)
    live_ref[...] = jnp.zeros((rows, 128), F32)
    for copy in copies[:3]:
        copy.wait()

    @pl.loop(0, len_ref.shape[0])
    def _(clip):
        @pl.when(own_ref[clip] == device)
        def _():
            first = start_ref[clip]
            inside = (place >= first) & (place < first + len_ref[clip])
            live_ref[...] = jnp.where(inside, 1.0, live_ref[...])

    live = jnp.tile(live_ref[...], (1, width // 128))
    for copy in copies[3:5]:
        copy.wait()
    stream_ref[...] = act_ref[...].astype(F32) * live
    write_snake(stream_ref, alpha_ref[0:1, :], snake_ref)
    copies[5].wait()
    grad_ref[...] = (cot_ref[...].astype(F32) * live).astype(BF16)
    for copy in loads:
        copy.wait()


def forward_own_kernel(layer, load, snake_ref, weight_ref, *rest):
    if load is None:
        out_ref, shifts_ref = rest
        loads = []
    else:
        weight_hbm, out_ref, loaded_ref, shifts_ref, sems = rest
        loads = load_weights(load, weight_hbm, loaded_ref, sems)
    write_shifts(snake_ref, shifts_ref, dilations[layer])
    out_ref[...] = jnp.dot(shifts_ref[...], weight_ref[0], preferred_element_type=F32)
    for copy in loads:
        copy.wait()


def forward_partner_kernel(layer, last, load, snake_ref, weight_ref, own_ref, old_ref, live_ref, *rest):
    rest = list(rest)
    alpha_ref = None if last else rest.pop(0)
    weight_hbm = None if load is None else rest.pop(0)
    result_ref = rest.pop(0)
    next_ref = None if last else rest.pop(0)
    loads = []
    if load is not None:
        loaded_ref, shifts_ref, sems = rest
        loads = load_weights(load, weight_hbm, loaded_ref, sems)
    else:
        (shifts_ref,) = rest
    write_shifts(snake_ref, shifts_ref, dilations[layer])
    part = jnp.dot(shifts_ref[...], weight_ref[1], preferred_element_type=F32)
    live = jnp.tile(live_ref[...], (1, old_ref.shape[1] // 128))
    new = (old_ref[...] + (own_ref[...] + part)) * live
    result_ref[...] = new.astype(result_ref.dtype)
    if not last:
        write_snake(result_ref, alpha_ref[layer + 1 : layer + 2, :], next_ref)
    for copy in loads:
        copy.wait()


def back_product(shifted_ref, weight_ref, side):
    half = weight_ref.shape[2]
    total = None
    for tap in range(3):
        span = slice(tap * half, (tap + 1) * half)
        part = lax.dot_general(
            shifted_ref[:, span], weight_ref[side, span, :], (((1,), (1,)), ((), ())),
            preferred_element_type=F32,
        )
        total = part if total is None else total + part
    return total


def back_partner_kernel(layer, grad_ref, weight_ref, shifted_ref, out_ref):
    write_shifts(grad_ref, shifted_ref, -dilations[layer])
    out_ref[...] = back_product(shifted_ref, weight_ref, 1).astype(BF16)


def back_own_kernel(shifted_ref, weight_ref, out_ref):
    out_ref[...] = back_product(shifted_ref, weight_ref, 0)


def combine_kernel(layer, own_ref, partner_ref, stream_ref, alphas_ref, *rest):
    if layer == 0:
        (alpha_grad_ref,) = rest
    elif len(rest) == 5:
        old_ref, live_ref, alpha_grad_ref, grad_ref, rounded_ref = rest
    else:
        old_ref, live_ref, alpha_grad_ref, rounded_ref = rest
        grad_ref = None
    alpha = alphas_ref[layer : layer + 1, :]
    inverse = 1.0 / alpha
    bound = jnp.max(jnp.abs(stream_ref[...])) * jnp.max(alpha)
    width = stream_ref.shape[1]

    def body(exact_range):
        def step_body(step, total):
            rows = pl.ds(pl.multiple_of(step * CHUNK, CHUNK), CHUNK)
            stream = stream_ref[rows, :]
            back = own_ref[rows, :] + partner_ref[rows, :].astype(F32)
            sin, cos = sine_cosine(alpha * stream, exact_range)
            double = 2.0 * sin * cos
            ratio = sin * inverse
            term = back * (stream * double * inverse - ratio * ratio)
            if layer > 0:
                live = jnp.tile(live_ref[rows, :], (1, width // 128))
                grad = (old_ref[rows, :].astype(F32) + back * (1.0 + double)) * live
                if grad_ref is not None:
                    grad_ref[rows, :] = grad
                rounded_ref[rows, :] = grad.astype(BF16)
            return total + jnp.sum(term.reshape(CHUNK // 8, 8, width), axis=0)

        total = lax.fori_loop(0, stream_ref.shape[0] // CHUNK, step_body, jnp.zeros((8, width), F32))
        alpha_grad_ref[...] = jnp.sum(total, axis=0, keepdims=True)

    by_range(bound, body)


def block_place(pieces, slice_index, part):
    apart = jnp.bitwise_xor(slice_index, lax.axis_index("dp"))
    order = (2 * pieces, 0, 2 * pieces + 1, 1)
    return 2 * part + jnp.where(
        apart == 0, order[0], jnp.where(apart == 1, order[1], jnp.where(apart == 2, order[2], order[3]))
    )


def weight_kernel(own_ref, partner_ref, shifted_ref, out_ref, turned_ref):
    half = own_ref.shape[1]
    chan = lax.axis_index("chan")
    for ref, side in ((own_ref, chan), (partner_ref, 1 - chan)):
        turned_ref[pl.ds(pl.multiple_of(side * half, half), half), :] = ref[...].T
    for tap in range(3):
        span = slice(tap * half, (tap + 1) * half)
        out_ref[:, span] = jnp.dot(turned_ref[...], shifted_ref[:, span], preferred_element_type=F32).astype(BF16)


def place_rows(pieces, rows_of, side, target_ref, columns):
    size = rows_of.shape[0] // (2 * pieces)
    for local in range(2):
        for part in range(pieces):
            begin = pl.multiple_of(block_place(pieces, side * 2 + local, part) * size, size)
            low = (local * pieces + part) * size
            target_ref[pl.ds(begin, size), columns] = rows_of[low : low + size, :]


def pick_parts(turned_ref, part, size):
    begin = pl.multiple_of(part * size, size)
    return [turned_ref[pl.ds(local * 2 * size + begin, size), :] for local in range(2)]


def turn_whole_kernel(own_ref, partner_ref, out_ref, turned_ref):
    size = own_ref.shape[1] // 4
    chan = lax.axis_index("chan")
    for ref, side in ((own_ref, chan), (partner_ref, 1 - chan)):
        turned_ref[...] = ref[...].T
        for local, piece in enumerate(pick_parts(turned_ref, 1 - lax.axis_index("replica"), size)):
            out_ref[pl.ds(pl.multiple_of((2 * side + local) * size, size), size), :] = piece


def turn_kernel(*refs):
    snakes, out_ref, turned_ref = refs[:-2], refs[-2], refs[-1]
    size = snakes[0].shape[1] // 4
    for index, ref in enumerate(snakes):
        turned_ref[...] = ref[...].T
        for local, piece in enumerate(pick_parts(turned_ref, 1 - lax.axis_index("replica"), size)):
            low = (2 * index + local) * size
            out_ref[low : low + size, :] = piece


def own_rows_kernel(pieces, own_ref, partner_ref, out_ref, half_ref):
    chan = lax.axis_index("chan")
    mine = lax.axis_index("replica")
    for ref, side in ((own_ref, chan), (partner_ref, 1 - chan)):
        half_ref[...] = ref[...].T
        both = jnp.concatenate(pick_parts(half_ref, mine, ref.shape[1] // 4), 0)
        place_rows(pieces, both, side, out_ref, slice(None))


def far_kernel(layer, grad_ref, out_ref):
    write_shifts(grad_ref, out_ref, -dilations[layer])


def write_carried(values, out_ref, low):
    first = values.astype(BF16).astype(F32)
    second = (values - first).astype(BF16).astype(F32)
    third = values - first - second
    shape = (CARRIED, values.shape[1])
    row = lax.broadcasted_iota(jnp.int32, shape, 0)
    block = jnp.where(row == 0, first, jnp.where(row == 1, second, jnp.where(row == 2, third, 0.0)))
    out_ref[low : low + CARRIED, :] = block.astype(BF16)


def read_carried(ref, low):
    block = ref[low : low + CARRIED, :].astype(F32)
    return (block[0:1, :] + block[1:2, :]) + block[2:3, :]


def paired_weight_kernel(pieces, low, carry, own_ref, shifted_ref, across_ref, across_other_ref, far_ref, *rest):
    if carry:
        write_carried(jnp.concatenate([ref[...] for ref in rest[:carry]], 1), rest[carry], own_ref.shape[0] // 2)
        rest = rest[carry:]
    outs, turned_ref = rest[:-1], rest[-1]
    half = own_ref.shape[0]
    chan = lax.axis_index("chan")
    whole = across_ref.shape[0] == half
    sources = ((across_ref, 0, 0), (across_ref, 1, half // 2)) if whole else (
        (across_ref, chan, 0), (across_other_ref, 1 - chan, 0))
    for ref, side, low in sources:
        place_rows(pieces, ref[low : low + half // 2, :], side, turned_ref, slice(None))
    for tap in range(3):
        span = slice(tap * half, (tap + 1) * half)
        product = jnp.dot(own_ref[...], shifted_ref[:, span], preferred_element_type=F32)
        product += jnp.dot(turned_ref[...], far_ref[:, span], preferred_element_type=F32)
        product = product.astype(BF16)
        size = product.shape[0] // len(outs)
        for place, ref in enumerate(outs):
            ref[0:size, span] = product[place * size : (place + 1) * size, :]


def finish_kernel(paired, held, carry, counts, *refs):
    total_ref, sems = refs[-2:]
    refs = list(refs[1:-2] if held else refs[:-2])
    if carry:
        alpha_ref = refs.pop()
        alpha_mine = refs.pop(0)
    out_ref = refs.pop()
    half = total_ref.shape[3]
    rows_of = total_ref.shape[2] // (2 if paired else 1)
    copies = []
    for index, (layer, pieces) in enumerate(counts):
        for part in range(pieces):
            mine_ref, other_ref = refs.pop(0), refs.pop(0)
            size = rows_of
            if carry and other_ref.shape[0] > size:
                alpha = alpha_mine[...] + read_carried(other_ref, size)
                for place in range(3):
                    alpha_ref[place : place + 1, :] = alpha[:, place * half : (place + 1) * half]
            for tap in range(3):
                span = slice(tap * half, (tap + 1) * half)
                mine, other = mine_ref[0:size, span].astype(F32), other_ref[0:size, span].astype(F32)
                if paired:
                    begin = lax.axis_index("replica") * (size * pieces)
                    for values, start in ((mine, begin), (other, size * pieces - begin)):
                        place = pl.multiple_of(start + part * size, size)
                        total_ref[index, tap, pl.ds(place, size), :] = values
                else:
                    total_ref[index, tap] = mine + other
        copies.append(pltpu.make_async_copy(total_ref.at[index], out_ref.at[layer], sems.at[index]))
        copies[-1].start()
    for copy in copies:
        copy.wait()


def fold_kernel(carry, keep, got, *rest):
    if carry:
        mine, rest = rest[:carry], rest[carry:]
        send, sum_ref = rest
    else:
        (send,) = rest
    rows = keep.shape[0] // 2
    send[0:rows, :] = (keep[rows:, :].astype(F32) + got[rows : 2 * rows, :].astype(F32)).astype(BF16)
    if carry:
        values = jnp.concatenate([ref[...] for ref in mine], 1) + read_carried(got, 2 * rows)
        sum_ref[...] = values
        write_carried(values, send, rows)


def total_kernel(carry, keep, got, late, *rest):
    if carry:
        mine, out_ref, sum_ref = rest
    else:
        (out_ref,) = rest
    rows = keep.shape[0] // 2
    total = keep[0:rows, :].astype(F32) + got[0:rows, :].astype(F32) + late[0:rows, :].astype(F32)
    out_ref[0:rows, :] = total.astype(BF16)
    if carry:
        values = mine[...] + read_carried(late, rows)
        sum_ref[...] = values
        write_carried(values, out_ref, rows)


def stack_kernel(*refs):
    for index, ref in enumerate(refs[:-1]):
        refs[-1][index : index + 1, :] = ref[...]


def add_kernel(left, right, out_ref):
    out_ref[...] = left[...] + right[...]


def struct(shape, dtype):
    return jax.ShapeDtypeStruct(shape, dtype)


def after(value, other):
    return value if other is None else lax.optimization_barrier((value, other))[0]


class Sequence:
    def __init__(self):
        self.latest = None
        self.weight = 10

    def hold(self, value):
        return after(value, self.latest)

    def call(self, kernel, name, ins, outs, scratch, flops, *args, specs=None, aliases=None):
        single = not isinstance(outs, list)
        size = sum(a.size * a.dtype.itemsize for a in args if a.size < 2000000)
        size += sum(math.prod(o.shape) * o.dtype.itemsize for o in ([outs] if single else outs))
        args = [pltpu.with_memory_space_constraint(a, pltpu.HBM) if i == 1 else a for i, a in zip(ins, args)]
        if self.latest is not None:
            held = ins.index(0)
            args[held] = self.hold(args[held])
        result = pl.pallas_call(
            kernel,
            in_specs=[ANY_HBM if i else IN_VMEM for i in ins],
            out_specs=specs or (IN_VMEM if single else [IN_VMEM] * len(outs)),
            out_shape=outs,
            scratch_shapes=scratch,
            input_output_aliases=aliases or {},
            compiler_params=pltpu.CompilerParams(vmem_limit_bytes=24 * 1024 * 1024),
            cost_estimate=pl.CostEstimate(flops=int(flops * self.weight), bytes_accessed=int(size * self.weight), transcendentals=0),
            name=name,
        )(*args)
        self.latest = result if single else result[-1]
        return result


def swap(x, axis, other):
    return lax.ppermute(x, axis, [(i, other(i)) for i in range(lax.axis_size(axis))])


def across_chan(x):
    return swap(x, "chan", lambda i: i ^ 1)


def across_replica(x):
    return swap(x, "replica", lambda i: i ^ 1)


def on_device(activations, cotangent, conv_weights, snake_alpha, seg_lengths, seg_owner, seg_start):
    rows, half = activations.shape
    layers, taps, channels, _ = conv_weights.shape
    top = layers - 1
    fast = lax.axis_size("dp") == 4 and lax.axis_size("replica") == 2
    counts = [1] * layers
    carrier = 1 if fast else None
    weight = {}
    tile, triple = (rows, half), (rows, taps * half)
    flops = 2 * rows * half * half * taps
    sequence = Sequence()
    streams, mine, partners, owns = [], [], {}, {}
    rounded, shifted, arrived, back_owns, far = {}, {}, {}, {}, {}
    across, across_other = {}, {}
    alpha_parts = [None] * layers
    kept, got, late, summed, crossed = {}, {}, {}, {}, {}

    loaded = (2, taps * half, half)
    sems = DMA((2 * taps,))

    def forward_own(layer, load=None):
        outs, args, ins = struct(tile, F32), [mine[layer], weight[layer]], [0, 0]
        scratch = [pltpu.VMEM(triple, BF16)]
        if load is not None:
            outs, args, ins = [outs, struct(loaded, BF16)], args + [conv_weights], ins + [1]
            scratch.append(sems)
        result = sequence.call(
            functools.partial(forward_own_kernel, layer, load), "forward_own", ins, outs, scratch, flops, *args
        )
        if load is None:
            owns[layer] = result
        else:
            owns[layer], weight[load] = result

    def forward_partner(layer, load=None):
        last = layer == top
        ins, args = [0] * 5, [partners[layer], weight[layer], owns[layer], streams[layer], live]
        outs = [struct(tile, BF16)] if last else [struct(tile, F32), struct(tile, BF16)]
        scratch = [pltpu.VMEM(triple, BF16)]
        if not last:
            ins, args = ins + [0], args + [alphas]
        if load is not None:
            ins, args, outs = ins + [1], args + [conv_weights], outs + [struct(loaded, BF16)]
            scratch.append(sems)
        result = sequence.call(
            functools.partial(forward_partner_kernel, layer, last, load), "forward_partner", ins, outs, scratch,
            flops, *args,
        )
        if load is not None:
            weight[load] = result[-1]
        if last:
            return result[0]
        streams.append(result[0])
        mine.append(result[1])
        partners[layer + 1] = across_chan(result[1])

    def back_partner(layer):
        shifted[layer], part = sequence.call(
            functools.partial(back_partner_kernel, layer), "back_partner", [0, 0],
            [struct(triple, BF16), struct(tile, BF16)], [], flops, rounded[layer + 1], weight[layer],
        )
        arrived[layer] = across_chan(part)

    def back_own(layer):
        back_owns[layer] = sequence.call(
            back_own_kernel, "back_own", [0, 0], struct(tile, F32), [], flops, shifted[layer], weight[layer]
        )

    def send_gradient(layer):
        if fast:
            far[layer] = across_replica(sequence.hold(rounded[layer + 1]))

    def combine(layer, grad):
        args = [back_owns[layer], arrived[layer], streams[layer], alphas]
        outs = [struct((1, half), F32)]
        if layer > 0:
            args += [grad, live]
            outs += [struct(tile, F32)] * (layer > 1) + [struct(tile, BF16)]
        result = sequence.call(
            functools.partial(combine_kernel, layer), "combine", [0] * len(args), outs, [], 60 * rows * half, *args
        )
        alpha_parts[layer] = result[0]
        if layer > 0:
            rounded[layer] = result[-1]
            return result[1]

    def turn(*chosen):
        if fast:
            moved_rows = across_replica(sequence.call(
                turn_kernel, "turn", [0] * len(chosen), struct((len(chosen) * half // 2, rows), BF16),
                [pltpu.VMEM((half, rows), BF16)], 10 * rows * half, *[mine[layer] for layer in chosen],
            ))
            for index, layer in enumerate(chosen):
                across[layer] = (moved_rows, index * half // 2)

    def turn_whole(layer):
        if fast:
            across_other[layer] = across_replica(sequence.call(
                turn_whole_kernel, "turn_whole", [0, 0], struct((half, rows), BF16),
                [pltpu.VMEM((half, rows), BF16)], 10 * rows * half, mine[layer], partners[layer],
            ))
            across[layer] = (across_other[layer], 0)

    def share(*chosen):
        if fast:
            shared = across_chan(sequence.hold(across[chosen[0]][0]))
            for layer in chosen:
                across_other[layer] = shared

    own_turned, far_shifted = {}, {}

    def own_rows(layer):
        if fast:
            own_turned[layer] = sequence.call(
                functools.partial(own_rows_kernel, counts[layer]), "own_rows", [0, 0], struct((half, rows), BF16),
                [pltpu.VMEM((half, rows), BF16)], 10 * rows * half, mine[layer], partners[layer],
            )

    def far_rows(layer):
        if fast:
            far_shifted[layer] = sequence.call(
                functools.partial(far_kernel, layer), "far_rows", [0], struct(triple, BF16), [],
                10 * rows * half, far[layer],
            )

    def weights(layer):
        if not fast:
            out = sequence.call(
                weight_kernel, "weight", [0] * 3, struct((channels, taps * half), BF16),
                [pltpu.VMEM((channels, rows), BF16)], 2 * flops, mine[layer], partners[layer], shifted[layer],
            )
            part = lax.psum_scatter(out, "dp", scatter_dimension=0, tiled=True)
            summed[layer, 0] = lax.psum(part, "replica")
            crossed[layer, 0] = jnp.zeros_like(part)
            return
        pieces, depth = counts[layer], channels // 4 // counts[layer]
        carried = alpha_parts if layer == carrier else []
        outs = [struct((depth, taps * half), BF16)] * (2 * pieces)
        if carried:
            outs[0] = struct((depth + CARRIED, taps * half), BF16)
        args = [own_turned[layer], shifted[layer], across[layer][0], across_other[layer], far_shifted[layer], *carried]
        out = sequence.call(
            functools.partial(paired_weight_kernel, pieces, across[layer][1], len(carried)), "paired_weight",
            [0] * len(args), outs, [pltpu.VMEM((half, rows), BF16)], 2 * flops, *args,
        )
        for part in range(pieces):
            got[layer, part] = swap(out[part], "dp", lambda i: i ^ 1)
            kept[layer, part] = out[pieces + part]

    carry_sum = [None]

    def fold(layer, part=0):
        if not fast:
            return
        keep, came = kept[layer, part], got[layer, part]
        depth, carried = keep.shape[0] // 2, alpha_parts if layer == carrier else []
        outs = [struct((depth + CARRIED * bool(carried), taps * half), BF16)]
        if carried:
            outs.append(struct((1, taps * half), F32))
        result = sequence.call(
            functools.partial(fold_kernel, len(carried)), "fold", [0] * (2 + len(carried)), outs, [], keep.size,
            keep, came, *carried,
        )
        if carried:
            carry_sum[0] = result[1]
        late[layer, part] = swap(result[0], "dp", lambda i: i ^ 2)

    def total(layer, part=0):
        if not fast:
            return
        keep, came, last = kept[layer, part], got[layer, part], late[layer, part]
        outs, args = [struct(last.shape, BF16)], [keep, came, last]
        if layer == carrier:
            outs.append(struct((1, taps * half), F32))
            args.append(carry_sum[0])
        result = sequence.call(
            functools.partial(total_kernel, layer == carrier), "total", [0] * len(args), outs, [], 2 * flops, *args
        )
        if layer == carrier:
            carry_sum[0] = result[1]
        summed[layer, part] = result[0]

    def cross(layer, part=0):
        if fast:
            crossed[layer, part] = across_replica(sequence.hold(summed[layer, part]))

    stream, snaked, grad, live, alphas, weight[0] = sequence.call(
        prep_kernel, "prep", [1] * 7,
        [struct(tile, F32), struct(tile, BF16), struct(tile, BF16), struct((rows, 128), F32),
         struct(snake_alpha.shape, F32), struct(loaded, BF16)],
        [pltpu.SMEM(seg_lengths.shape, jnp.int32)] * 3 + [pltpu.VMEM(tile, BF16)] * 2 + [DMA((6,)), sems],
        40 * rows * half,
        seg_lengths, seg_owner, seg_start, activations, cotangent, snake_alpha, conv_weights,
    )
    streams.append(stream)
    mine.append(snaked)
    partners[0] = across_chan(snaked)
    rounded[layers] = grad
    depth = channels // lax.axis_size("dp")

    def finish(chosen, before=None):
        pairs = [] if before is None else [before]
        carry = carrier in chosen
        if carry:
            pairs.append(carry_sum[0])
        for layer in chosen:
            for part in range(counts[layer]):
                pairs += [summed[layer, part], crossed[layer, part]]
        out = struct((layers, taps, depth, half), F32)
        return sequence.call(
            functools.partial(
                finish_kernel, fast, before is not None, carry, tuple((layer, counts[layer]) for layer in chosen)
            ),
            "finish", [2] * (before is not None) + [0] * (len(pairs) - (before is not None)),
            [out, struct((layers, half), F32)] if carry else [out],
            [pltpu.VMEM((len(chosen), taps, depth, half), F32), DMA((len(chosen),))],
            layers * taps * depth * half, *pairs, specs=[ANY_HBM] + [IN_VMEM] * carry,
            aliases={0: 0} if before is not None else None,
        )

    rounds = [("replica", 1 << bit) for bit in range(8) if lax.axis_size("replica") >> (bit + 1)]
    rounds += [("dp", 1 << bit) for bit in range(8) if lax.axis_size("dp") >> (bit + 1)]
    arrivals = []

    def alpha_round():
        if arrivals:
            value = sequence.call(
                add_kernel, "add", [0, 0], struct((layers, half), F32), [], layers * half, *arrivals.pop()
            )
        else:
            value = sequence.call(
                stack_kernel, "stack", [0] * layers, struct((layers, half), F32), [], layers * half, *alpha_parts
            )
        if not rounds:
            return value
        axis, apart = rounds.pop(0)
        arrivals.append((value, swap(value, axis, lambda place: place ^ apart)))

    send_gradient(2)
    forward_own(0, load=2)
    forward_partner(0, load=1)
    back_partner(2)
    forward_own(1)
    forward_partner(1)
    turn(2)
    back_own(2)
    grad = combine(2, grad)
    send_gradient(1)
    far_rows(2)
    own_rows(2)
    turn(1)
    back_partner(1)
    share(2)
    back_own(1)
    combine(1, grad)
    weights(2)
    back_partner(0)
    back_own(0)
    sequence.weight = 10
    combine(0, None)
    own_rows(1)
    far_rows(1)
    own_rows(0)
    share(1)
    turn_whole(0)
    send_gradient(0)
    forward_own(2)
    sequence.weight = 0.01
    weights(1)
    fold(2)
    residual_out = forward_partner(2)
    far_rows(0)
    sequence.weight = 0.01
    weights(0)
    sequence.weight = 3
    fold(1)
    total(2)
    cross(2)
    fold(0)
    total(1)
    cross(1)
    total(0)
    cross(0)
    if fast:
        weight_grads, alpha_grads = finish((2, 1))
        (weight_grads,) = finish((0,), weight_grads)
    else:
        alpha_grads = alpha_round()
        while alpha_grads is None:
            alpha_grads = alpha_round()
        (weight_grads,) = finish((2, 1, 0))
    return (residual_out, weight_grads, alpha_grads)


def solution(mesh):
    return jax.shard_map(
        on_device,
        mesh=mesh,
        in_specs=(
            P(("groups", "dp", "replica"), "chan"),
            P(("groups", "dp", "replica"), "chan"),
            P(None, None, None, "chan"),
            P(None, "chan"),
            P("groups"),
            P("groups"),
            P("groups"),
        ),
        out_specs=(
            P(("groups", "dp", "replica"), "chan"),
            P("groups", None, "dp", "chan"),
            P("groups", "chan"),
        ),
        check_vma=False,
    )
```
